512 devices in a mesh: leaf: 16 (over y, core), sub: 32 (over x, z).
Axes of the slice: x: 4, y: 8, z: 8, core: 2. Of those that a mesh axis runs over, the one named last changes fastest.
Arguments:
- panels: bfloat16 [3072, 4, 256, 128], P(('leaf', 'sub')), may hold values from -1 to 1
- root_panels: bfloat16 [3072, 256, 128], P(('leaf', 'sub')), may hold values from -1 to 1
- low_inverse: bfloat16 [3072, 128, 128], P(('leaf', 'sub')), may hold values from -4 to 1.5, as said below
- structure: int32 [3072, 4], P(('leaf', 'sub')), may hold values from 0 to 31, all different within a row; in each aligned block of 6 rows (0 to 5, 6 to 11, ...) at most 2 rows name the same one
- owner_map: int32 [16, 32], replicated, may hold values from 0 to 31, each once within a row
- upper_block: float32 [512, 256, 256], P(('leaf', 'sub')), may hold values from -1 to 10, as said below
- upper_cot: float32 [512, 256, 256], P(('leaf', 'sub')), may hold values from -6 to 6
- root_block: float32 [256, 256], replicated, may hold values from -1 to 10, as said below
- root_cot: float32 [256, 256], replicated, may hold values from -6 to 6
Outputs:
- panel_grad: bfloat16 [3072, 4, 256, 128], P(('leaf', 'sub'))
- root_grad: bfloat16 [3072, 256, 128], P(('leaf', 'sub'))
The draws below stay inside these ranges and needn't reach their ends.
Inputs may be any that keep to these rules, and one draw needn't show every extreme that they name: `structure`: among the 6 rows of one device no upper supernode is named more than 2 times; the names within a row differ. Each row of owner_map is a permutation of the group's devices. `upper_block`: Symmetric; diagonal from 6 to 10, every off-diagonal entry at most 2 / 256 in size, so that the diagonal dominates its row. `root_block`: Symmetric; diagonal from 8 to 10, every off-diagonal entry at most 1 / 256 in size, so that the diagonal dominates its row. `low_inverse`: lower triangular, diagonal from 0.5 to 1.5.
All inputs are finite; a program needn't handle non-finite values.
Results may differ from the reference program's by a relative error of at most 0.0014.
The reference program's roundings to bfloat16 on the way (of `upper_adjoint`, `panel_adjoint`, `root_adjoint` and `root_panel_adjoint`) count: a program that leaves them out, or rounds other values in their place, can miss the bound.
Values may be sent and summed in bfloat16 or wider, within the bound.
A program may use at most 64 MiB of HBM per device.

```python
import math
import jax
import jax.numpy as jnp
import numpy as np
from jax import lax

B = 256
W = 128
LD = 6
R = 4
CAP = 2
UPPER = 512
NLOW = 3072
N_LEAF = 16
N_SUB = 32


def draw_dominant(key, count, low_end, high_end, reach):
    first_key, second_key = jax.random.split(key)
    diagonal = jax.random.uniform(first_key, (count, B), jnp.float32, low_end, high_end)
    off_limit = reach / B
    spread = off_limit * jnp.clip(0.5 * jax.random.normal(second_key, (count, B, B), jnp.float32), -1.0, 1.0)
    mirror = 0.5 * (spread + jnp.swapaxes(spread, 1, 2))
    identity = jnp.eye(B, dtype=jnp.float32)
    return mirror * (1.0 - identity) + diagonal[:, :, None] * identity


def draw_upper_block(key, part):
    return draw_dominant(key, UPPER, 6.0, 10.0, 2.0)


def draw_root_block(key, part):
    return draw_dominant(key, 1, 8.0, 10.0, 1.0)[0]


def draw_panels(key, part):
    first_key = jax.random.fold_in(jax.random.fold_in(key, 29), 0)
    deviation = 0.6 / math.sqrt(W * LD * R)
    noise = jnp.clip(jax.random.normal(first_key, (NLOW, R, B, W), jnp.float32), -3.0, 3.0)
    values = deviation * noise
    return values.astype(jnp.bfloat16)


def draw_root_panels(key, part):
    key_list = jax.random.split(jax.random.fold_in(key, 17), 6)
    index = jnp.arange(NLOW, dtype=jnp.int32)
    devices_all = NLOW // LD
    rising = 1.0 + 2.0 * (index // LD).astype(jnp.float32) / max(devices_all - 1, 1)
    node_weight = jnp.exp(jax.random.uniform(key_list[0], (NLOW,), jnp.float32, math.log(0.3), math.log(3.0)))
    row_square = jnp.exp(jax.random.uniform(key_list[1], (B,), jnp.float32, math.log(0.25), math.log(2.5)))
    noise = jnp.clip(jax.random.normal(key_list[2], (NLOW, B, W), jnp.float32), -6.0, 6.0)
    shared = jnp.clip(jax.random.normal(key_list[3], (NLOW, 8, W), jnp.float32), -6.0, 6.0)
    magnitude = jax.random.uniform(key_list[4], (B,), jnp.float32, 0.5, 1.0)
    signs = jnp.where(jax.random.bernoulli(key_list[5], 0.5, (B,)), 1.0, -1.0)
    loading = signs * magnitude * math.sqrt(1.6 * 8.0 / B)
    scale_node = jnp.sqrt(rising * node_weight / (2.35 * NLOW * W))
    common = jnp.tile(shared, (1, B // 8, 1))
    values = scale_node[:, None, None] * (jnp.sqrt(row_square)[None, :, None] * noise + loading[None, :, None] * common)
    return values.astype(jnp.bfloat16)


def draw_low_inverse(key, part):
    first_key, second_key = jax.random.split(key)
    strict = jnp.tril(jax.random.normal(first_key, (NLOW, W, W), jnp.float32) * (0.5 / W ** 0.5), -1)
    diagonal = jax.random.uniform(second_key, (NLOW, W), jnp.float32, 0.5, 1.5)
    identity = jnp.eye(W, dtype=jnp.float32)
    return (strict + diagonal[:, :, None] * identity).astype(jnp.bfloat16)


def levels(key, shape, cuts, least, largest):
    def one(position, shards_of):
        steps = jax.random.uniform(jax.random.fold_in(jax.random.fold_in(key, 6), position), (shards_of,), jnp.float32, least / len(cuts), largest / len(cuts))
        return jnp.repeat(jnp.exp(steps), shape[position] // shards_of).reshape((-1,) + (1,) * (len(shape) - position - 1))

    level = one(*cuts[0])
    for cut in cuts[1:]:
        level = level * one(*cut)
    return level


def routed_block(key, own, number, rows, count, top, most, slope):
    sequence = jax.random.permutation(key, count)
    packed, usual = portions_of(count, rows * top, most, slope, True), portions_of(count, rows * top, most, slope, False)
    places = jnp.arange(count)

    def named(tallies, turn):
        used = int((tallies > 0).sum())
        fixed = max(1, used // 4)
        passed = fixed + (places - fixed + turn * (used - fixed)) % max(1, count - fixed)
        return jnp.zeros((count,), jnp.int32).at[sequence[jnp.where(places < fixed, places, passed)]].set(jnp.asarray(tallies, jnp.int32))

    tallies = jnp.where(number % 4 == 0, named(packed, number // 4), named(usual, number - number // 4 - 1))
    mixed = jax.random.permutation(jax.random.fold_in(own, 3), count)
    donor, receiver = mixed[0:count // 2 * 2:2], mixed[1:count // 2 * 2:2]
    margin = jnp.minimum(tallies[donor] - 1, most - tallies[receiver]) // 2
    margin = jnp.where((donor == sequence[0]) | (receiver == sequence[0]) | (tallies[receiver] == 0), 0, jnp.maximum(margin, 0))
    passed = jax.random.randint(jax.random.fold_in(own, 4), (count // 2,), 0, 1 << 20) % (margin + 1)
    tallies = tallies.at[donor].add(-passed).at[receiver].add(passed)
    items = jnp.searchsorted(jnp.cumsum(tallies), jnp.arange(rows * top), side="right").astype(jnp.int32)
    listing = items.reshape(top, rows).T
    listing = listing[jax.random.permutation(jax.random.fold_in(own, 1), rows)]
    turn = jax.random.randint(jax.random.fold_in(own, 2), (rows, 1), 0, top)
    return jnp.take_along_axis(listing, (jnp.arange(top)[None, :] + turn) % top, axis=1)


def portions_of(amount, total, most, skew, full):
    loads = [(1 << 20) // math.isqrt(rank ** skew) + 1 for rank in range(1, amount + 1)]
    largest = most if full else min(most, max(-(-total // amount), total * loads[0] // sum(loads)))
    least = 1 if total - largest >= amount - 1 else 0
    holding, rest = [largest] + [least] * (amount - 1), total - largest - least * (amount - 1)
    while rest > 0:
        free = [i for i in range(1, amount) if holding[i] < largest] or [i for i in range(1, amount) if holding[i] < most]
        mass, left = sum([loads[i] for i in free]), rest
        for i in free:
            more = min(most - holding[i], max(1, left * loads[i] // mass), rest)
            holding[i] = holding[i] + more
            rest = rest - more
    return np.array(holding)


def normal_values(key, dims, scale, limit, shards=(), kind=jnp.bfloat16):
    array = scale * jax.random.normal(key, dims, jnp.float32)
    if shards:
        array = array * levels(key, dims, shards, -0.22, 0.18)
    return jnp.clip(array, -limit, limit).astype(kind)


def setup_inputs(seed: int = 0) -> dict:
    splits = jax.random.split(jax.random.key(seed), 10)
    panels = draw_panels(jax.random.fold_in(splits[9], 71), 0)
    root_panels = draw_root_panels(jax.random.fold_in(splits[9], 71), 0)
    low_inverse = draw_low_inverse(jax.random.fold_in(splits[9], 71), 0)
    structure_keys = jax.random.split(jax.random.fold_in(splits[3], 1), NLOW // LD)
    structure_turns = jax.random.permutation(jax.random.fold_in(splits[3], 3), NLOW // LD)
    structure = jax.vmap(lambda own, number: routed_block(jax.random.fold_in(splits[3], 2), own, number, LD, N_SUB, R, CAP, 2))(structure_keys, structure_turns).reshape((NLOW, R))
    owner_map = jax.vmap(lambda own: jax.random.permutation(own, N_SUB))(jax.random.split(splits[4], N_LEAF)).reshape((N_LEAF, N_SUB)).astype(jnp.int32)
    upper_block = draw_upper_block(jax.random.fold_in(splits[9], 71), 0)
    upper_cot = normal_values(splits[6], (UPPER, B, B), 1.0, 6.0, ((0, 512),), jnp.float32)
    root_block = draw_root_block(jax.random.fold_in(splits[9], 71), 0)
    root_cot = normal_values(splits[8], (B, B), 1.0, 6.0, (), jnp.float32)
    return dict(panels=panels, root_panels=root_panels, low_inverse=low_inverse, structure=structure, owner_map=owner_map, upper_block=upper_block, upper_cot=upper_cot, root_block=root_block, root_cot=root_cot)


def adjoint_block(schur, cotangent):
    factor = jnp.linalg.cholesky(schur)
    identity = jnp.eye(schur.shape[0], dtype=schur.dtype)
    inverse = jax.scipy.linalg.solve_triangular(factor, identity, lower=True)
    product = jnp.dot(factor.T, cotangent, precision=lax.Precision.HIGHEST)
    lowered = jnp.tril(product) - 0.5 * jnp.diag(jnp.diag(product))
    adjoint_full = jnp.dot(jnp.dot(inverse.T, lowered, precision=lax.Precision.HIGHEST), inverse, precision=lax.Precision.HIGHEST)
    return (0.5 * (adjoint_full + adjoint_full.T)).astype(jnp.bfloat16)

def reference(panels, root_panels, low_inverse, structure, owner_map, upper_block, upper_cot, root_block, root_cot):
    rows_group = N_SUB * LD
    group_of = (jnp.arange(NLOW, dtype=jnp.int32) // rows_group).astype(jnp.int32)
    target = (group_of[:, None] * N_SUB + owner_map[group_of[:, None], structure]).astype(jnp.int32)
    group_panels = panels.reshape(N_LEAF, rows_group * R, B, W)
    group_target = (target.reshape(N_LEAF, rows_group * R) % N_SUB).astype(jnp.int32)

    def group_gram(pieces):
        blocks, where = pieces
        wide = blocks.astype(jnp.float32)
        grams = jnp.einsum('nbw,ncw->nbc', wide, wide)
        return jax.ops.segment_sum(grams, where, num_segments=N_SUB)
    totals = lax.map(group_gram, (group_panels, group_target)).reshape(UPPER, B, B)
    schur = upper_block - totals

    def one_adjoint(pieces):
        return adjoint_block(pieces[0], pieces[1])
    upper_adjoint = lax.map(one_adjoint, (schur, upper_cot))

    def per_row(pieces):
        blocks, where, inverse_low = pieces
        chosen = upper_adjoint[where].astype(jnp.float32)
        panel_adjoint = (-2.0 * jnp.einsum('rbc,rcw->rbw', chosen, blocks.astype(jnp.float32))).astype(jnp.bfloat16)
        return jnp.einsum('rbw,wv->rbv', panel_adjoint.astype(jnp.float32), inverse_low.astype(jnp.float32)).astype(jnp.bfloat16)
    panel_grad = lax.map(per_row, (panels, target, low_inverse))
    root_wide = root_panels.astype(jnp.float32)
    root_total = jnp.einsum('sbw,scw->bc', root_wide, root_wide)
    root_adjoint = adjoint_block(root_block - root_total, root_cot)
    root_panel_adjoint = (-2.0 * jnp.einsum('bc,scw->sbw', root_adjoint.astype(jnp.float32), root_wide)).astype(jnp.bfloat16)
    root_grad = jnp.einsum('sbw,swv->sbv', root_panel_adjoint.astype(jnp.float32), low_inverse.astype(jnp.float32)).astype(jnp.bfloat16)
    return (panel_grad, root_grad)
```

```python
import jax
import jax.numpy as jnp
from jax import lax
from jax.experimental import pallas as pl
from jax.experimental.pallas import tpu as pltpu
from jax.sharding import PartitionSpec as P

MESH = pl.DeviceIdType.MESH

def _allreduce_kernel(
    x_ref, o_ref, full, a1, a2, a3, rs1, rs2, rs3, rs4, ssem, rsem1, rsem2, rsem3, rsem4, gsem3, gsem2, gsem1
):
    leaf = lax.axis_index("leaf")
    sub = lax.axis_index("sub")
    c = leaf % 2
    y = leaf // 2
    x = sub // 8
    z = sub % 8

    def core_peer():
        return (leaf + 1 - 2 * c, sub)

    def x_peer(xx):
        return (leaf, xx * 8 + z)

    def y_peer(yy):
        return (yy * 2 + c, sub)

    def z_peer(zz):
        return (leaf, x * 8 + zz)

    peers = [core_peer()]
    peers += [x_peer((x + d) % 4) for d in range(1, 4)]
    peers += [y_peer((y + d) % 8) for d in range(1, 8)]
    peers += [z_peer((z + d) % 8) for d in range(1, 8)]
    barrier = pltpu.get_barrier_semaphore()
    for p in peers:
        pl.semaphore_signal(barrier, inc=1, device_id=p, device_id_type=MESH)
    pl.semaphore_wait(barrier, len(peers))

    sends = []

    def send(src, dst, rsem, dev):
        cp = pltpu.make_async_remote_copy(
            src_ref=src, dst_ref=dst, send_sem=ssem.at[len(sends)], recv_sem=rsem, device_id=dev, device_id_type=MESH
        )
        cp.start()
        sends.append(cp)

    def recv_wait(dst, rsem, dev):
        pltpu.make_async_remote_copy(
            src_ref=dst, dst_ref=dst, send_sem=ssem.at[0], recv_sem=rsem, device_id=dev, device_id_type=MESH
        ).wait_recv()

    mine1 = pl.multiple_of(c * 256, 256)
    send(x_ref.at[pl.ds(pl.multiple_of((1 - c) * 256, 256), 256)], rs1, rsem1.at[0], core_peer())
    recv_wait(rs1, rsem1.at[0], core_peer())
    a1[...] = x_ref[pl.ds(mine1, 256), :] + rs1[...]

    for d in range(1, 4):
        xx = (x + d) % 4
        send(a1.at[pl.ds(pl.multiple_of(xx * 64, 64), 64)], rs2.at[x], rsem2.at[x], x_peer(xx))
    for d in range(1, 4):
        xx = (x + d) % 4
        recv_wait(rs2.at[xx], rsem2.at[xx], x_peer(xx))
    rs2[x] = a1[pl.ds(pl.multiple_of(x * 64, 64), 64), :]
    a2[...] = rs2[0] + rs2[1] + rs2[2] + rs2[3]

    for d in range(1, 8):
        yy = (y + d) % 8
        send(a2.at[pl.ds(pl.multiple_of(yy * 8, 8), 8)], rs3.at[y], rsem3.at[y], y_peer(yy))
    for d in range(1, 8):
        yy = (y + d) % 8
        recv_wait(rs3.at[yy], rsem3.at[yy], y_peer(yy))
    rs3[y] = a2[pl.ds(pl.multiple_of(y * 8, 8), 8), :]
    total3 = rs3[0]
    for i in range(1, 8):
        total3 = total3 + rs3[i]
    a3[...] = total3

    for d in range(1, 8):
        zz = (z + d) % 8
        send(a3, rs4.at[z], rsem4.at[z], z_peer(zz))
    for d in range(1, 8):
        zz = (z + d) % 8
        recv_wait(rs4.at[zz], rsem4.at[zz], z_peer(zz))
    rs4[z] = a3[...]
    total4 = rs4[0]
    for i in range(1, 8):
        total4 = total4 + rs4[i]
    base2 = c * 256 + x * 64
    full[pl.ds(pl.multiple_of(base2 + y * 8, 8), 8), :] = total4

    for d in range(1, 8):
        yy = (y + d) % 8
        blk = full.at[pl.ds(pl.multiple_of(base2 + y * 8, 8), 8)]
        send(blk, blk, gsem3.at[y], y_peer(yy))
    for d in range(1, 8):
        yy = (y + d) % 8
        recv_wait(full.at[pl.ds(pl.multiple_of(base2 + yy * 8, 8), 8)], gsem3.at[yy], y_peer(yy))
    for d in range(1, 4):
        xx = (x + d) % 4
        blk = full.at[pl.ds(pl.multiple_of(base2, 64), 64)]
        send(blk, blk, gsem2.at[x], x_peer(xx))
    for d in range(1, 4):
        xx = (x + d) % 4
        recv_wait(full.at[pl.ds(pl.multiple_of(c * 256 + xx * 64, 64), 64)], gsem2.at[xx], x_peer(xx))
    blk = full.at[pl.ds(mine1, 256)]
    send(blk, blk, gsem1.at[0], core_peer())
    recv_wait(full.at[pl.ds(pl.multiple_of((1 - c) * 256, 256), 256)], gsem1.at[0], core_peer())
    for cp in sends:
        cp.wait_send()
    o_ref[...] = full[...]


def allreduce_root(gram):
    flat = gram.reshape(512, 128)
    n_sends = 1 + 3 + 7 + 7 + 7 + 3 + 1
    out = pl.pallas_call(
        _allreduce_kernel,
        out_shape=jax.ShapeDtypeStruct((512, 128), jnp.float32),
        in_specs=[pl.BlockSpec(memory_space=pltpu.VMEM)],
        out_specs=pl.BlockSpec(memory_space=pltpu.VMEM),
        scratch_shapes=[
            pltpu.VMEM((512, 128), jnp.float32),
            pltpu.VMEM((256, 128), jnp.float32),
            pltpu.VMEM((64, 128), jnp.float32),
            pltpu.VMEM((8, 128), jnp.float32),
            pltpu.VMEM((256, 128), jnp.float32),
            pltpu.VMEM((4, 64, 128), jnp.float32),
            pltpu.VMEM((8, 8, 128), jnp.float32),
            pltpu.VMEM((8, 8, 128), jnp.float32),
            pltpu.SemaphoreType.DMA((n_sends,)),
            pltpu.SemaphoreType.DMA((1,)),
            pltpu.SemaphoreType.DMA((4,)),
            pltpu.SemaphoreType.DMA((8,)),
            pltpu.SemaphoreType.DMA((8,)),
            pltpu.SemaphoreType.DMA((8,)),
            pltpu.SemaphoreType.DMA((4,)),
            pltpu.SemaphoreType.DMA((1,)),
        ],
        compiler_params=pltpu.CompilerParams(collective_id=0, has_side_effects=True),
        cost_estimate=pl.CostEstimate(flops=4 * 65536, bytes_accessed=3 * 262144, transcendentals=0),
    )(flat)
    return out.reshape(256, 256)


def adjoint_block(schur, cotangent):
    factor = jnp.linalg.cholesky(schur)
    identity = jnp.eye(schur.shape[0], dtype=schur.dtype)
    inverse = jax.scipy.linalg.solve_triangular(factor, identity, lower=True)
    product = jnp.dot(factor.T, cotangent, precision=lax.Precision.HIGHEST)
    lowered = jnp.tril(product) - 0.5 * jnp.diag(jnp.diag(product))
    adjoint_full = jnp.dot(
        jnp.dot(inverse.T, lowered, precision=lax.Precision.HIGHEST),
        inverse,
        precision=lax.Precision.HIGHEST,
    )
    return (0.5 * (adjoint_full + adjoint_full.T)).astype(jnp.bfloat16)


def body(
    panels,
    root_panels,
    low_inverse,
    structure,
    owner_map,
    upper_block,
    upper_cot,
    root_block,
    root_cot,
):
    devices_sub = lax.axis_size("sub")
    rows_dev, blocks_row, height, breadth = panels.shape
    item_count = rows_dev * blocks_row
    capacity = max(2, 2 * item_count // devices_sub)
    group_id = lax.axis_index("leaf")
    owners = lax.dynamic_index_in_dim(owner_map, group_id, 0, keepdims=False)
    target = jnp.take(owners, structure.reshape(item_count))
    onehot = (target[:, None] == jnp.arange(devices_sub, dtype=jnp.int32)[None, :]).astype(
        jnp.int32
    )
    earlier = jnp.cumsum(onehot, axis=0) - onehot
    slot_id = jnp.sum(earlier * onehot, axis=1)
    position = target * capacity + slot_id
    flat_panels = panels.reshape(item_count, height, breadth)
    outgoing = (
        jnp.zeros((devices_sub * capacity, height, breadth), jnp.bfloat16)
        .at[position]
        .set(flat_panels)
    )
    incoming = lax.all_to_all(outgoing, "sub", split_axis=0, concat_axis=0, tiled=True)
    gram_sum = jnp.einsum("nbw,ncw->bc", incoming, incoming, preferred_element_type=jnp.float32)
    upper_adjoint = adjoint_block(upper_block[0] - gram_sum, upper_cot[0])
    answer = (
        -2.0
        * jnp.einsum("bc,ncw->nbw", upper_adjoint, incoming, preferred_element_type=jnp.float32)
    ).astype(jnp.bfloat16)
    returned = lax.all_to_all(answer, "sub", split_axis=0, concat_axis=0, tiled=True)
    panel_adjoint = returned[position]
    panel_adjoint = panel_adjoint.reshape(rows_dev, blocks_row, height, breadth)
    panel_grad = jnp.einsum(
        "srbw,swv->srbv", panel_adjoint, low_inverse, preferred_element_type=jnp.float32
    ).astype(jnp.bfloat16)
    local_gram = jnp.einsum(
        "sbw,scw->bc", root_panels, root_panels, preferred_element_type=jnp.float32
    )
    root_total = allreduce_root(local_gram)
    root_adjoint = adjoint_block(root_block - root_total, root_cot)
    root_panel_adjoint = (
        -2.0
        * jnp.einsum("bc,scw->sbw", root_adjoint, root_panels, preferred_element_type=jnp.float32)
    ).astype(jnp.bfloat16)
    root_grad = jnp.einsum(
        "sbw,swv->sbv", root_panel_adjoint, low_inverse, preferred_element_type=jnp.float32
    ).astype(jnp.bfloat16)
    return (panel_grad, root_grad)


def solution(mesh):
    in_specs = (
        P(("leaf", "sub"), None, None, None),
        P(("leaf", "sub"), None, None),
        P(("leaf", "sub"), None, None),
        P(("leaf", "sub"), None),
        P(),
        P(("leaf", "sub"), None, None),
        P(("leaf", "sub"), None, None),
        P(),
        P(),
    )
    out_specs = (P(("leaf", "sub"), None, None, None), P(("leaf", "sub"), None, None))
    return jax.shard_map(body, mesh=mesh, in_specs=in_specs, out_specs=out_specs, check_vma=False)
```

```python
import jax
import jax.numpy as jnp
from jax import lax
from jax.experimental import pallas as pl
from jax.experimental.pallas import tpu as pltpu
from jax.sharding import PartitionSpec as P

MESH = pl.DeviceIdType.MESH

def _allreduce_kernel(
    x_ref, o_ref, full, a1, a2, a3, rs1, rs2, rs3, rs4, ssem, rsem1, rsem2, rsem3, rsem4, gsem3, gsem2, gsem1
):
    leaf = lax.axis_index("leaf")
    sub = lax.axis_index("sub")
    c = leaf % 2
    y = leaf // 2
    x = sub // 8
    z = sub % 8

    def core_peer():
        return (leaf + 1 - 2 * c, sub)

    def x_peer(xx):
        return (leaf, xx * 8 + z)

    def y_peer(yy):
        return (yy * 2 + c, sub)

    def z_peer(zz):
        return (leaf, x * 8 + zz)

    peers = [core_peer()]
    peers += [x_peer((x + d) % 4) for d in range(1, 4)]
    peers += [y_peer((y + d) % 8) for d in range(1, 8)]
    peers += [z_peer((z + d) % 8) for d in range(1, 8)]
    barrier = pltpu.get_barrier_semaphore()
    for p in peers:
        pl.semaphore_signal(barrier, inc=1, device_id=p, device_id_type=MESH)
    pl.semaphore_wait(barrier, len(peers))

    sends = []

    def send(src, dst, rsem, dev):
        cp = pltpu.make_async_remote_copy(
            src_ref=src, dst_ref=dst, send_sem=ssem.at[len(sends)], recv_sem=rsem, device_id=dev, device_id_type=MESH
        )
        cp.start()
        sends.append(cp)

    def recv_wait(dst, rsem, dev):
        pltpu.make_async_remote_copy(
            src_ref=dst, dst_ref=dst, send_sem=ssem.at[0], recv_sem=rsem, device_id=dev, device_id_type=MESH
        ).wait_recv()

    mine1 = pl.multiple_of(c * 256, 256)
    send(x_ref.at[pl.ds(pl.multiple_of((1 - c) * 256, 256), 256)], rs1, rsem1.at[0], core_peer())
    recv_wait(rs1, rsem1.at[0], core_peer())
    a1[...] = x_ref[pl.ds(mine1, 256), :] + rs1[...]

    for d in range(1, 4):
        xx = (x + d) % 4
        send(a1.at[pl.ds(pl.multiple_of(xx * 64, 64), 64)], rs2.at[x], rsem2.at[x], x_peer(xx))
    for d in range(1, 4):
        xx = (x + d) % 4
        recv_wait(rs2.at[xx], rsem2.at[xx], x_peer(xx))
    rs2[x] = a1[pl.ds(pl.multiple_of(x * 64, 64), 64), :]
    a2[...] = rs2[0] + rs2[1] + rs2[2] + rs2[3]

    for d in range(1, 8):
        yy = (y + d) % 8
        send(a2.at[pl.ds(pl.multiple_of(yy * 8, 8), 8)], rs3.at[y], rsem3.at[y], y_peer(yy))
    for d in range(1, 8):
        yy = (y + d) % 8
        recv_wait(rs3.at[yy], rsem3.at[yy], y_peer(yy))
    rs3[y] = a2[pl.ds(pl.multiple_of(y * 8, 8), 8), :]
    total3 = rs3[0]
    for i in range(1, 8):
        total3 = total3 + rs3[i]
    a3[...] = total3

    for d in range(1, 8):
        zz = (z + d) % 8
        send(a3, rs4.at[z], rsem4.at[z], z_peer(zz))
    for d in range(1, 8):
        zz = (z + d) % 8
        recv_wait(rs4.at[zz], rsem4.at[zz], z_peer(zz))
    rs4[z] = a3[...]
    total4 = rs4[0]
    for i in range(1, 8):
        total4 = total4 + rs4[i]
    base2 = c * 256 + x * 64
    full[pl.ds(pl.multiple_of(base2 + y * 8, 8), 8), :] = total4

    for d in range(1, 8):
        yy = (y + d) % 8
        blk = full.at[pl.ds(pl.multiple_of(base2 + y * 8, 8), 8)]
        send(blk, blk, gsem3.at[y], y_peer(yy))
    for d in range(1, 8):
        yy = (y + d) % 8
        recv_wait(full.at[pl.ds(pl.multiple_of(base2 + yy * 8, 8), 8)], gsem3.at[yy], y_peer(yy))
    for d in range(1, 4):
        xx = (x + d) % 4
        blk = full.at[pl.ds(pl.multiple_of(base2, 64), 64)]
        send(blk, blk, gsem2.at[x], x_peer(xx))
    for d in range(1, 4):
        xx = (x + d) % 4
        recv_wait(full.at[pl.ds(pl.multiple_of(c * 256 + xx * 64, 64), 64)], gsem2.at[xx], x_peer(xx))
    blk = full.at[pl.ds(mine1, 256)]
    send(blk, blk, gsem1.at[0], core_peer())
    recv_wait(full.at[pl.ds(pl.multiple_of((1 - c) * 256, 256), 256)], gsem1.at[0], core_peer())
    for cp in sends:
        cp.wait_send()
    o_ref[...] = full[...]


def allreduce_root(gram):
    flat = gram.reshape(512, 128)
    n_sends = 1 + 3 + 7 + 7 + 7 + 3 + 1
    out = pl.pallas_call(
        _allreduce_kernel,
        out_shape=jax.ShapeDtypeStruct((512, 128), jnp.float32),
        in_specs=[pl.BlockSpec(memory_space=pltpu.VMEM)],
        out_specs=pl.BlockSpec(memory_space=pltpu.VMEM),
        scratch_shapes=[
            pltpu.VMEM((512, 128), jnp.float32),
            pltpu.VMEM((256, 128), jnp.float32),
            pltpu.VMEM((64, 128), jnp.float32),
            pltpu.VMEM((8, 128), jnp.float32),
            pltpu.VMEM((256, 128), jnp.float32),
            pltpu.VMEM((4, 64, 128), jnp.float32),
            pltpu.VMEM((8, 8, 128), jnp.float32),
            pltpu.VMEM((8, 8, 128), jnp.float32),
            pltpu.SemaphoreType.DMA((n_sends,)),
            pltpu.SemaphoreType.DMA((1,)),
            pltpu.SemaphoreType.DMA((4,)),
            pltpu.SemaphoreType.DMA((8,)),
            pltpu.SemaphoreType.DMA((8,)),
            pltpu.SemaphoreType.DMA((8,)),
            pltpu.SemaphoreType.DMA((4,)),
            pltpu.SemaphoreType.DMA((1,)),
        ],
        compiler_params=pltpu.CompilerParams(collective_id=0, has_side_effects=True),
        cost_estimate=pl.CostEstimate(flops=4 * 65536, bytes_accessed=3 * 262144, transcendentals=0),
    )(flat)
    return out.reshape(256, 256)


def adjoint_block(schur, cotangent):
    factor = jnp.linalg.cholesky(schur)
    identity = jnp.eye(schur.shape[0], dtype=schur.dtype)
    inverse = jax.scipy.linalg.solve_triangular(factor, identity, lower=True)
    product = jnp.dot(factor.T, cotangent, precision=lax.Precision.HIGHEST)
    lowered = jnp.tril(product) - 0.5 * jnp.diag(jnp.diag(product))
    adjoint_full = jnp.dot(
        jnp.dot(inverse.T, lowered, precision=lax.Precision.HIGHEST),
        inverse,
        precision=lax.Precision.HIGHEST,
    )
    return (0.5 * (adjoint_full + adjoint_full.T)).astype(jnp.bfloat16)


def body(
    panels,
    root_panels,
    low_inverse,
    structure,
    owner_map,
    upper_block,
    upper_cot,
    root_block,
    root_cot,
):
    devices_sub = lax.axis_size("sub")
    local_gram = jnp.einsum(
        "sbw,scw->bc", root_panels, root_panels, preferred_element_type=jnp.float32
    )
    root_total = allreduce_root(local_gram)
    root_total, panels = lax.optimization_barrier((root_total, panels))
    root_adjoint = adjoint_block(root_block - root_total, root_cot)
    rows_dev, blocks_row, height, breadth = panels.shape
    item_count = rows_dev * blocks_row
    capacity = max(2, 2 * item_count // devices_sub)
    group_id = lax.axis_index("leaf")
    owners = lax.dynamic_index_in_dim(owner_map, group_id, 0, keepdims=False)
    target = jnp.take(owners, structure.reshape(item_count))
    onehot = (target[:, None] == jnp.arange(devices_sub, dtype=jnp.int32)[None, :]).astype(
        jnp.int32
    )
    earlier = jnp.cumsum(onehot, axis=0) - onehot
    slot_id = jnp.sum(earlier * onehot, axis=1)
    position = target * capacity + slot_id
    flat_panels = panels.reshape(item_count, height, breadth)
    outgoing = (
        jnp.zeros((devices_sub * capacity, height, breadth), jnp.bfloat16)
        .at[position]
        .set(flat_panels)
    )
    incoming = lax.all_to_all(outgoing, "sub", split_axis=0, concat_axis=0, tiled=True)
    root_adjoint, incoming = lax.optimization_barrier((root_adjoint, incoming))
    gram_sum = jnp.einsum("nbw,ncw->bc", incoming, incoming, preferred_element_type=jnp.float32)
    upper_adjoint = adjoint_block(upper_block[0] - gram_sum, upper_cot[0])
    answer = (
        -2.0
        * jnp.einsum("bc,ncw->nbw", upper_adjoint, incoming, preferred_element_type=jnp.float32)
    ).astype(jnp.bfloat16)
    returned = lax.all_to_all(answer, "sub", split_axis=0, concat_axis=0, tiled=True)
    panel_adjoint = returned[position]
    panel_adjoint = panel_adjoint.reshape(rows_dev, blocks_row, height, breadth)
    panel_grad = jnp.einsum(
        "srbw,swv->srbv", panel_adjoint, low_inverse, preferred_element_type=jnp.float32
    ).astype(jnp.bfloat16)
    root_panel_adjoint = (
        -2.0
        * jnp.einsum("bc,scw->sbw", root_adjoint, root_panels, preferred_element_type=jnp.float32)
    ).astype(jnp.bfloat16)
    root_grad = jnp.einsum(
        "sbw,swv->sbv", root_panel_adjoint, low_inverse, preferred_element_type=jnp.float32
    ).astype(jnp.bfloat16)
    return (panel_grad, root_grad)


def solution(mesh):
    in_specs = (
        P(("leaf", "sub"), None, None, None),
        P(("leaf", "sub"), None, None),
        P(("leaf", "sub"), None, None),
        P(("leaf", "sub"), None),
        P(),
        P(("leaf", "sub"), None, None),
        P(("leaf", "sub"), None, None),
        P(),
        P(),
    )
    out_specs = (P(("leaf", "sub"), None, None, None), P(("leaf", "sub"), None, None))
    return jax.shard_map(body, mesh=mesh, in_specs=in_specs, out_specs=out_specs, check_vma=False)
```

```python
import jax
import jax.numpy as jnp
from jax import lax
from jax.experimental import pallas as pl
from jax.experimental.pallas import tpu as pltpu
from jax.sharding import PartitionSpec as P

MESH = pl.DeviceIdType.MESH

def _allreduce_kernel(
    x_ref, o_ref, full, a1, a2, a3, rs1, rs2, rs3, rs4, ssem, rsem1, rsem2, rsem3, rsem4, gsem3, gsem2, gsem1
):
    leaf = lax.axis_index("leaf")
    sub = lax.axis_index("sub")
    c = leaf % 2
    y = leaf // 2
    x = sub // 8
    z = sub % 8

    def core_peer():
        return (leaf + 1 - 2 * c, sub)

    def x_peer(xx):
        return (leaf, xx * 8 + z)

    def y_peer(yy):
        return (yy * 2 + c, sub)

    def z_peer(zz):
        return (leaf, x * 8 + zz)

    peers = [core_peer()]
    peers += [x_peer((x + d) % 4) for d in range(1, 4)]
    peers += [y_peer((y + d) % 8) for d in range(1, 8)]
    peers += [z_peer((z + d) % 8) for d in range(1, 8)]
    barrier = pltpu.get_barrier_semaphore()
    for p in peers:
        pl.semaphore_signal(barrier, inc=1, device_id=p, device_id_type=MESH)
    pl.semaphore_wait(barrier, len(peers))

    sends = []

    def send(src, dst, rsem, dev):
        cp = pltpu.make_async_remote_copy(
            src_ref=src, dst_ref=dst, send_sem=ssem.at[len(sends)], recv_sem=rsem, device_id=dev, device_id_type=MESH
        )
        cp.start()
        sends.append(cp)

    def recv_wait(dst, rsem, dev):
        pltpu.make_async_remote_copy(
            src_ref=dst, dst_ref=dst, send_sem=ssem.at[0], recv_sem=rsem, device_id=dev, device_id_type=MESH
        ).wait_recv()

    mine1 = pl.multiple_of(c * 256, 256)
    send(x_ref.at[pl.ds(pl.multiple_of((1 - c) * 256, 256), 256)], rs1, rsem1.at[0], core_peer())
    recv_wait(rs1, rsem1.at[0], core_peer())
    a1[...] = x_ref[pl.ds(mine1, 256), :] + rs1[...]

    for d in range(1, 4):
        xx = (x + d) % 4
        send(a1.at[pl.ds(pl.multiple_of(xx * 64, 64), 64)], rs2.at[x], rsem2.at[x], x_peer(xx))
    for d in range(1, 4):
        xx = (x + d) % 4
        recv_wait(rs2.at[xx], rsem2.at[xx], x_peer(xx))
    rs2[x] = a1[pl.ds(pl.multiple_of(x * 64, 64), 64), :]
    a2[...] = rs2[0] + rs2[1] + rs2[2] + rs2[3]

    for d in range(1, 8):
        yy = (y + d) % 8
        send(a2.at[pl.ds(pl.multiple_of(yy * 8, 8), 8)], rs3.at[y], rsem3.at[y], y_peer(yy))
    for d in range(1, 8):
        yy = (y + d) % 8
        recv_wait(rs3.at[yy], rsem3.at[yy], y_peer(yy))
    rs3[y] = a2[pl.ds(pl.multiple_of(y * 8, 8), 8), :]
    total3 = rs3[0]
    for i in range(1, 8):
        total3 = total3 + rs3[i]
    a3[...] = total3

    for d in range(1, 8):
        zz = (z + d) % 8
        send(a3, rs4.at[z], rsem4.at[z], z_peer(zz))
    for d in range(1, 8):
        zz = (z + d) % 8
        recv_wait(rs4.at[zz], rsem4.at[zz], z_peer(zz))
    rs4[z] = a3[...]
    total4 = rs4[0]
    for i in range(1, 8):
        total4 = total4 + rs4[i]
    base2 = c * 256 + x * 64
    full[pl.ds(pl.multiple_of(base2 + y * 8, 8), 8), :] = total4

    for d in range(1, 8):
        yy = (y + d) % 8
        blk = full.at[pl.ds(pl.multiple_of(base2 + y * 8, 8), 8)]
        send(blk, blk, gsem3.at[y], y_peer(yy))
    for d in range(1, 8):
        yy = (y + d) % 8
        recv_wait(full.at[pl.ds(pl.multiple_of(base2 + yy * 8, 8), 8)], gsem3.at[yy], y_peer(yy))
    for d in range(1, 4):
        xx = (x + d) % 4
        blk = full.at[pl.ds(pl.multiple_of(base2, 64), 64)]
        send(blk, blk, gsem2.at[x], x_peer(xx))
    for d in range(1, 4):
        xx = (x + d) % 4
        recv_wait(full.at[pl.ds(pl.multiple_of(c * 256 + xx * 64, 64), 64)], gsem2.at[xx], x_peer(xx))
    blk = full.at[pl.ds(mine1, 256)]
    send(blk, blk, gsem1.at[0], core_peer())
    recv_wait(full.at[pl.ds(pl.multiple_of((1 - c) * 256, 256), 256)], gsem1.at[0], core_peer())
    for cp in sends:
        cp.wait_send()
    o_ref[...] = full[...]


def allreduce_root(gram):
    flat = gram.reshape(512, 128)
    n_sends = 1 + 3 + 7 + 7 + 7 + 3 + 1
    out = pl.pallas_call(
        _allreduce_kernel,
        out_shape=jax.ShapeDtypeStruct((512, 128), jnp.float32),
        in_specs=[pl.BlockSpec(memory_space=pltpu.VMEM)],
        out_specs=pl.BlockSpec(memory_space=pltpu.VMEM),
        scratch_shapes=[
            pltpu.VMEM((512, 128), jnp.float32),
            pltpu.VMEM((256, 128), jnp.float32),
            pltpu.VMEM((64, 128), jnp.float32),
            pltpu.VMEM((8, 128), jnp.float32),
            pltpu.VMEM((256, 128), jnp.float32),
            pltpu.VMEM((4, 64, 128), jnp.float32),
            pltpu.VMEM((8, 8, 128), jnp.float32),
            pltpu.VMEM((8, 8, 128), jnp.float32),
            pltpu.SemaphoreType.DMA((n_sends,)),
            pltpu.SemaphoreType.DMA((1,)),
            pltpu.SemaphoreType.DMA((4,)),
            pltpu.SemaphoreType.DMA((8,)),
            pltpu.SemaphoreType.DMA((8,)),
            pltpu.SemaphoreType.DMA((8,)),
            pltpu.SemaphoreType.DMA((4,)),
            pltpu.SemaphoreType.DMA((1,)),
        ],
        compiler_params=pltpu.CompilerParams(collective_id=0, has_side_effects=True),
        cost_estimate=pl.CostEstimate(flops=4 * 65536, bytes_accessed=3 * 262144, transcendentals=0),
    )(flat)
    return out.reshape(256, 256)


def _gather_kernel(a_ref, o_ref, gathered, ssem, rsz, rsx, lsem):
    leaf = lax.axis_index("leaf")
    sub = lax.axis_index("sub")
    x = sub // 8
    z = sub % 8
    peers = [(leaf, x * 8 + (z + d) % 8) for d in range(1, 8)]
    peers += [(leaf, ((x + d) % 4) * 8 + z) for d in range(1, 4)]
    barrier = pltpu.get_barrier_semaphore()
    for p in peers:
        pl.semaphore_signal(barrier, inc=1, device_id=p, device_id_type=MESH)
    pl.semaphore_wait(barrier, len(peers))

    sends = []

    def send(src, dst, rsem, dev):
        cp = pltpu.make_async_remote_copy(
            src_ref=src, dst_ref=dst, send_sem=ssem.at[len(sends)], recv_sem=rsem, device_id=dev, device_id_type=MESH
        )
        cp.start()
        sends.append(cp)

    def recv_wait(dst, rsem, dev):
        pltpu.make_async_remote_copy(
            src_ref=dst, dst_ref=dst, send_sem=ssem.at[0], recv_sem=rsem, device_id=dev, device_id_type=MESH
        ).wait_recv()

    for d in range(1, 8):
        zz = (z + d) % 8
        send(a_ref, gathered.at[x * 8 + z], rsz.at[z], (leaf, x * 8 + zz))
    own = pltpu.make_async_copy(a_ref, gathered.at[x * 8 + z], lsem.at[0])
    own.start()
    for d in range(1, 8):
        zz = (z + d) % 8
        recv_wait(gathered.at[x * 8 + zz], rsz.at[zz], (leaf, x * 8 + zz))
    own.wait()
    column = gathered.at[pl.ds(pl.multiple_of(x * 8, 8), 8)]
    for d in range(1, 4):
        xx = (x + d) % 4
        send(column, column, rsx.at[x], (leaf, xx * 8 + z))
    for d in range(1, 4):
        xx = (x + d) % 4
        recv_wait(gathered.at[pl.ds(pl.multiple_of(xx * 8, 8), 8)], rsx.at[xx], (leaf, xx * 8 + z))
    for cp in sends:
        cp.wait_send()
    o_ref[...] = gathered[...]


def gather_sub(block):
    rows = block.shape[0]
    return pl.pallas_call(
        _gather_kernel,
        out_shape=jax.ShapeDtypeStruct((32, rows, 128), block.dtype),
        in_specs=[pl.BlockSpec(memory_space=pltpu.VMEM)],
        out_specs=pl.BlockSpec(memory_space=pltpu.VMEM),
        scratch_shapes=[
            pltpu.VMEM((32, rows, 128), block.dtype),
            pltpu.SemaphoreType.DMA((10,)),
            pltpu.SemaphoreType.DMA((8,)),
            pltpu.SemaphoreType.DMA((4,)),
            pltpu.SemaphoreType.DMA((1,)),
        ],
        compiler_params=pltpu.CompilerParams(collective_id=1, has_side_effects=True),
        cost_estimate=pl.CostEstimate(flops=0, bytes_accessed=2 * 32 * rows * 128 * 2, transcendentals=0),
    )(block)


def pack_symmetric(a):
    h = a.shape[0] // 2
    row = lax.broadcasted_iota(jnp.int32, (h, h), 0)
    col = lax.broadcasted_iota(jnp.int32, (h, h), 1)
    folded = jnp.where(col <= row, a[:h, :h], a[h:, h:])
    diag = jnp.where(row == col, a[h:, h:], jnp.zeros_like(a[h:, h:]))
    diag_row = jnp.sum(diag.astype(jnp.float32), axis=0, keepdims=True).astype(a.dtype)
    pad = jnp.zeros((15, h), a.dtype)
    return jnp.concatenate([folded, a[h:, :h], diag_row, pad], axis=0)


def unpack_symmetric(packed):
    h = 128
    folded = packed[:, :h, :]
    lower = packed[:, h:2 * h, :]
    diag_row = packed[:, 2 * h:2 * h + 1, :]
    row = lax.broadcasted_iota(jnp.int32, (1, h, h), 1)
    col = lax.broadcasted_iota(jnp.int32, (1, h, h), 2)
    folded_t = jnp.swapaxes(folded, 1, 2)
    top_left = jnp.where(col <= row, folded, folded_t)
    bottom_right = jnp.where(col > row, folded, jnp.where(col < row, folded_t, diag_row))
    top = jnp.concatenate([top_left, jnp.swapaxes(lower, 1, 2)], axis=2)
    bottom = jnp.concatenate([lower, bottom_right], axis=2)
    return jnp.concatenate([top, bottom], axis=1)


def adjoint_block(schur, cotangent):
    factor = jnp.linalg.cholesky(schur)
    identity = jnp.eye(schur.shape[0], dtype=schur.dtype)
    inverse = jax.scipy.linalg.solve_triangular(factor, identity, lower=True)
    product = jnp.dot(factor.T, cotangent, precision=lax.Precision.HIGHEST)
    lowered = jnp.tril(product) - 0.5 * jnp.diag(jnp.diag(product))
    adjoint_full = jnp.dot(
        jnp.dot(inverse.T, lowered, precision=lax.Precision.HIGHEST),
        inverse,
        precision=lax.Precision.HIGHEST,
    )
    return (0.5 * (adjoint_full + adjoint_full.T)).astype(jnp.bfloat16)


def body(
    panels,
    root_panels,
    low_inverse,
    structure,
    owner_map,
    upper_block,
    upper_cot,
    root_block,
    root_cot,
):
    devices_sub = lax.axis_size("sub")
    local_gram = jnp.einsum(
        "sbw,scw->bc", root_panels, root_panels, preferred_element_type=jnp.float32
    )
    root_total = allreduce_root(local_gram)
    root_total, panels = lax.optimization_barrier((root_total, panels))
    root_adjoint = adjoint_block(root_block - root_total, root_cot)
    rows_dev, blocks_row, height, breadth = panels.shape
    item_count = rows_dev * blocks_row
    capacity = max(2, 2 * item_count // devices_sub)
    group_id = lax.axis_index("leaf")
    owners = lax.dynamic_index_in_dim(owner_map, group_id, 0, keepdims=False)
    target = jnp.take(owners, structure.reshape(item_count))
    onehot = (target[:, None] == jnp.arange(devices_sub, dtype=jnp.int32)[None, :]).astype(
        jnp.int32
    )
    earlier = jnp.cumsum(onehot, axis=0) - onehot
    slot_id = jnp.sum(earlier * onehot, axis=1)
    position = target * capacity + slot_id
    flat_panels = panels.reshape(item_count, height, breadth)
    outgoing = (
        jnp.zeros((devices_sub * capacity, height, breadth), jnp.bfloat16)
        .at[position]
        .set(flat_panels)
    )
    incoming = lax.all_to_all(outgoing, "sub", split_axis=0, concat_axis=0, tiled=True)
    root_adjoint, incoming = lax.optimization_barrier((root_adjoint, incoming))
    gram_sum = jnp.einsum("nbw,ncw->bc", incoming, incoming, preferred_element_type=jnp.float32)
    upper_adjoint = adjoint_block(upper_block[0] - gram_sum, upper_cot[0])
    every_adjoint = unpack_symmetric(gather_sub(pack_symmetric(upper_adjoint)))
    chosen = jnp.take(every_adjoint, target, axis=0)
    panel_adjoint = (
        -2.0
        * jnp.einsum("nbc,ncw->nbw", chosen, flat_panels, preferred_element_type=jnp.float32)
    ).astype(jnp.bfloat16)
    panel_adjoint = panel_adjoint.reshape(rows_dev, blocks_row, height, breadth)
    panel_grad = jnp.einsum(
        "srbw,swv->srbv", panel_adjoint, low_inverse, preferred_element_type=jnp.float32
    ).astype(jnp.bfloat16)
    root_panel_adjoint = (
        -2.0
        * jnp.einsum("bc,scw->sbw", root_adjoint, root_panels, preferred_element_type=jnp.float32)
    ).astype(jnp.bfloat16)
    root_grad = jnp.einsum(
        "sbw,swv->sbv", root_panel_adjoint, low_inverse, preferred_element_type=jnp.float32
    ).astype(jnp.bfloat16)
    return (panel_grad, root_grad)


def solution(mesh):
    in_specs = (
        P(("leaf", "sub"), None, None, None),
        P(("leaf", "sub"), None, None),
        P(("leaf", "sub"), None, None),
        P(("leaf", "sub"), None),
        P(),
        P(("leaf", "sub"), None, None),
        P(("leaf", "sub"), None, None),
        P(),
        P(),
    )
    out_specs = (P(("leaf", "sub"), None, None, None), P(("leaf", "sub"), None, None))
    return jax.shard_map(body, mesh=mesh, in_specs=in_specs, out_specs=out_specs, check_vma=False)
```

```python
import jax
import jax.numpy as jnp
from jax import lax
from jax.experimental import pallas as pl
from jax.experimental.pallas import tpu as pltpu
from jax.sharding import PartitionSpec as P

MESH = pl.DeviceIdType.MESH

def _allreduce_kernel(
    x_ref, o_ref, full, a1, a2, a3, rs1, rs2, rs3, rs4, ssem, rsem1, rsem2, rsem3, rsem4, gsem3, gsem2, gsem1
):
    leaf = lax.axis_index("leaf")
    sub = lax.axis_index("sub")
    c = leaf % 2
    y = leaf // 2
    x = sub // 8
    z = sub % 8

    def core_peer():
        return (leaf + 1 - 2 * c, sub)

    def x_peer(xx):
        return (leaf, xx * 8 + z)

    def y_peer(yy):
        return (yy * 2 + c, sub)

    def z_peer(zz):
        return (leaf, x * 8 + zz)

    peers = [core_peer()]
    peers += [x_peer((x + d) % 4) for d in range(1, 4)]
    peers += [y_peer((y + d) % 8) for d in range(1, 8)]
    peers += [z_peer((z + d) % 8) for d in range(1, 8)]
    barrier = pltpu.get_barrier_semaphore()
    for p in peers:
        pl.semaphore_signal(barrier, inc=1, device_id=p, device_id_type=MESH)
    pl.semaphore_wait(barrier, len(peers))

    sends = []

    def send(src, dst, rsem, dev):
        cp = pltpu.make_async_remote_copy(
            src_ref=src, dst_ref=dst, send_sem=ssem.at[len(sends)], recv_sem=rsem, device_id=dev, device_id_type=MESH
        )
        cp.start()
        sends.append(cp)

    def recv_wait(dst, rsem, dev):
        pltpu.make_async_remote_copy(
            src_ref=dst, dst_ref=dst, send_sem=ssem.at[0], recv_sem=rsem, device_id=dev, device_id_type=MESH
        ).wait_recv()

    mine1 = pl.multiple_of(c * 256, 256)
    send(x_ref.at[pl.ds(pl.multiple_of((1 - c) * 256, 256), 256)], rs1, rsem1.at[0], core_peer())
    recv_wait(rs1, rsem1.at[0], core_peer())
    a1[...] = x_ref[pl.ds(mine1, 256), :] + rs1[...]

    for d in range(1, 4):
        xx = (x + d) % 4
        send(a1.at[pl.ds(pl.multiple_of(xx * 64, 64), 64)], rs2.at[x], rsem2.at[x], x_peer(xx))
    for d in range(1, 4):
        xx = (x + d) % 4
        recv_wait(rs2.at[xx], rsem2.at[xx], x_peer(xx))
    rs2[x] = a1[pl.ds(pl.multiple_of(x * 64, 64), 64), :]
    a2[...] = rs2[0] + rs2[1] + rs2[2] + rs2[3]

    for d in range(1, 8):
        yy = (y + d) % 8
        send(a2.at[pl.ds(pl.multiple_of(yy * 8, 8), 8)], rs3.at[y], rsem3.at[y], y_peer(yy))
    for d in range(1, 8):
        yy = (y + d) % 8
        recv_wait(rs3.at[yy], rsem3.at[yy], y_peer(yy))
    rs3[y] = a2[pl.ds(pl.multiple_of(y * 8, 8), 8), :]
    total3 = rs3[0]
    for i in range(1, 8):
        total3 = total3 + rs3[i]
    a3[...] = total3

    for d in range(1, 8):
        zz = (z + d) % 8
        send(a3, rs4.at[z], rsem4.at[z], z_peer(zz))
    for d in range(1, 8):
        zz = (z + d) % 8
        recv_wait(rs4.at[zz], rsem4.at[zz], z_peer(zz))
    rs4[z] = a3[...]
    total4 = rs4[0]
    for i in range(1, 8):
        total4 = total4 + rs4[i]
    base2 = c * 256 + x * 64
    full[pl.ds(pl.multiple_of(base2 + y * 8, 8), 8), :] = total4

    for d in range(1, 8):
        yy = (y + d) % 8
        blk = full.at[pl.ds(pl.multiple_of(base2 + y * 8, 8), 8)]
        send(blk, blk, gsem3.at[y], y_peer(yy))
    for d in range(1, 8):
        yy = (y + d) % 8
        recv_wait(full.at[pl.ds(pl.multiple_of(base2 + yy * 8, 8), 8)], gsem3.at[yy], y_peer(yy))
    for d in range(1, 4):
        xx = (x + d) % 4
        blk = full.at[pl.ds(pl.multiple_of(base2, 64), 64)]
        send(blk, blk, gsem2.at[x], x_peer(xx))
    for d in range(1, 4):
        xx = (x + d) % 4
        recv_wait(full.at[pl.ds(pl.multiple_of(c * 256 + xx * 64, 64), 64)], gsem2.at[xx], x_peer(xx))
    blk = full.at[pl.ds(mine1, 256)]
    send(blk, blk, gsem1.at[0], core_peer())
    recv_wait(full.at[pl.ds(pl.multiple_of((1 - c) * 256, 256), 256)], gsem1.at[0], core_peer())
    for cp in sends:
        cp.wait_send()
    o_ref[...] = full[...]


def allreduce_root(gram):
    flat = gram.reshape(512, 128)
    n_sends = 1 + 3 + 7 + 7 + 7 + 3 + 1
    out = pl.pallas_call(
        _allreduce_kernel,
        out_shape=jax.ShapeDtypeStruct((512, 128), jnp.float32),
        in_specs=[pl.BlockSpec(memory_space=pltpu.VMEM)],
        out_specs=pl.BlockSpec(memory_space=pltpu.VMEM),
        scratch_shapes=[
            pltpu.VMEM((512, 128), jnp.float32),
            pltpu.VMEM((256, 128), jnp.float32),
            pltpu.VMEM((64, 128), jnp.float32),
            pltpu.VMEM((8, 128), jnp.float32),
            pltpu.VMEM((256, 128), jnp.float32),
            pltpu.VMEM((4, 64, 128), jnp.float32),
            pltpu.VMEM((8, 8, 128), jnp.float32),
            pltpu.VMEM((8, 8, 128), jnp.float32),
            pltpu.SemaphoreType.DMA((n_sends,)),
            pltpu.SemaphoreType.DMA((1,)),
            pltpu.SemaphoreType.DMA((4,)),
            pltpu.SemaphoreType.DMA((8,)),
            pltpu.SemaphoreType.DMA((8,)),
            pltpu.SemaphoreType.DMA((8,)),
            pltpu.SemaphoreType.DMA((4,)),
            pltpu.SemaphoreType.DMA((1,)),
        ],
        compiler_params=pltpu.CompilerParams(collective_id=0, has_side_effects=True),
        cost_estimate=pl.CostEstimate(flops=4 * 65536, bytes_accessed=3 * 262144, transcendentals=0),
    )(flat)
    return out.reshape(256, 256)


def _gather_kernel(a_ref, o_ref, gathered, ssem, rsz, rsx, lsem):
    leaf = lax.axis_index("leaf")
    sub = lax.axis_index("sub")
    x = sub // 8
    z = sub % 8
    peers = [(leaf, x * 8 + (z + d) % 8) for d in range(1, 8)]
    peers += [(leaf, ((x + d) % 4) * 8 + z) for d in range(1, 4)]
    barrier = pltpu.get_barrier_semaphore()
    for p in peers:
        pl.semaphore_signal(barrier, inc=1, device_id=p, device_id_type=MESH)
    pl.semaphore_wait(barrier, len(peers))

    sends = []

    def send(src, dst, rsem, dev):
        cp = pltpu.make_async_remote_copy(
            src_ref=src, dst_ref=dst, send_sem=ssem.at[len(sends)], recv_sem=rsem, device_id=dev, device_id_type=MESH
        )
        cp.start()
        sends.append(cp)

    def recv_wait(dst, rsem, dev):
        pltpu.make_async_remote_copy(
            src_ref=dst, dst_ref=dst, send_sem=ssem.at[0], recv_sem=rsem, device_id=dev, device_id_type=MESH
        ).wait_recv()

    for d in range(1, 8):
        zz = (z + d) % 8
        send(a_ref, gathered.at[x * 8 + z], rsz.at[z], (leaf, x * 8 + zz))
    own = pltpu.make_async_copy(a_ref, gathered.at[x * 8 + z], lsem.at[0])
    own.start()
    for d in range(1, 8):
        zz = (z + d) % 8
        recv_wait(gathered.at[x * 8 + zz], rsz.at[zz], (leaf, x * 8 + zz))
    own.wait()
    column = gathered.at[pl.ds(pl.multiple_of(x * 8, 8), 8)]
    for d in range(1, 4):
        xx = (x + d) % 4
        send(column, column, rsx.at[x], (leaf, xx * 8 + z))
    for d in range(1, 4):
        xx = (x + d) % 4
        recv_wait(gathered.at[pl.ds(pl.multiple_of(xx * 8, 8), 8)], rsx.at[xx], (leaf, xx * 8 + z))
    for cp in sends:
        cp.wait_send()
    o_ref[...] = gathered[...]


def gather_sub(block):
    rows = block.shape[0]
    return pl.pallas_call(
        _gather_kernel,
        out_shape=jax.ShapeDtypeStruct((32, rows, 128), block.dtype),
        in_specs=[pl.BlockSpec(memory_space=pltpu.VMEM)],
        out_specs=pl.BlockSpec(memory_space=pltpu.VMEM),
        scratch_shapes=[
            pltpu.VMEM((32, rows, 128), block.dtype),
            pltpu.SemaphoreType.DMA((10,)),
            pltpu.SemaphoreType.DMA((8,)),
            pltpu.SemaphoreType.DMA((4,)),
            pltpu.SemaphoreType.DMA((1,)),
        ],
        compiler_params=pltpu.CompilerParams(collective_id=1, has_side_effects=True),
        cost_estimate=pl.CostEstimate(flops=0, bytes_accessed=2 * 32 * rows * 128 * 2, transcendentals=0),
    )(block)


def pack_symmetric(a):
    h = a.shape[0] // 2
    row = lax.broadcasted_iota(jnp.int32, (h, h), 0)
    col = lax.broadcasted_iota(jnp.int32, (h, h), 1)
    folded = jnp.where(col <= row, a[:h, :h], a[h:, h:])
    diag = jnp.where(row == col, a[h:, h:], jnp.zeros_like(a[h:, h:]))
    diag_row = jnp.sum(diag.astype(jnp.float32), axis=0, keepdims=True).astype(a.dtype)
    pad = jnp.zeros((15, h), a.dtype)
    return jnp.concatenate([folded, a[h:, :h], diag_row, pad], axis=0)


def unpack_symmetric(packed):
    h = 128
    folded = packed[:, :h, :]
    lower = packed[:, h:2 * h, :]
    diag_row = packed[:, 2 * h:2 * h + 1, :]
    row = lax.broadcasted_iota(jnp.int32, (1, h, h), 1)
    col = lax.broadcasted_iota(jnp.int32, (1, h, h), 2)
    folded_t = jnp.swapaxes(folded, 1, 2)
    top_left = jnp.where(col <= row, folded, folded_t)
    bottom_right = jnp.where(col > row, folded, jnp.where(col < row, folded_t, diag_row))
    top = jnp.concatenate([top_left, jnp.swapaxes(lower, 1, 2)], axis=2)
    bottom = jnp.concatenate([lower, bottom_right], axis=2)
    return jnp.concatenate([top, bottom], axis=1)


def _dot(a, b):
    return jnp.dot(a, b, precision=lax.Precision.HIGHEST)


def factor_and_inverse(schur):
    h = schur.shape[0] // 2
    identity = jnp.eye(h, dtype=schur.dtype)
    f11 = jnp.linalg.cholesky(schur[:h, :h])
    i11 = jax.scipy.linalg.solve_triangular(f11, identity, lower=True)
    f21 = _dot(schur[h:, :h], i11.T)
    f22 = jnp.linalg.cholesky(schur[h:, h:] - _dot(f21, f21.T))
    i22 = jax.scipy.linalg.solve_triangular(f22, identity, lower=True)
    i21 = -_dot(_dot(i22, f21), i11)
    zero = jnp.zeros((h, h), schur.dtype)
    factor = jnp.concatenate([jnp.concatenate([f11, zero], 1), jnp.concatenate([f21, f22], 1)], 0)
    inverse = jnp.concatenate([jnp.concatenate([i11, zero], 1), jnp.concatenate([i21, i22], 1)], 0)
    return factor, inverse


def adjoint_block(schur, cotangent):
    factor, inverse = factor_and_inverse(schur)
    product = jnp.dot(factor.T, cotangent, precision=lax.Precision.HIGHEST)
    lowered = jnp.tril(product) - 0.5 * jnp.diag(jnp.diag(product))
    adjoint_full = jnp.dot(
        jnp.dot(inverse.T, lowered, precision=lax.Precision.HIGHEST),
        inverse,
        precision=lax.Precision.HIGHEST,
    )
    return (0.5 * (adjoint_full + adjoint_full.T)).astype(jnp.bfloat16)


def body(
    panels,
    root_panels,
    low_inverse,
    structure,
    owner_map,
    upper_block,
    upper_cot,
    root_block,
    root_cot,
):
    devices_sub = lax.axis_size("sub")
    local_gram = jnp.einsum(
        "sbw,scw->bc", root_panels, root_panels, preferred_element_type=jnp.float32
    )
    root_total = allreduce_root(local_gram)
    root_total, panels = lax.optimization_barrier((root_total, panels))
    root_adjoint = adjoint_block(root_block - root_total, root_cot)
    rows_dev, blocks_row, height, breadth = panels.shape
    item_count = rows_dev * blocks_row
    capacity = max(2, 2 * item_count // devices_sub)
    group_id = lax.axis_index("leaf")
    owners = lax.dynamic_index_in_dim(owner_map, group_id, 0, keepdims=False)
    target = jnp.take(owners, structure.reshape(item_count))
    onehot = (target[:, None] == jnp.arange(devices_sub, dtype=jnp.int32)[None, :]).astype(
        jnp.int32
    )
    earlier = jnp.cumsum(onehot, axis=0) - onehot
    slot_id = jnp.sum(earlier * onehot, axis=1)
    position = target * capacity + slot_id
    flat_panels = panels.reshape(item_count, height, breadth)
    outgoing = (
        jnp.zeros((devices_sub * capacity, height, breadth), jnp.bfloat16)
        .at[position]
        .set(flat_panels)
    )
    incoming = lax.all_to_all(outgoing, "sub", split_axis=0, concat_axis=0, tiled=True)
    root_adjoint, incoming = lax.optimization_barrier((root_adjoint, incoming))
    gram_sum = jnp.einsum("nbw,ncw->bc", incoming, incoming, preferred_element_type=jnp.float32)
    upper_adjoint = adjoint_block(upper_block[0] - gram_sum, upper_cot[0])
    every_adjoint = unpack_symmetric(gather_sub(pack_symmetric(upper_adjoint)))
    chosen = jnp.take(every_adjoint, target, axis=0)
    panel_adjoint = (
        -2.0
        * jnp.einsum("nbc,ncw->nbw", chosen, flat_panels, preferred_element_type=jnp.float32)
    ).astype(jnp.bfloat16)
    panel_adjoint = panel_adjoint.reshape(rows_dev, blocks_row, height, breadth)
    panel_grad = jnp.einsum(
        "srbw,swv->srbv", panel_adjoint, low_inverse, preferred_element_type=jnp.float32
    ).astype(jnp.bfloat16)
    root_panel_adjoint = (
        -2.0
        * jnp.einsum("bc,scw->sbw", root_adjoint, root_panels, preferred_element_type=jnp.float32)
    ).astype(jnp.bfloat16)
    root_grad = jnp.einsum(
        "sbw,swv->sbv", root_panel_adjoint, low_inverse, preferred_element_type=jnp.float32
    ).astype(jnp.bfloat16)
    return (panel_grad, root_grad)


def solution(mesh):
    in_specs = (
        P(("leaf", "sub"), None, None, None),
        P(("leaf", "sub"), None, None),
        P(("leaf", "sub"), None, None),
        P(("leaf", "sub"), None),
        P(),
        P(("leaf", "sub"), None, None),
        P(("leaf", "sub"), None, None),
        P(),
        P(),
    )
    out_specs = (P(("leaf", "sub"), None, None, None), P(("leaf", "sub"), None, None))
    return jax.shard_map(body, mesh=mesh, in_specs=in_specs, out_specs=out_specs, check_vma=False)
```

```python
import jax
import jax.numpy as jnp
from jax import lax
from jax.experimental import pallas as pl
from jax.experimental.pallas import tpu as pltpu
from jax.sharding import PartitionSpec as P

MESH = pl.DeviceIdType.MESH

def _allreduce_kernel(
    x_ref, o_ref, full, a1, a2, a3, rs1, rs2, rs3, rs4, ssem, rsem1, rsem2, rsem3, rsem4, gsem3, gsem2, gsem1
):
    leaf = lax.axis_index("leaf")
    sub = lax.axis_index("sub")
    c = leaf % 2
    y = leaf // 2
    x = sub // 8
    z = sub % 8

    def core_peer():
        return (leaf + 1 - 2 * c, sub)

    def x_peer(xx):
        return (leaf, xx * 8 + z)

    def y_peer(yy):
        return (yy * 2 + c, sub)

    def z_peer(zz):
        return (leaf, x * 8 + zz)

    peers = [core_peer()]
    peers += [x_peer((x + d) % 4) for d in range(1, 4)]
    peers += [y_peer((y + d) % 8) for d in range(1, 8)]
    peers += [z_peer((z + d) % 8) for d in range(1, 8)]
    barrier = pltpu.get_barrier_semaphore()
    for p in peers:
        pl.semaphore_signal(barrier, inc=1, device_id=p, device_id_type=MESH)
    pl.semaphore_wait(barrier, len(peers))

    sends = []

    def send(src, dst, rsem, dev):
        cp = pltpu.make_async_remote_copy(
            src_ref=src, dst_ref=dst, send_sem=ssem.at[len(sends)], recv_sem=rsem, device_id=dev, device_id_type=MESH
        )
        cp.start()
        sends.append(cp)

    def recv_wait(dst, rsem, dev):
        pltpu.make_async_remote_copy(
            src_ref=dst, dst_ref=dst, send_sem=ssem.at[0], recv_sem=rsem, device_id=dev, device_id_type=MESH
        ).wait_recv()

    mine1 = pl.multiple_of(c * 256, 256)
    send(x_ref.at[pl.ds(pl.multiple_of((1 - c) * 256, 256), 256)], rs1, rsem1.at[0], core_peer())
    recv_wait(rs1, rsem1.at[0], core_peer())
    a1[...] = x_ref[pl.ds(mine1, 256), :] + rs1[...]

    for d in range(1, 4):
        xx = (x + d) % 4
        send(a1.at[pl.ds(pl.multiple_of(xx * 64, 64), 64)], rs2.at[x], rsem2.at[x], x_peer(xx))
    for d in range(1, 4):
        xx = (x + d) % 4
        recv_wait(rs2.at[xx], rsem2.at[xx], x_peer(xx))
    rs2[x] = a1[pl.ds(pl.multiple_of(x * 64, 64), 64), :]
    a2[...] = rs2[0] + rs2[1] + rs2[2] + rs2[3]

    for d in range(1, 8):
        yy = (y + d) % 8
        send(a2.at[pl.ds(pl.multiple_of(yy * 8, 8), 8)], rs3.at[y], rsem3.at[y], y_peer(yy))
    for d in range(1, 8):
        yy = (y + d) % 8
        recv_wait(rs3.at[yy], rsem3.at[yy], y_peer(yy))
    rs3[y] = a2[pl.ds(pl.multiple_of(y * 8, 8), 8), :]
    total3 = rs3[0]
    for i in range(1, 8):
        total3 = total3 + rs3[i]
    a3[...] = total3

    for d in range(1, 8):
        zz = (z + d) % 8
        send(a3, rs4.at[z], rsem4.at[z], z_peer(zz))
    for d in range(1, 8):
        zz = (z + d) % 8
        recv_wait(rs4.at[zz], rsem4.at[zz], z_peer(zz))
    rs4[z] = a3[...]
    total4 = rs4[0]
    for i in range(1, 8):
        total4 = total4 + rs4[i]
    base2 = c * 256 + x * 64
    full[pl.ds(pl.multiple_of(base2 + y * 8, 8), 8), :] = total4

    for d in range(1, 8):
        yy = (y + d) % 8
        blk = full.at[pl.ds(pl.multiple_of(base2 + y * 8, 8), 8)]
        send(blk, blk, gsem3.at[y], y_peer(yy))
    for d in range(1, 8):
        yy = (y + d) % 8
        recv_wait(full.at[pl.ds(pl.multiple_of(base2 + yy * 8, 8), 8)], gsem3.at[yy], y_peer(yy))
    for d in range(1, 4):
        xx = (x + d) % 4
        blk = full.at[pl.ds(pl.multiple_of(base2, 64), 64)]
        send(blk, blk, gsem2.at[x], x_peer(xx))
    for d in range(1, 4):
        xx = (x + d) % 4
        recv_wait(full.at[pl.ds(pl.multiple_of(c * 256 + xx * 64, 64), 64)], gsem2.at[xx], x_peer(xx))
    blk = full.at[pl.ds(mine1, 256)]
    send(blk, blk, gsem1.at[0], core_peer())
    recv_wait(full.at[pl.ds(pl.multiple_of((1 - c) * 256, 256), 256)], gsem1.at[0], core_peer())
    for cp in sends:
        cp.wait_send()
    o_ref[...] = full[...]


def allreduce_root(gram):
    flat = gram.reshape(512, 128)
    n_sends = 1 + 3 + 7 + 7 + 7 + 3 + 1
    out = pl.pallas_call(
        _allreduce_kernel,
        out_shape=jax.ShapeDtypeStruct((512, 128), jnp.float32),
        in_specs=[pl.BlockSpec(memory_space=pltpu.VMEM)],
        out_specs=pl.BlockSpec(memory_space=pltpu.VMEM),
        scratch_shapes=[
            pltpu.VMEM((512, 128), jnp.float32),
            pltpu.VMEM((256, 128), jnp.float32),
            pltpu.VMEM((64, 128), jnp.float32),
            pltpu.VMEM((8, 128), jnp.float32),
            pltpu.VMEM((256, 128), jnp.float32),
            pltpu.VMEM((4, 64, 128), jnp.float32),
            pltpu.VMEM((8, 8, 128), jnp.float32),
            pltpu.VMEM((8, 8, 128), jnp.float32),
            pltpu.SemaphoreType.DMA((n_sends,)),
            pltpu.SemaphoreType.DMA((1,)),
            pltpu.SemaphoreType.DMA((4,)),
            pltpu.SemaphoreType.DMA((8,)),
            pltpu.SemaphoreType.DMA((8,)),
            pltpu.SemaphoreType.DMA((8,)),
            pltpu.SemaphoreType.DMA((4,)),
            pltpu.SemaphoreType.DMA((1,)),
        ],
        compiler_params=pltpu.CompilerParams(collective_id=0, has_side_effects=True),
        cost_estimate=pl.CostEstimate(flops=4 * 65536, bytes_accessed=3 * 262144, transcendentals=0),
    )(flat)
    return out.reshape(256, 256)


def _gather_kernel(a_ref, o_ref, gathered, ssem, rsz, rsx, lsem):
    leaf = lax.axis_index("leaf")
    sub = lax.axis_index("sub")
    x = sub // 8
    z = sub % 8
    right = ((x + 1) % 4) * 8 + z
    left = ((x + 3) % 4) * 8 + z
    peers = [(leaf, x * 8 + (z + d) % 8) for d in range(1, 8)]
    peers += [(leaf, right), (leaf, left)]
    barrier = pltpu.get_barrier_semaphore()
    for p in peers:
        pl.semaphore_signal(barrier, inc=1, device_id=p, device_id_type=MESH)
    pl.semaphore_wait(barrier, len(peers))

    sends = []

    def send(src, dst, rsem, dev):
        cp = pltpu.make_async_remote_copy(
            src_ref=src, dst_ref=dst, send_sem=ssem.at[len(sends)], recv_sem=rsem, device_id=dev, device_id_type=MESH
        )
        cp.start()
        sends.append(cp)

    def recv_wait(dst, rsem, dev):
        pltpu.make_async_remote_copy(
            src_ref=dst, dst_ref=dst, send_sem=ssem.at[0], recv_sem=rsem, device_id=dev, device_id_type=MESH
        ).wait_recv()

    for d in range(1, 8):
        zz = (z + d) % 8
        send(a_ref, gathered.at[x * 8 + z], rsz.at[z], (leaf, x * 8 + zz))
    own = pltpu.make_async_copy(a_ref, gathered.at[x * 8 + z], lsem.at[0])
    own.start()
    for d in range(1, 8):
        zz = (z + d) % 8
        recv_wait(gathered.at[x * 8 + zz], rsz.at[zz], (leaf, x * 8 + zz))
    own.wait()

    def column(xx, first, count):
        return gathered.at[pl.ds(pl.multiple_of(xx * 8 + first, 4), count)]

    x_left = (x + 3) % 4
    x_right = (x + 1) % 4
    x_far = (x + 2) % 4
    send(column(x, 0, 8), column(x, 0, 8), rsx.at[0], (leaf, right))
    send(column(x, 0, 8), column(x, 0, 8), rsx.at[1], (leaf, left))
    recv_wait(column(x_left, 0, 8), rsx.at[0], (leaf, left))
    send(column(x_left, 0, 4), column(x_left, 0, 4), rsx.at[2], (leaf, right))
    recv_wait(column(x_right, 0, 8), rsx.at[1], (leaf, right))
    send(column(x_right, 4, 4), column(x_right, 4, 4), rsx.at[3], (leaf, left))
    recv_wait(column(x_far, 0, 4), rsx.at[2], (leaf, left))
    recv_wait(column(x_far, 4, 4), rsx.at[3], (leaf, right))
    for cp in sends:
        cp.wait_send()
    o_ref[...] = gathered[...]


def gather_sub(block):
    rows = block.shape[0]
    return pl.pallas_call(
        _gather_kernel,
        out_shape=jax.ShapeDtypeStruct((32, rows, 128), block.dtype),
        in_specs=[pl.BlockSpec(memory_space=pltpu.VMEM)],
        out_specs=pl.BlockSpec(memory_space=pltpu.VMEM),
        scratch_shapes=[
            pltpu.VMEM((32, rows, 128), block.dtype),
            pltpu.SemaphoreType.DMA((11,)),
            pltpu.SemaphoreType.DMA((8,)),
            pltpu.SemaphoreType.DMA((4,)),
            pltpu.SemaphoreType.DMA((1,)),
        ],
        compiler_params=pltpu.CompilerParams(collective_id=1, has_side_effects=True),
        cost_estimate=pl.CostEstimate(flops=0, bytes_accessed=2 * 32 * rows * 128 * 2, transcendentals=0),
    )(block)


def pack_symmetric(a):
    h = a.shape[0] // 2
    row = lax.broadcasted_iota(jnp.int32, (h, h), 0)
    col = lax.broadcasted_iota(jnp.int32, (h, h), 1)
    folded = jnp.where(col <= row, a[:h, :h], a[h:, h:])
    diag = jnp.where(row == col, a[h:, h:], jnp.zeros_like(a[h:, h:]))
    diag_row = jnp.sum(diag.astype(jnp.float32), axis=0, keepdims=True).astype(a.dtype)
    pad = jnp.zeros((15, h), a.dtype)
    return jnp.concatenate([folded, a[h:, :h], diag_row, pad], axis=0)


def unpack_symmetric(packed):
    h = 128
    folded = packed[:, :h, :]
    lower = packed[:, h:2 * h, :]
    diag_row = packed[:, 2 * h:2 * h + 1, :]
    row = lax.broadcasted_iota(jnp.int32, (1, h, h), 1)
    col = lax.broadcasted_iota(jnp.int32, (1, h, h), 2)
    folded_t = jnp.swapaxes(folded, 1, 2)
    top_left = jnp.where(col <= row, folded, folded_t)
    bottom_right = jnp.where(col > row, folded, jnp.where(col < row, folded_t, diag_row))
    top = jnp.concatenate([top_left, jnp.swapaxes(lower, 1, 2)], axis=2)
    bottom = jnp.concatenate([lower, bottom_right], axis=2)
    return jnp.concatenate([top, bottom], axis=1)


def _dot(a, b):
    return jnp.dot(a, b, precision=lax.Precision.HIGHEST)


def factor_and_inverse(schur):
    h = schur.shape[0] // 2
    identity = jnp.eye(h, dtype=schur.dtype)
    f11 = jnp.linalg.cholesky(schur[:h, :h])
    i11 = jax.scipy.linalg.solve_triangular(f11, identity, lower=True)
    f21 = _dot(schur[h:, :h], i11.T)
    f22 = jnp.linalg.cholesky(schur[h:, h:] - _dot(f21, f21.T))
    i22 = jax.scipy.linalg.solve_triangular(f22, identity, lower=True)
    i21 = -_dot(_dot(i22, f21), i11)
    zero = jnp.zeros((h, h), schur.dtype)
    factor = jnp.concatenate([jnp.concatenate([f11, zero], 1), jnp.concatenate([f21, f22], 1)], 0)
    inverse = jnp.concatenate([jnp.concatenate([i11, zero], 1), jnp.concatenate([i21, i22], 1)], 0)
    return factor, inverse


def adjoint_block(schur, cotangent):
    factor, inverse = factor_and_inverse(schur)
    product = jnp.dot(factor.T, cotangent, precision=lax.Precision.HIGHEST)
    lowered = jnp.tril(product) - 0.5 * jnp.diag(jnp.diag(product))
    adjoint_full = jnp.dot(
        jnp.dot(inverse.T, lowered, precision=lax.Precision.HIGHEST),
        inverse,
        precision=lax.Precision.HIGHEST,
    )
    return (0.5 * (adjoint_full + adjoint_full.T)).astype(jnp.bfloat16)


def body(
    panels,
    root_panels,
    low_inverse,
    structure,
    owner_map,
    upper_block,
    upper_cot,
    root_block,
    root_cot,
):
    devices_sub = lax.axis_size("sub")
    local_gram = jnp.einsum(
        "sbw,scw->bc", root_panels, root_panels, preferred_element_type=jnp.float32
    )
    root_total = allreduce_root(local_gram)
    root_total, panels = lax.optimization_barrier((root_total, panels))
    root_adjoint = adjoint_block(root_block - root_total, root_cot)
    rows_dev, blocks_row, height, breadth = panels.shape
    item_count = rows_dev * blocks_row
    capacity = max(2, 2 * item_count // devices_sub)
    group_id = lax.axis_index("leaf")
    owners = lax.dynamic_index_in_dim(owner_map, group_id, 0, keepdims=False)
    target = jnp.take(owners, structure.reshape(item_count))
    onehot = (target[:, None] == jnp.arange(devices_sub, dtype=jnp.int32)[None, :]).astype(
        jnp.int32
    )
    earlier = jnp.cumsum(onehot, axis=0) - onehot
    slot_id = jnp.sum(earlier * onehot, axis=1)
    position = target * capacity + slot_id
    flat_panels = panels.reshape(item_count, height, breadth)
    outgoing = (
        jnp.zeros((devices_sub * capacity, height, breadth), jnp.bfloat16)
        .at[position]
        .set(flat_panels)
    )
    incoming = lax.all_to_all(outgoing, "sub", split_axis=0, concat_axis=0, tiled=True)
    root_adjoint, incoming = lax.optimization_barrier((root_adjoint, incoming))
    gram_sum = jnp.einsum("nbw,ncw->bc", incoming, incoming, preferred_element_type=jnp.float32)
    upper_adjoint = adjoint_block(upper_block[0] - gram_sum, upper_cot[0])
    every_adjoint = unpack_symmetric(gather_sub(pack_symmetric(upper_adjoint)))
    chosen = jnp.take(every_adjoint, target, axis=0)
    panel_adjoint = (
        -2.0
        * jnp.einsum("nbc,ncw->nbw", chosen, flat_panels, preferred_element_type=jnp.float32)
    ).astype(jnp.bfloat16)
    panel_adjoint = panel_adjoint.reshape(rows_dev, blocks_row, height, breadth)
    panel_grad = jnp.einsum(
        "srbw,swv->srbv", panel_adjoint, low_inverse, preferred_element_type=jnp.float32
    ).astype(jnp.bfloat16)
    root_panel_adjoint = (
        -2.0
        * jnp.einsum("bc,scw->sbw", root_adjoint, root_panels, preferred_element_type=jnp.float32)
    ).astype(jnp.bfloat16)
    root_grad = jnp.einsum(
        "sbw,swv->sbv", root_panel_adjoint, low_inverse, preferred_element_type=jnp.float32
    ).astype(jnp.bfloat16)
    return (panel_grad, root_grad)


def solution(mesh):
    in_specs = (
        P(("leaf", "sub"), None, None, None),
        P(("leaf", "sub"), None, None),
        P(("leaf", "sub"), None, None),
        P(("leaf", "sub"), None),
        P(),
        P(("leaf", "sub"), None, None),
        P(("leaf", "sub"), None, None),
        P(),
        P(),
    )
    out_specs = (P(("leaf", "sub"), None, None, None), P(("leaf", "sub"), None, None))
    return jax.shard_map(body, mesh=mesh, in_specs=in_specs, out_specs=out_specs, check_vma=False)
```

```python
import jax
import jax.numpy as jnp
from jax import lax
from jax.experimental import pallas as pl
from jax.experimental.pallas import tpu as pltpu
from jax.sharding import PartitionSpec as P

MESH = pl.DeviceIdType.MESH

def _allreduce_kernel(
    x_ref, o_ref, full, a1, a2, a3, rs1, rs2, rs3, rs4, ssem, rsem1, rsem2, rsem3, rsem4, gsem3, gsem2, gsem1
):
    leaf = lax.axis_index("leaf")
    sub = lax.axis_index("sub")
    c = leaf % 2
    y = leaf // 2
    x = sub // 8
    z = sub % 8

    def core_peer():
        return (leaf + 1 - 2 * c, sub)

    def x_peer(xx):
        return (leaf, xx * 8 + z)

    def y_peer(yy):
        return (yy * 2 + c, sub)

    def z_peer(zz):
        return (leaf, x * 8 + zz)

    peers = [core_peer()]
    peers += [x_peer((x + d) % 4) for d in range(1, 4)]
    peers += [y_peer((y + d) % 8) for d in range(1, 8)]
    peers += [z_peer((z + d) % 8) for d in range(1, 8)]
    barrier = pltpu.get_barrier_semaphore()
    for p in peers:
        pl.semaphore_signal(barrier, inc=1, device_id=p, device_id_type=MESH)
    pl.semaphore_wait(barrier, len(peers))

    sends = []

    def send(src, dst, rsem, dev):
        cp = pltpu.make_async_remote_copy(
            src_ref=src, dst_ref=dst, send_sem=ssem.at[len(sends)], recv_sem=rsem, device_id=dev, device_id_type=MESH
        )
        cp.start()
        sends.append(cp)

    def recv_wait(dst, rsem, dev):
        pltpu.make_async_remote_copy(
            src_ref=dst, dst_ref=dst, send_sem=ssem.at[0], recv_sem=rsem, device_id=dev, device_id_type=MESH
        ).wait_recv()

    mine1 = pl.multiple_of(c * 256, 256)
    send(x_ref.at[pl.ds(pl.multiple_of((1 - c) * 256, 256), 256)], rs1, rsem1.at[0], core_peer())
    recv_wait(rs1, rsem1.at[0], core_peer())
    a1[...] = x_ref[pl.ds(mine1, 256), :] + rs1[...]

    for d in range(1, 4):
        xx = (x + d) % 4
        send(a1.at[pl.ds(pl.multiple_of(xx * 64, 64), 64)], rs2.at[x], rsem2.at[x], x_peer(xx))
    for d in range(1, 4):
        xx = (x + d) % 4
        recv_wait(rs2.at[xx], rsem2.at[xx], x_peer(xx))
    rs2[x] = a1[pl.ds(pl.multiple_of(x * 64, 64), 64), :]
    a2[...] = rs2[0] + rs2[1] + rs2[2] + rs2[3]

    for d in range(1, 8):
        yy = (y + d) % 8
        send(a2.at[pl.ds(pl.multiple_of(yy * 8, 8), 8)], rs3.at[y], rsem3.at[y], y_peer(yy))
    for d in range(1, 8):
        yy = (y + d) % 8
        recv_wait(rs3.at[yy], rsem3.at[yy], y_peer(yy))
    rs3[y] = a2[pl.ds(pl.multiple_of(y * 8, 8), 8), :]
    total3 = rs3[0]
    for i in range(1, 8):
        total3 = total3 + rs3[i]
    a3[...] = total3

    for d in range(1, 8):
        zz = (z + d) % 8
        send(a3, rs4.at[z], rsem4.at[z], z_peer(zz))
    for d in range(1, 8):
        zz = (z + d) % 8
        recv_wait(rs4.at[zz], rsem4.at[zz], z_peer(zz))
    rs4[z] = a3[...]
    total4 = rs4[0]
    for i in range(1, 8):
        total4 = total4 + rs4[i]
    base2 = c * 256 + x * 64
    full[pl.ds(pl.multiple_of(base2 + y * 8, 8), 8), :] = total4

    for d in range(1, 8):
        yy = (y + d) % 8
        blk = full.at[pl.ds(pl.multiple_of(base2 + y * 8, 8), 8)]
        send(blk, blk, gsem3.at[y], y_peer(yy))
    for d in range(1, 8):
        yy = (y + d) % 8
        recv_wait(full.at[pl.ds(pl.multiple_of(base2 + yy * 8, 8), 8)], gsem3.at[yy], y_peer(yy))
    for d in range(1, 4):
        xx = (x + d) % 4
        blk = full.at[pl.ds(pl.multiple_of(base2, 64), 64)]
        send(blk, blk, gsem2.at[x], x_peer(xx))
    for d in range(1, 4):
        xx = (x + d) % 4
        recv_wait(full.at[pl.ds(pl.multiple_of(c * 256 + xx * 64, 64), 64)], gsem2.at[xx], x_peer(xx))
    blk = full.at[pl.ds(mine1, 256)]
    send(blk, blk, gsem1.at[0], core_peer())
    recv_wait(full.at[pl.ds(pl.multiple_of((1 - c) * 256, 256), 256)], gsem1.at[0], core_peer())
    for cp in sends:
        cp.wait_send()
    o_ref[...] = full[...]


def allreduce_root(gram):
    flat = gram.reshape(512, 128)
    n_sends = 1 + 3 + 7 + 7 + 7 + 3 + 1
    out = pl.pallas_call(
        _allreduce_kernel,
        out_shape=jax.ShapeDtypeStruct((512, 128), jnp.float32),
        in_specs=[pl.BlockSpec(memory_space=pltpu.VMEM)],
        out_specs=pl.BlockSpec(memory_space=pltpu.VMEM),
        scratch_shapes=[
            pltpu.VMEM((512, 128), jnp.float32),
            pltpu.VMEM((256, 128), jnp.float32),
            pltpu.VMEM((64, 128), jnp.float32),
            pltpu.VMEM((8, 128), jnp.float32),
            pltpu.VMEM((256, 128), jnp.float32),
            pltpu.VMEM((4, 64, 128), jnp.float32),
            pltpu.VMEM((8, 8, 128), jnp.float32),
            pltpu.VMEM((8, 8, 128), jnp.float32),
            pltpu.SemaphoreType.DMA((n_sends,)),
            pltpu.SemaphoreType.DMA((1,)),
            pltpu.SemaphoreType.DMA((4,)),
            pltpu.SemaphoreType.DMA((8,)),
            pltpu.SemaphoreType.DMA((8,)),
            pltpu.SemaphoreType.DMA((8,)),
            pltpu.SemaphoreType.DMA((4,)),
            pltpu.SemaphoreType.DMA((1,)),
        ],
        compiler_params=pltpu.CompilerParams(collective_id=0, has_side_effects=True),
        cost_estimate=pl.CostEstimate(flops=4 * 65536, bytes_accessed=3 * 262144, transcendentals=0),
    )(flat)
    return out.reshape(256, 256)


def _gather_kernel(a_ref, o_ref, gathered, ssem, rsz, rsx, lsem):
    leaf = lax.axis_index("leaf")
    sub = lax.axis_index("sub")
    x = sub // 8
    z = sub % 8
    right = ((x + 1) % 4) * 8 + z
    left = ((x + 3) % 4) * 8 + z
    peers = [(leaf, x * 8 + (z + d) % 8) for d in range(1, 8)]
    peers += [(leaf, right), (leaf, left)]
    barrier = pltpu.get_barrier_semaphore()
    for p in peers:
        pl.semaphore_signal(barrier, inc=1, device_id=p, device_id_type=MESH)
    pl.semaphore_wait(barrier, len(peers))

    sends = []

    def send(src, dst, rsem, dev):
        cp = pltpu.make_async_remote_copy(
            src_ref=src, dst_ref=dst, send_sem=ssem.at[len(sends)], recv_sem=rsem, device_id=dev, device_id_type=MESH
        )
        cp.start()
        sends.append(cp)

    def recv_wait(dst, rsem, dev):
        pltpu.make_async_remote_copy(
            src_ref=dst, dst_ref=dst, send_sem=ssem.at[0], recv_sem=rsem, device_id=dev, device_id_type=MESH
        ).wait_recv()

    for d in range(1, 8):
        zz = (z + d) % 8
        send(a_ref, gathered.at[x * 8 + z], rsz.at[z], (leaf, x * 8 + zz))
    own = pltpu.make_async_copy(a_ref, gathered.at[x * 8 + z], lsem.at[0])
    own.start()
    for d in range(1, 8):
        zz = (z + d) % 8
        recv_wait(gathered.at[x * 8 + zz], rsz.at[zz], (leaf, x * 8 + zz))
    own.wait()

    def column(xx, first, count):
        return gathered.at[pl.ds(pl.multiple_of(xx * 8 + first, 4), count)]

    x_left = (x + 3) % 4
    x_right = (x + 1) % 4
    x_far = (x + 2) % 4
    send(column(x, 0, 8), column(x, 0, 8), rsx.at[0], (leaf, right))
    send(column(x, 0, 8), column(x, 0, 8), rsx.at[1], (leaf, left))
    recv_wait(column(x_left, 0, 8), rsx.at[0], (leaf, left))
    send(column(x_left, 0, 4), column(x_left, 0, 4), rsx.at[2], (leaf, right))
    recv_wait(column(x_right, 0, 8), rsx.at[1], (leaf, right))
    send(column(x_right, 4, 4), column(x_right, 4, 4), rsx.at[3], (leaf, left))
    recv_wait(column(x_far, 0, 4), rsx.at[2], (leaf, left))
    recv_wait(column(x_far, 4, 4), rsx.at[3], (leaf, right))
    for cp in sends:
        cp.wait_send()
    o_ref[...] = gathered[...]


def gather_sub(block):
    rows = block.shape[0]
    return pl.pallas_call(
        _gather_kernel,
        out_shape=jax.ShapeDtypeStruct((32, rows, 128), block.dtype),
        in_specs=[pl.BlockSpec(memory_space=pltpu.VMEM)],
        out_specs=pl.BlockSpec(memory_space=pltpu.VMEM),
        scratch_shapes=[
            pltpu.VMEM((32, rows, 128), block.dtype),
            pltpu.SemaphoreType.DMA((11,)),
            pltpu.SemaphoreType.DMA((8,)),
            pltpu.SemaphoreType.DMA((4,)),
            pltpu.SemaphoreType.DMA((1,)),
        ],
        compiler_params=pltpu.CompilerParams(collective_id=1, has_side_effects=True),
        cost_estimate=pl.CostEstimate(flops=0, bytes_accessed=2 * 32 * rows * 128 * 2, transcendentals=0),
    )(block)


def pack_symmetric(a):
    h = a.shape[0] // 2
    row = lax.broadcasted_iota(jnp.int32, (h, h), 0)
    col = lax.broadcasted_iota(jnp.int32, (h, h), 1)
    folded = jnp.where(col <= row, a[:h, :h], a[h:, h:])
    diag = jnp.where(row == col, a[h:, h:], jnp.zeros_like(a[h:, h:]))
    diag_row = jnp.sum(diag.astype(jnp.float32), axis=0, keepdims=True).astype(a.dtype)
    pad = jnp.zeros((15, h), a.dtype)
    return jnp.concatenate([folded, a[h:, :h], diag_row, pad], axis=0)


def unpack_symmetric(packed):
    h = 128
    folded = packed[:, :h, :]
    lower = packed[:, h:2 * h, :]
    diag_row = packed[:, 2 * h:2 * h + 1, :]
    row = lax.broadcasted_iota(jnp.int32, (1, h, h), 1)
    col = lax.broadcasted_iota(jnp.int32, (1, h, h), 2)
    folded_t = jnp.swapaxes(folded, 1, 2)
    top_left = jnp.where(col <= row, folded, folded_t)
    bottom_right = jnp.where(col > row, folded, jnp.where(col < row, folded_t, diag_row))
    top = jnp.concatenate([top_left, jnp.swapaxes(lower, 1, 2)], axis=2)
    bottom = jnp.concatenate([lower, bottom_right], axis=2)
    return jnp.concatenate([top, bottom], axis=1)


def _dot(a, b):
    return jnp.dot(a, b, precision=lax.Precision.HIGHEST)


def factor_and_inverse(schur):
    h = schur.shape[0] // 2
    identity = jnp.eye(h, dtype=schur.dtype)
    f11 = jnp.linalg.cholesky(schur[:h, :h])
    i11 = jax.scipy.linalg.solve_triangular(f11, identity, lower=True)
    f21 = _dot(schur[h:, :h], i11.T)
    f22 = jnp.linalg.cholesky(schur[h:, h:] - _dot(f21, f21.T))
    i22 = jax.scipy.linalg.solve_triangular(f22, identity, lower=True)
    i21 = -_dot(_dot(i22, f21), i11)
    zero = jnp.zeros((h, h), schur.dtype)
    factor = jnp.concatenate([jnp.concatenate([f11, zero], 1), jnp.concatenate([f21, f22], 1)], 0)
    inverse = jnp.concatenate([jnp.concatenate([i11, zero], 1), jnp.concatenate([i21, i22], 1)], 0)
    return factor, inverse


def packed_times(packed, panels):
    h = 128
    folded = packed[:, :h, :]
    lower = packed[:, h:2 * h, :]
    diag_col = jnp.swapaxes(packed[:, 2 * h:2 * h + 1, :], 1, 2).astype(jnp.float32)
    row = lax.broadcasted_iota(jnp.int32, (1, h, h), 1)
    col = lax.broadcasted_iota(jnp.int32, (1, h, h), 2)
    zero = jnp.zeros_like(folded)
    low_incl = jnp.where(col <= row, folded, zero)
    low_strict = jnp.where(col < row, folded, zero)
    up_strict = jnp.where(col > row, folded, zero)
    top_in, bottom_in = panels[:, :h, :], panels[:, h:, :]

    def mul(a, b):
        return jnp.einsum("nbk,nkw->nbw", a, b, preferred_element_type=jnp.float32)

    def mul_t(a, b):
        return jnp.einsum("nkb,nkw->nbw", a, b, preferred_element_type=jnp.float32)

    top = mul(low_incl, top_in) + mul_t(low_strict, top_in) + mul_t(lower, bottom_in)
    bottom = (
        mul(lower, top_in)
        + mul(up_strict, bottom_in)
        + mul_t(up_strict, bottom_in)
        + diag_col * bottom_in.astype(jnp.float32)
    )
    return jnp.concatenate([top, bottom], axis=1)


def adjoint_block(schur, cotangent):
    factor, inverse = factor_and_inverse(schur)
    product = jnp.dot(factor.T, cotangent, precision=lax.Precision.HIGHEST)
    lowered = jnp.tril(product) - 0.5 * jnp.diag(jnp.diag(product))
    adjoint_full = jnp.dot(
        jnp.dot(inverse.T, lowered, precision=lax.Precision.HIGHEST),
        inverse,
        precision=lax.Precision.HIGHEST,
    )
    return (0.5 * (adjoint_full + adjoint_full.T)).astype(jnp.bfloat16)


def body(
    panels,
    root_panels,
    low_inverse,
    structure,
    owner_map,
    upper_block,
    upper_cot,
    root_block,
    root_cot,
):
    devices_sub = lax.axis_size("sub")
    local_gram = jnp.einsum(
        "sbw,scw->bc", root_panels, root_panels, preferred_element_type=jnp.float32
    )
    root_total = allreduce_root(local_gram)
    root_total, panels = lax.optimization_barrier((root_total, panels))
    root_adjoint = adjoint_block(root_block - root_total, root_cot)
    rows_dev, blocks_row, height, breadth = panels.shape
    item_count = rows_dev * blocks_row
    capacity = max(2, 2 * item_count // devices_sub)
    group_id = lax.axis_index("leaf")
    owners = lax.dynamic_index_in_dim(owner_map, group_id, 0, keepdims=False)
    target = jnp.take(owners, structure.reshape(item_count))
    onehot = (target[:, None] == jnp.arange(devices_sub, dtype=jnp.int32)[None, :]).astype(
        jnp.int32
    )
    earlier = jnp.cumsum(onehot, axis=0) - onehot
    slot_id = jnp.sum(earlier * onehot, axis=1)
    position = target * capacity + slot_id
    flat_panels = panels.reshape(item_count, height, breadth)
    outgoing = (
        jnp.zeros((devices_sub * capacity, height, breadth), jnp.bfloat16)
        .at[position]
        .set(flat_panels)
    )
    incoming = lax.all_to_all(outgoing, "sub", split_axis=0, concat_axis=0, tiled=True)
    root_adjoint, incoming = lax.optimization_barrier((root_adjoint, incoming))
    gram_sum = jnp.einsum("nbw,ncw->bc", incoming, incoming, preferred_element_type=jnp.float32)
    upper_adjoint = adjoint_block(upper_block[0] - gram_sum, upper_cot[0])
    chosen = jnp.take(gather_sub(pack_symmetric(upper_adjoint)), target, axis=0)
    panel_adjoint = (-2.0 * packed_times(chosen, flat_panels)).astype(jnp.bfloat16)
    panel_adjoint = panel_adjoint.reshape(rows_dev, blocks_row, height, breadth)
    panel_grad = jnp.einsum(
        "srbw,swv->srbv", panel_adjoint, low_inverse, preferred_element_type=jnp.float32
    ).astype(jnp.bfloat16)
    root_panel_adjoint = (
        -2.0
        * jnp.einsum("bc,scw->sbw", root_adjoint, root_panels, preferred_element_type=jnp.float32)
    ).astype(jnp.bfloat16)
    root_grad = jnp.einsum(
        "sbw,swv->sbv", root_panel_adjoint, low_inverse, preferred_element_type=jnp.float32
    ).astype(jnp.bfloat16)
    return (panel_grad, root_grad)


def solution(mesh):
    in_specs = (
        P(("leaf", "sub"), None, None, None),
        P(("leaf", "sub"), None, None),
        P(("leaf", "sub"), None, None),
        P(("leaf", "sub"), None),
        P(),
        P(("leaf", "sub"), None, None),
        P(("leaf", "sub"), None, None),
        P(),
        P(),
    )
    out_specs = (P(("leaf", "sub"), None, None, None), P(("leaf", "sub"), None, None))
    return jax.shard_map(body, mesh=mesh, in_specs=in_specs, out_specs=out_specs, check_vma=False)
```

```python
import jax
import jax.numpy as jnp
from jax import lax
from jax.experimental import pallas as pl
from jax.experimental.pallas import tpu as pltpu
from jax.sharding import PartitionSpec as P

MESH = pl.DeviceIdType.MESH

def _allreduce_kernel(
    x_ref, o_ref, full, a1, a2, a3, rs1, rs2, rs3, rs4, ssem, rsem1, rsem2, rsem3, rsem4, gsem3, gsem2, gsem1
):
    leaf = lax.axis_index("leaf")
    sub = lax.axis_index("sub")
    c = leaf % 2
    y = leaf // 2
    x = sub // 8
    z = sub % 8

    def core_peer():
        return (leaf + 1 - 2 * c, sub)

    def x_peer(xx):
        return (leaf, xx * 8 + z)

    def y_peer(yy):
        return (yy * 2 + c, sub)

    def z_peer(zz):
        return (leaf, x * 8 + zz)

    peers = [core_peer()]
    peers += [x_peer((x + d) % 4) for d in range(1, 4)]
    peers += [y_peer((y + d) % 8) for d in range(1, 8)]
    peers += [z_peer((z + d) % 8) for d in range(1, 8)]
    barrier = pltpu.get_barrier_semaphore()
    for p in peers:
        pl.semaphore_signal(barrier, inc=1, device_id=p, device_id_type=MESH)
    pl.semaphore_wait(barrier, len(peers))

    sends = []

    def send(src, dst, rsem, dev):
        cp = pltpu.make_async_remote_copy(
            src_ref=src, dst_ref=dst, send_sem=ssem.at[len(sends)], recv_sem=rsem, device_id=dev, device_id_type=MESH
        )
        cp.start()
        sends.append(cp)

    def recv_wait(dst, rsem, dev):
        pltpu.make_async_remote_copy(
            src_ref=dst, dst_ref=dst, send_sem=ssem.at[0], recv_sem=rsem, device_id=dev, device_id_type=MESH
        ).wait_recv()

    mine1 = pl.multiple_of(c * 256, 256)
    send(x_ref.at[pl.ds(pl.multiple_of((1 - c) * 256, 256), 256)], rs1, rsem1.at[0], core_peer())
    recv_wait(rs1, rsem1.at[0], core_peer())
    a1[...] = x_ref[pl.ds(mine1, 256), :] + rs1[...]

    for d in range(1, 4):
        xx = (x + d) % 4
        send(a1.at[pl.ds(pl.multiple_of(xx * 64, 64), 64)], rs2.at[x], rsem2.at[x], x_peer(xx))
    for d in range(1, 4):
        xx = (x + d) % 4
        recv_wait(rs2.at[xx], rsem2.at[xx], x_peer(xx))
    rs2[x] = a1[pl.ds(pl.multiple_of(x * 64, 64), 64), :]
    a2[...] = rs2[0] + rs2[1] + rs2[2] + rs2[3]

    for d in range(1, 8):
        yy = (y + d) % 8
        send(a2.at[pl.ds(pl.multiple_of(yy * 8, 8), 8)], rs3.at[y], rsem3.at[y], y_peer(yy))
    for d in range(1, 8):
        yy = (y + d) % 8
        recv_wait(rs3.at[yy], rsem3.at[yy], y_peer(yy))
    rs3[y] = a2[pl.ds(pl.multiple_of(y * 8, 8), 8), :]
    total3 = rs3[0]
    for i in range(1, 8):
        total3 = total3 + rs3[i]
    a3[...] = total3

    for d in range(1, 8):
        zz = (z + d) % 8
        send(a3, rs4.at[z], rsem4.at[z], z_peer(zz))
    for d in range(1, 8):
        zz = (z + d) % 8
        recv_wait(rs4.at[zz], rsem4.at[zz], z_peer(zz))
    rs4[z] = a3[...]
    total4 = rs4[0]
    for i in range(1, 8):
        total4 = total4 + rs4[i]
    base2 = c * 256 + x * 64
    full[pl.ds(pl.multiple_of(base2 + y * 8, 8), 8), :] = total4

    for d in range(1, 8):
        yy = (y + d) % 8
        blk = full.at[pl.ds(pl.multiple_of(base2 + y * 8, 8), 8)]
        send(blk, blk, gsem3.at[y], y_peer(yy))
    for d in range(1, 8):
        yy = (y + d) % 8
        recv_wait(full.at[pl.ds(pl.multiple_of(base2 + yy * 8, 8), 8)], gsem3.at[yy], y_peer(yy))
    for d in range(1, 4):
        xx = (x + d) % 4
        blk = full.at[pl.ds(pl.multiple_of(base2, 64), 64)]
        send(blk, blk, gsem2.at[x], x_peer(xx))
    for d in range(1, 4):
        xx = (x + d) % 4
        recv_wait(full.at[pl.ds(pl.multiple_of(c * 256 + xx * 64, 64), 64)], gsem2.at[xx], x_peer(xx))
    blk = full.at[pl.ds(mine1, 256)]
    send(blk, blk, gsem1.at[0], core_peer())
    recv_wait(full.at[pl.ds(pl.multiple_of((1 - c) * 256, 256), 256)], gsem1.at[0], core_peer())
    for cp in sends:
        cp.wait_send()
    o_ref[...] = full[...]


def allreduce_root(gram):
    flat = gram.reshape(512, 128)
    n_sends = 1 + 3 + 7 + 7 + 7 + 3 + 1
    out = pl.pallas_call(
        _allreduce_kernel,
        out_shape=jax.ShapeDtypeStruct((512, 128), jnp.float32),
        in_specs=[pl.BlockSpec(memory_space=pltpu.VMEM)],
        out_specs=pl.BlockSpec(memory_space=pltpu.VMEM),
        scratch_shapes=[
            pltpu.VMEM((512, 128), jnp.float32),
            pltpu.VMEM((256, 128), jnp.float32),
            pltpu.VMEM((64, 128), jnp.float32),
            pltpu.VMEM((8, 128), jnp.float32),
            pltpu.VMEM((256, 128), jnp.float32),
            pltpu.VMEM((4, 64, 128), jnp.float32),
            pltpu.VMEM((8, 8, 128), jnp.float32),
            pltpu.VMEM((8, 8, 128), jnp.float32),
            pltpu.SemaphoreType.DMA((n_sends,)),
            pltpu.SemaphoreType.DMA((1,)),
            pltpu.SemaphoreType.DMA((4,)),
            pltpu.SemaphoreType.DMA((8,)),
            pltpu.SemaphoreType.DMA((8,)),
            pltpu.SemaphoreType.DMA((8,)),
            pltpu.SemaphoreType.DMA((4,)),
            pltpu.SemaphoreType.DMA((1,)),
        ],
        compiler_params=pltpu.CompilerParams(collective_id=0, has_side_effects=True),
        cost_estimate=pl.CostEstimate(flops=4 * 65536, bytes_accessed=3 * 262144, transcendentals=0),
    )(flat)
    return out.reshape(256, 256)


def _gather_kernel(a_ref, o_ref, gathered, ssem, rsz, rsx, lsem):
    leaf = lax.axis_index("leaf")
    sub = lax.axis_index("sub")
    x = sub // 8
    z = sub % 8
    right = ((x + 1) % 4) * 8 + z
    left = ((x + 3) % 4) * 8 + z
    peers = [(leaf, x * 8 + (z + d) % 8) for d in range(1, 8)]
    peers += [(leaf, right), (leaf, left)]
    barrier = pltpu.get_barrier_semaphore()
    for p in peers:
        pl.semaphore_signal(barrier, inc=1, device_id=p, device_id_type=MESH)
    pl.semaphore_wait(barrier, len(peers))

    sends = []

    def send(src, dst, rsem, dev):
        cp = pltpu.make_async_remote_copy(
            src_ref=src, dst_ref=dst, send_sem=ssem.at[len(sends)], recv_sem=rsem, device_id=dev, device_id_type=MESH
        )
        cp.start()
        sends.append(cp)

    def recv_wait(dst, rsem, dev):
        pltpu.make_async_remote_copy(
            src_ref=dst, dst_ref=dst, send_sem=ssem.at[0], recv_sem=rsem, device_id=dev, device_id_type=MESH
        ).wait_recv()

    for d in range(1, 8):
        zz = (z + d) % 8
        send(a_ref, gathered.at[x * 8 + z], rsz.at[z], (leaf, x * 8 + zz))
    own = pltpu.make_async_copy(a_ref, gathered.at[x * 8 + z], lsem.at[0])
    own.start()
    for d in range(1, 8):
        zz = (z + d) % 8
        recv_wait(gathered.at[x * 8 + zz], rsz.at[zz], (leaf, x * 8 + zz))
    own.wait()

    def column(xx, first, count):
        return gathered.at[pl.ds(pl.multiple_of(xx * 8 + first, 4), count)]

    x_left = (x + 3) % 4
    x_right = (x + 1) % 4
    x_far = (x + 2) % 4
    send(column(x, 0, 8), column(x, 0, 8), rsx.at[0], (leaf, right))
    send(column(x, 0, 8), column(x, 0, 8), rsx.at[1], (leaf, left))
    recv_wait(column(x_left, 0, 8), rsx.at[0], (leaf, left))
    send(column(x_left, 0, 4), column(x_left, 0, 4), rsx.at[2], (leaf, right))
    recv_wait(column(x_right, 0, 8), rsx.at[1], (leaf, right))
    send(column(x_right, 4, 4), column(x_right, 4, 4), rsx.at[3], (leaf, left))
    recv_wait(column(x_far, 0, 4), rsx.at[2], (leaf, left))
    recv_wait(column(x_far, 4, 4), rsx.at[3], (leaf, right))
    for cp in sends:
        cp.wait_send()
    o_ref[...] = gathered[...]


def gather_sub(block):
    rows = block.shape[0]
    return pl.pallas_call(
        _gather_kernel,
        out_shape=jax.ShapeDtypeStruct((32, rows, 128), block.dtype),
        in_specs=[pl.BlockSpec(memory_space=pltpu.VMEM)],
        out_specs=pl.BlockSpec(memory_space=pltpu.VMEM),
        scratch_shapes=[
            pltpu.VMEM((32, rows, 128), block.dtype),
            pltpu.SemaphoreType.DMA((11,)),
            pltpu.SemaphoreType.DMA((8,)),
            pltpu.SemaphoreType.DMA((4,)),
            pltpu.SemaphoreType.DMA((1,)),
        ],
        compiler_params=pltpu.CompilerParams(collective_id=1, has_side_effects=True),
        cost_estimate=pl.CostEstimate(flops=0, bytes_accessed=2 * 32 * rows * 128 * 2, transcendentals=0),
    )(block)


def pack_symmetric(a):
    h = a.shape[0] // 2
    row = lax.broadcasted_iota(jnp.int32, (h, h), 0)
    col = lax.broadcasted_iota(jnp.int32, (h, h), 1)
    folded = jnp.where(col <= row, a[:h, :h], a[h:, h:])
    diag = jnp.where(row == col, a[h:, h:], jnp.zeros_like(a[h:, h:]))
    diag_row = jnp.sum(diag.astype(jnp.float32), axis=0, keepdims=True).astype(a.dtype)
    pad = jnp.zeros((15, h), a.dtype)
    return jnp.concatenate([folded, a[h:, :h], diag_row, pad], axis=0)


def unpack_symmetric(packed):
    h = 128
    folded = packed[:, :h, :]
    lower = packed[:, h:2 * h, :]
    diag_row = packed[:, 2 * h:2 * h + 1, :]
    row = lax.broadcasted_iota(jnp.int32, (1, h, h), 1)
    col = lax.broadcasted_iota(jnp.int32, (1, h, h), 2)
    folded_t = jnp.swapaxes(folded, 1, 2)
    top_left = jnp.where(col <= row, folded, folded_t)
    bottom_right = jnp.where(col > row, folded, jnp.where(col < row, folded_t, diag_row))
    top = jnp.concatenate([top_left, jnp.swapaxes(lower, 1, 2)], axis=2)
    bottom = jnp.concatenate([lower, bottom_right], axis=2)
    return jnp.concatenate([top, bottom], axis=1)


def _dot(a, b):
    return jnp.dot(a, b, precision=lax.Precision.HIGHEST)


def factor_and_inverse(schur):
    h = schur.shape[0] // 2
    identity = jnp.eye(h, dtype=schur.dtype)
    f11 = jnp.linalg.cholesky(schur[:h, :h])
    i11 = jax.scipy.linalg.solve_triangular(f11, identity, lower=True)
    f21 = _dot(schur[h:, :h], i11.T)
    f22 = jnp.linalg.cholesky(schur[h:, h:] - _dot(f21, f21.T))
    i22 = jax.scipy.linalg.solve_triangular(f22, identity, lower=True)
    i21 = -_dot(_dot(i22, f21), i11)
    zero = jnp.zeros((h, h), schur.dtype)
    factor = jnp.concatenate([jnp.concatenate([f11, zero], 1), jnp.concatenate([f21, f22], 1)], 0)
    inverse = jnp.concatenate([jnp.concatenate([i11, zero], 1), jnp.concatenate([i21, i22], 1)], 0)
    return factor, inverse


def packed_times(packed, panels):
    h = 128
    folded = packed[:, :h, :]
    lower = packed[:, h:2 * h, :]
    diag_col = jnp.swapaxes(packed[:, 2 * h:2 * h + 1, :], 1, 2).astype(jnp.float32)
    row = lax.broadcasted_iota(jnp.int32, (1, h, h), 1)
    col = lax.broadcasted_iota(jnp.int32, (1, h, h), 2)
    zero = jnp.zeros_like(folded)
    low_incl = jnp.where(col <= row, folded, zero)
    low_strict = jnp.where(col < row, folded, zero)
    up_strict = jnp.where(col > row, folded, zero)
    top_in, bottom_in = panels[:, :h, :], panels[:, h:, :]

    def mul(a, b):
        return jnp.einsum("nbk,nkw->nbw", a, b, preferred_element_type=jnp.float32)

    def mul_t(a, b):
        return jnp.einsum("nkb,nkw->nbw", a, b, preferred_element_type=jnp.float32)

    top = mul(low_incl, top_in) + mul_t(low_strict, top_in) + mul_t(lower, bottom_in)
    bottom = (
        mul(lower, top_in)
        + mul(up_strict, bottom_in)
        + mul_t(up_strict, bottom_in)
        + diag_col * bottom_in.astype(jnp.float32)
    )
    return jnp.concatenate([top, bottom], axis=1)


def adjoint_block(schur, cotangent):
    factor, inverse = factor_and_inverse(schur)
    product = jnp.dot(factor.T, cotangent, precision=lax.Precision.HIGHEST)
    lowered = jnp.tril(product) - 0.5 * jnp.diag(jnp.diag(product))
    adjoint_full = jnp.dot(
        jnp.dot(inverse.T, lowered, precision=lax.Precision.HIGHEST),
        inverse,
        precision=lax.Precision.HIGHEST,
    )
    return (0.5 * (adjoint_full + adjoint_full.T)).astype(jnp.bfloat16)


def body(
    panels,
    root_panels,
    low_inverse,
    structure,
    owner_map,
    upper_block,
    upper_cot,
    root_block,
    root_cot,
):
    devices_sub = lax.axis_size("sub")
    local_gram = jnp.einsum(
        "sbw,scw->bc", root_panels, root_panels, preferred_element_type=jnp.float32
    )
    root_total = allreduce_root(local_gram)
    root_total, panels = lax.optimization_barrier((root_total, panels))
    root_adjoint = adjoint_block(root_block - root_total, root_cot)
    rows_dev, blocks_row, height, breadth = panels.shape
    item_count = rows_dev * blocks_row
    capacity = max(2, 2 * item_count // devices_sub)
    group_id = lax.axis_index("leaf")
    owners = lax.dynamic_index_in_dim(owner_map, group_id, 0, keepdims=False)
    target = jnp.take(owners, structure.reshape(item_count))
    onehot = (target[:, None] == jnp.arange(devices_sub, dtype=jnp.int32)[None, :]).astype(
        jnp.int32
    )
    earlier = jnp.cumsum(onehot, axis=0) - onehot
    slot_id = jnp.sum(earlier * onehot, axis=1)
    position = target * capacity + slot_id
    flat_panels = panels.reshape(item_count, height, breadth)
    slots = jnp.arange(devices_sub * capacity, dtype=jnp.int32)
    match = position[None, :] == slots[:, None]
    source = jnp.where(jnp.any(match, axis=1), jnp.argmax(match, axis=1), item_count)
    outgoing = jnp.take(flat_panels, source, axis=0, mode="fill", fill_value=0)
    incoming = lax.all_to_all(outgoing, "sub", split_axis=0, concat_axis=0, tiled=True)
    root_panel_adjoint = (
        -2.0
        * jnp.einsum("bc,scw->sbw", root_adjoint, root_panels, preferred_element_type=jnp.float32)
    ).astype(jnp.bfloat16)
    root_grad = jnp.einsum(
        "sbw,swv->sbv", root_panel_adjoint, low_inverse, preferred_element_type=jnp.float32
    ).astype(jnp.bfloat16)
    root_grad, incoming = lax.optimization_barrier((root_grad, incoming))
    gram_sum = jnp.einsum("nbw,ncw->bc", incoming, incoming, preferred_element_type=jnp.float32)
    upper_adjoint = adjoint_block(upper_block[0] - gram_sum, upper_cot[0])
    chosen = jnp.take(gather_sub(pack_symmetric(upper_adjoint)), target, axis=0)
    panel_adjoint = (-2.0 * packed_times(chosen, flat_panels)).astype(jnp.bfloat16)
    panel_adjoint = panel_adjoint.reshape(rows_dev, blocks_row, height, breadth)
    panel_grad = jnp.einsum(
        "srbw,swv->srbv", panel_adjoint, low_inverse, preferred_element_type=jnp.float32
    ).astype(jnp.bfloat16)
    return (panel_grad, root_grad)


def solution(mesh):
    in_specs = (
        P(("leaf", "sub"), None, None, None),
        P(("leaf", "sub"), None, None),
        P(("leaf", "sub"), None, None),
        P(("leaf", "sub"), None),
        P(),
        P(("leaf", "sub"), None, None),
        P(("leaf", "sub"), None, None),
        P(),
        P(),
    )
    out_specs = (P(("leaf", "sub"), None, None, None), P(("leaf", "sub"), None, None))
    return jax.shard_map(body, mesh=mesh, in_specs=in_specs, out_specs=out_specs, check_vma=False)
```

```python
import jax
import jax.numpy as jnp
from jax import lax
from jax.experimental import pallas as pl
from jax.experimental.pallas import tpu as pltpu
from jax.sharding import PartitionSpec as P

MESH = pl.DeviceIdType.MESH

def _allreduce_kernel(
    x_ref, o_ref, full, a1, a2, a3, rs1, rs2, rs3, rs4, ssem, rsem1, rsem2, rsem3, rsem4, gsem3, gsem2, gsem1
):
    leaf = lax.axis_index("leaf")
    sub = lax.axis_index("sub")
    c = leaf % 2
    y = leaf // 2
    x = sub // 8
    z = sub % 8

    def core_peer():
        return (leaf + 1 - 2 * c, sub)

    def x_peer(xx):
        return (leaf, xx * 8 + z)

    def y_peer(yy):
        return (yy * 2 + c, sub)

    def z_peer(zz):
        return (leaf, x * 8 + zz)

    peers = [core_peer()]
    peers += [x_peer((x + d) % 4) for d in range(1, 4)]
    peers += [y_peer((y + d) % 8) for d in range(1, 8)]
    peers += [z_peer((z + d) % 8) for d in range(1, 8)]
    barrier = pltpu.get_barrier_semaphore()
    for p in peers:
        pl.semaphore_signal(barrier, inc=1, device_id=p, device_id_type=MESH)
    pl.semaphore_wait(barrier, len(peers))

    sends = []

    def send(src, dst, rsem, dev):
        cp = pltpu.make_async_remote_copy(
            src_ref=src, dst_ref=dst, send_sem=ssem.at[len(sends)], recv_sem=rsem, device_id=dev, device_id_type=MESH
        )
        cp.start()
        sends.append(cp)

    def recv_wait(dst, rsem, dev):
        pltpu.make_async_remote_copy(
            src_ref=dst, dst_ref=dst, send_sem=ssem.at[0], recv_sem=rsem, device_id=dev, device_id_type=MESH
        ).wait_recv()

    mine1 = pl.multiple_of(c * 256, 256)
    send(x_ref.at[pl.ds(pl.multiple_of((1 - c) * 256, 256), 256)], rs1, rsem1.at[0], core_peer())
    recv_wait(rs1, rsem1.at[0], core_peer())
    a1[...] = x_ref[pl.ds(mine1, 256), :] + rs1[...]

    for d in range(1, 4):
        xx = (x + d) % 4
        send(a1.at[pl.ds(pl.multiple_of(xx * 64, 64), 64)], rs2.at[x], rsem2.at[x], x_peer(xx))
    for d in range(1, 4):
        xx = (x + d) % 4
        recv_wait(rs2.at[xx], rsem2.at[xx], x_peer(xx))
    rs2[x] = a1[pl.ds(pl.multiple_of(x * 64, 64), 64), :]
    a2[...] = rs2[0] + rs2[1] + rs2[2] + rs2[3]

    for d in range(1, 8):
        yy = (y + d) % 8
        send(a2.at[pl.ds(pl.multiple_of(yy * 8, 8), 8)], rs3.at[y], rsem3.at[y], y_peer(yy))
    for d in range(1, 8):
        yy = (y + d) % 8
        recv_wait(rs3.at[yy], rsem3.at[yy], y_peer(yy))
    rs3[y] = a2[pl.ds(pl.multiple_of(y * 8, 8), 8), :]
    total3 = rs3[0]
    for i in range(1, 8):
        total3 = total3 + rs3[i]
    a3[...] = total3

    for d in range(1, 8):
        zz = (z + d) % 8
        send(a3, rs4.at[z], rsem4.at[z], z_peer(zz))
    for d in range(1, 8):
        zz = (z + d) % 8
        recv_wait(rs4.at[zz], rsem4.at[zz], z_peer(zz))
    rs4[z] = a3[...]
    total4 = rs4[0]
    for i in range(1, 8):
        total4 = total4 + rs4[i]
    base2 = c * 256 + x * 64
    full[pl.ds(pl.multiple_of(base2 + y * 8, 8), 8), :] = total4

    for d in range(1, 8):
        yy = (y + d) % 8
        blk = full.at[pl.ds(pl.multiple_of(base2 + y * 8, 8), 8)]
        send(blk, blk, gsem3.at[y], y_peer(yy))
    for d in range(1, 8):
        yy = (y + d) % 8
        recv_wait(full.at[pl.ds(pl.multiple_of(base2 + yy * 8, 8), 8)], gsem3.at[yy], y_peer(yy))
    for d in range(1, 4):
        xx = (x + d) % 4
        blk = full.at[pl.ds(pl.multiple_of(base2, 64), 64)]
        send(blk, blk, gsem2.at[x], x_peer(xx))
    for d in range(1, 4):
        xx = (x + d) % 4
        recv_wait(full.at[pl.ds(pl.multiple_of(c * 256 + xx * 64, 64), 64)], gsem2.at[xx], x_peer(xx))
    blk = full.at[pl.ds(mine1, 256)]
    send(blk, blk, gsem1.at[0], core_peer())
    recv_wait(full.at[pl.ds(pl.multiple_of((1 - c) * 256, 256), 256)], gsem1.at[0], core_peer())
    for cp in sends:
        cp.wait_send()
    o_ref[...] = full[...]


def allreduce_root(gram):
    flat = gram.reshape(512, 128)
    n_sends = 1 + 3 + 7 + 7 + 7 + 3 + 1
    out = pl.pallas_call(
        _allreduce_kernel,
        out_shape=jax.ShapeDtypeStruct((512, 128), jnp.float32),
        in_specs=[pl.BlockSpec(memory_space=pltpu.VMEM)],
        out_specs=pl.BlockSpec(memory_space=pltpu.VMEM),
        scratch_shapes=[
            pltpu.VMEM((512, 128), jnp.float32),
            pltpu.VMEM((256, 128), jnp.float32),
            pltpu.VMEM((64, 128), jnp.float32),
            pltpu.VMEM((8, 128), jnp.float32),
            pltpu.VMEM((256, 128), jnp.float32),
            pltpu.VMEM((4, 64, 128), jnp.float32),
            pltpu.VMEM((8, 8, 128), jnp.float32),
            pltpu.VMEM((8, 8, 128), jnp.float32),
            pltpu.SemaphoreType.DMA((n_sends,)),
            pltpu.SemaphoreType.DMA((1,)),
            pltpu.SemaphoreType.DMA((4,)),
            pltpu.SemaphoreType.DMA((8,)),
            pltpu.SemaphoreType.DMA((8,)),
            pltpu.SemaphoreType.DMA((8,)),
            pltpu.SemaphoreType.DMA((4,)),
            pltpu.SemaphoreType.DMA((1,)),
        ],
        compiler_params=pltpu.CompilerParams(collective_id=0, has_side_effects=True),
        cost_estimate=pl.CostEstimate(flops=4 * 65536, bytes_accessed=3 * 262144, transcendentals=0),
    )(flat)
    return out.reshape(256, 256)


def _gather_kernel(a_ref, o_ref, gathered, ssem, rsz, rsx, lsem):
    leaf = lax.axis_index("leaf")
    sub = lax.axis_index("sub")
    x = sub // 8
    z = sub % 8
    right = ((x + 1) % 4) * 8 + z
    left = ((x + 3) % 4) * 8 + z
    peers = [(leaf, x * 8 + (z + d) % 8) for d in range(1, 8)]
    peers += [(leaf, right), (leaf, left)]
    barrier = pltpu.get_barrier_semaphore()
    for p in peers:
        pl.semaphore_signal(barrier, inc=1, device_id=p, device_id_type=MESH)
    pl.semaphore_wait(barrier, len(peers))

    sends = []

    def send(src, dst, rsem, dev):
        cp = pltpu.make_async_remote_copy(
            src_ref=src, dst_ref=dst, send_sem=ssem.at[len(sends)], recv_sem=rsem, device_id=dev, device_id_type=MESH
        )
        cp.start()
        sends.append(cp)

    def recv_wait(dst, rsem, dev):
        pltpu.make_async_remote_copy(
            src_ref=dst, dst_ref=dst, send_sem=ssem.at[0], recv_sem=rsem, device_id=dev, device_id_type=MESH
        ).wait_recv()

    for d in range(1, 8):
        zz = (z + d) % 8
        send(a_ref, gathered.at[x * 8 + z], rsz.at[z], (leaf, x * 8 + zz))
    own = pltpu.make_async_copy(a_ref, gathered.at[x * 8 + z], lsem.at[0])
    own.start()
    for d in range(1, 8):
        zz = (z + d) % 8
        recv_wait(gathered.at[x * 8 + zz], rsz.at[zz], (leaf, x * 8 + zz))
    own.wait()

    def column(xx, first, count):
        return gathered.at[pl.ds(pl.multiple_of(xx * 8 + first, 4), count)]

    x_left = (x + 3) % 4
    x_right = (x + 1) % 4
    x_far = (x + 2) % 4
    send(column(x, 0, 8), column(x, 0, 8), rsx.at[0], (leaf, right))
    send(column(x, 0, 8), column(x, 0, 8), rsx.at[1], (leaf, left))
    recv_wait(column(x_left, 0, 8), rsx.at[0], (leaf, left))
    send(column(x_left, 0, 4), column(x_left, 0, 4), rsx.at[2], (leaf, right))
    recv_wait(column(x_right, 0, 8), rsx.at[1], (leaf, right))
    send(column(x_right, 4, 4), column(x_right, 4, 4), rsx.at[3], (leaf, left))
    recv_wait(column(x_far, 0, 4), rsx.at[2], (leaf, left))
    recv_wait(column(x_far, 4, 4), rsx.at[3], (leaf, right))
    for cp in sends:
        cp.wait_send()
    o_ref[...] = gathered[...]


def gather_sub(block):
    rows = block.shape[0]
    return pl.pallas_call(
        _gather_kernel,
        out_shape=jax.ShapeDtypeStruct((32, rows, 128), block.dtype),
        in_specs=[pl.BlockSpec(memory_space=pltpu.VMEM)],
        out_specs=pl.BlockSpec(memory_space=pltpu.VMEM),
        scratch_shapes=[
            pltpu.VMEM((32, rows, 128), block.dtype),
            pltpu.SemaphoreType.DMA((11,)),
            pltpu.SemaphoreType.DMA((8,)),
            pltpu.SemaphoreType.DMA((4,)),
            pltpu.SemaphoreType.DMA((1,)),
        ],
        compiler_params=pltpu.CompilerParams(collective_id=1, has_side_effects=True),
        cost_estimate=pl.CostEstimate(flops=0, bytes_accessed=2 * 32 * rows * 128 * 2, transcendentals=0),
    )(block)


def pack_symmetric(a):
    h = a.shape[0] // 2
    row = lax.broadcasted_iota(jnp.int32, (h, h), 0)
    col = lax.broadcasted_iota(jnp.int32, (h, h), 1)
    folded = jnp.where(col <= row, a[:h, :h], a[h:, h:])
    diag = jnp.where(row == col, a[h:, h:], jnp.zeros_like(a[h:, h:]))
    diag_row = jnp.sum(diag.astype(jnp.float32), axis=0, keepdims=True).astype(a.dtype)
    pad = jnp.zeros((15, h), a.dtype)
    return jnp.concatenate([folded, a[h:, :h], diag_row, pad], axis=0)


def unpack_symmetric(packed):
    h = 128
    folded = packed[:, :h, :]
    lower = packed[:, h:2 * h, :]
    diag_row = packed[:, 2 * h:2 * h + 1, :]
    row = lax.broadcasted_iota(jnp.int32, (1, h, h), 1)
    col = lax.broadcasted_iota(jnp.int32, (1, h, h), 2)
    folded_t = jnp.swapaxes(folded, 1, 2)
    top_left = jnp.where(col <= row, folded, folded_t)
    bottom_right = jnp.where(col > row, folded, jnp.where(col < row, folded_t, diag_row))
    top = jnp.concatenate([top_left, jnp.swapaxes(lower, 1, 2)], axis=2)
    bottom = jnp.concatenate([lower, bottom_right], axis=2)
    return jnp.concatenate([top, bottom], axis=1)


def _dot(a, b):
    return jnp.dot(a, b, precision=lax.Precision.HIGHEST)


def factor_and_inverse(schur):
    h = schur.shape[0] // 2
    identity = jnp.eye(h, dtype=schur.dtype)
    f11 = jnp.linalg.cholesky(schur[:h, :h])
    i11 = jax.scipy.linalg.solve_triangular(f11, identity, lower=True)
    f21 = _dot(schur[h:, :h], i11.T)
    f22 = jnp.linalg.cholesky(schur[h:, h:] - _dot(f21, f21.T))
    i22 = jax.scipy.linalg.solve_triangular(f22, identity, lower=True)
    i21 = -_dot(_dot(i22, f21), i11)
    zero = jnp.zeros((h, h), schur.dtype)
    factor = jnp.concatenate([jnp.concatenate([f11, zero], 1), jnp.concatenate([f21, f22], 1)], 0)
    inverse = jnp.concatenate([jnp.concatenate([i11, zero], 1), jnp.concatenate([i21, i22], 1)], 0)
    return factor, inverse


def packed_times(packed, panels):
    h = 128
    folded = packed[:, :h, :]
    lower = packed[:, h:2 * h, :]
    diag_col = jnp.swapaxes(packed[:, 2 * h:2 * h + 1, :], 1, 2).astype(jnp.float32)
    row = lax.broadcasted_iota(jnp.int32, (1, h, h), 1)
    col = lax.broadcasted_iota(jnp.int32, (1, h, h), 2)
    zero = jnp.zeros_like(folded)
    low_incl = jnp.where(col <= row, folded, zero)
    low_strict = jnp.where(col < row, folded, zero)
    up_strict = jnp.where(col > row, folded, zero)
    top_in, bottom_in = panels[:, :h, :], panels[:, h:, :]

    def mul(a, b):
        return jnp.einsum("nbk,nkw->nbw", a, b, preferred_element_type=jnp.float32)

    def mul_t(a, b):
        return jnp.einsum("nkb,nkw->nbw", a, b, preferred_element_type=jnp.float32)

    top = mul(low_incl, top_in) + mul_t(low_strict, top_in) + mul_t(lower, bottom_in)
    bottom = (
        mul(lower, top_in)
        + mul(up_strict, bottom_in)
        + mul_t(up_strict, bottom_in)
        + diag_col * bottom_in.astype(jnp.float32)
    )
    return jnp.concatenate([top, bottom], axis=1)


def adjoint_block(schur, cotangent):
    factor, inverse = factor_and_inverse(schur)
    product = jnp.dot(factor.T, cotangent, precision=lax.Precision.HIGHEST)
    lowered = jnp.tril(product) - 0.5 * jnp.diag(jnp.diag(product))
    adjoint_full = jnp.dot(
        jnp.dot(inverse.T, lowered, precision=lax.Precision.HIGHEST),
        inverse,
        precision=lax.Precision.HIGHEST,
    )
    return (0.5 * (adjoint_full + adjoint_full.T)).astype(jnp.bfloat16)


def body(
    panels,
    root_panels,
    low_inverse,
    structure,
    owner_map,
    upper_block,
    upper_cot,
    root_block,
    root_cot,
):
    devices_sub = lax.axis_size("sub")
    local_gram = jnp.einsum(
        "sbw,scw->bc", root_panels, root_panels, preferred_element_type=jnp.float32
    )
    root_total = allreduce_root(local_gram)
    root_total, panels = lax.optimization_barrier((root_total, panels))
    root_adjoint = adjoint_block(root_block - root_total, root_cot)
    rows_dev, blocks_row, height, breadth = panels.shape
    item_count = rows_dev * blocks_row
    capacity = max(2, 2 * item_count // devices_sub)
    group_id = lax.axis_index("leaf")
    owners = lax.dynamic_index_in_dim(owner_map, group_id, 0, keepdims=False)
    target = jnp.take(owners, structure.reshape(item_count))
    onehot = (target[:, None] == jnp.arange(devices_sub, dtype=jnp.int32)[None, :]).astype(
        jnp.int32
    )
    earlier = jnp.cumsum(onehot, axis=0) - onehot
    slot_id = jnp.sum(earlier * onehot, axis=1)
    position = target * capacity + slot_id
    flat_panels = panels.reshape(item_count, height, breadth)
    slots = jnp.arange(devices_sub * capacity, dtype=jnp.int32)
    match = position[None, :] == slots[:, None]
    source = jnp.where(jnp.any(match, axis=1), jnp.argmax(match, axis=1), item_count)
    with_zero = jnp.concatenate([flat_panels, jnp.zeros((1, height, breadth), flat_panels.dtype)], axis=0)
    outgoing = jnp.take(with_zero, source, axis=0, mode="clip")
    incoming = lax.all_to_all(outgoing, "sub", split_axis=0, concat_axis=0, tiled=True)
    root_panel_adjoint = (
        -2.0
        * jnp.einsum("bc,scw->sbw", root_adjoint, root_panels, preferred_element_type=jnp.float32)
    ).astype(jnp.bfloat16)
    root_grad = jnp.einsum(
        "sbw,swv->sbv", root_panel_adjoint, low_inverse, preferred_element_type=jnp.float32
    ).astype(jnp.bfloat16)
    root_grad, incoming = lax.optimization_barrier((root_grad, incoming))
    gram_sum = jnp.einsum("nbw,ncw->bc", incoming, incoming, preferred_element_type=jnp.float32)
    upper_adjoint = adjoint_block(upper_block[0] - gram_sum, upper_cot[0])
    chosen = jnp.take(gather_sub(pack_symmetric(upper_adjoint)), target, axis=0)
    panel_adjoint = (-2.0 * packed_times(chosen, flat_panels)).astype(jnp.bfloat16)
    panel_adjoint = panel_adjoint.reshape(rows_dev, blocks_row, height, breadth)
    panel_grad = jnp.einsum(
        "srbw,swv->srbv", panel_adjoint, low_inverse, preferred_element_type=jnp.float32
    ).astype(jnp.bfloat16)
    return (panel_grad, root_grad)


def solution(mesh):
    in_specs = (
        P(("leaf", "sub"), None, None, None),
        P(("leaf", "sub"), None, None),
        P(("leaf", "sub"), None, None),
        P(("leaf", "sub"), None),
        P(),
        P(("leaf", "sub"), None, None),
        P(("leaf", "sub"), None, None),
        P(),
        P(),
    )
    out_specs = (P(("leaf", "sub"), None, None, None), P(("leaf", "sub"), None, None))
    return jax.shard_map(body, mesh=mesh, in_specs=in_specs, out_specs=out_specs, check_vma=False)
```

```python
import jax
import jax.numpy as jnp
from jax import lax
from jax.experimental import pallas as pl
from jax.experimental.pallas import tpu as pltpu
from jax.sharding import PartitionSpec as P

MESH = pl.DeviceIdType.MESH

def _allreduce_kernel(x_ref, o_ref, full, a2, a3, rs2, rs3, rs4, ssem, rsem2, rsem3, rsem4, gsem3, gsem2):
    leaf = lax.axis_index("leaf")
    sub = lax.axis_index("sub")
    c = leaf % 2
    y = leaf // 2
    x = sub // 8
    z = sub % 8
    k = x * 2 + c

    def y_peer(yy):
        return (yy * 2 + c, sub)

    def z_peer(zz):
        return (leaf, x * 8 + zz)

    group = []
    for e in range(2):
        for d in range(4):
            if e == 0 and d == 0:
                continue
            cc = (c + e) % 2
            xx = (x + d) % 4
            group.append((xx * 2 + cc, (y * 2 + cc, xx * 8 + z)))
    peers = [dev for _, dev in group]
    peers += [y_peer((y + d) % 8) for d in range(1, 8)]
    peers += [z_peer((z + d) % 8) for d in range(1, 8)]
    barrier = pltpu.get_barrier_semaphore()
    for p in peers:
        pl.semaphore_signal(barrier, inc=1, device_id=p, device_id_type=MESH)
    pl.semaphore_wait(barrier, len(peers))

    sends = []

    def send(src, dst, rsem, dev):
        cp = pltpu.make_async_remote_copy(
            src_ref=src, dst_ref=dst, send_sem=ssem.at[len(sends)], recv_sem=rsem, device_id=dev, device_id_type=MESH
        )
        cp.start()
        sends.append(cp)

    def recv_wait(dst, rsem, dev):
        pltpu.make_async_remote_copy(
            src_ref=dst, dst_ref=dst, send_sem=ssem.at[0], recv_sem=rsem, device_id=dev, device_id_type=MESH
        ).wait_recv()

    def chunk(ref, kk, rows):
        return ref.at[pl.ds(pl.multiple_of(kk * rows, rows), rows)]

    for kk, dev in group:
        send(chunk(x_ref, kk, 64), rs2.at[k], rsem2.at[k], dev)
    for kk, dev in group:
        recv_wait(rs2.at[kk], rsem2.at[kk], dev)
    rs2[k] = x_ref[pl.ds(pl.multiple_of(k * 64, 64), 64), :]
    total2 = rs2[0]
    for i in range(1, 8):
        total2 = total2 + rs2[i]
    a2[...] = total2

    for d in range(1, 8):
        yy = (y + d) % 8
        send(chunk(a2, yy, 8), rs3.at[y], rsem3.at[y], y_peer(yy))
    for d in range(1, 8):
        yy = (y + d) % 8
        recv_wait(rs3.at[yy], rsem3.at[yy], y_peer(yy))
    rs3[y] = a2[pl.ds(pl.multiple_of(y * 8, 8), 8), :]
    total3 = rs3[0]
    for i in range(1, 8):
        total3 = total3 + rs3[i]
    a3[...] = total3

    for d in range(1, 8):
        zz = (z + d) % 8
        send(a3, rs4.at[z], rsem4.at[z], z_peer(zz))
    for d in range(1, 8):
        zz = (z + d) % 8
        recv_wait(rs4.at[zz], rsem4.at[zz], z_peer(zz))
    rs4[z] = a3[...]
    total4 = rs4[0]
    for i in range(1, 8):
        total4 = total4 + rs4[i]
    base = k * 64
    full[pl.ds(pl.multiple_of(base + y * 8, 8), 8), :] = total4

    for d in range(1, 8):
        yy = (y + d) % 8
        blk = full.at[pl.ds(pl.multiple_of(base + y * 8, 8), 8)]
        send(blk, blk, gsem3.at[y], y_peer(yy))
    for d in range(1, 8):
        yy = (y + d) % 8
        recv_wait(full.at[pl.ds(pl.multiple_of(base + yy * 8, 8), 8)], gsem3.at[yy], y_peer(yy))
    own = chunk(full, k, 64)
    for kk, dev in group:
        send(own, own, gsem2.at[k], dev)
    for kk, dev in group:
        recv_wait(chunk(full, kk, 64), gsem2.at[kk], dev)
    for cp in sends:
        cp.wait_send()
    o_ref[...] = full[...]


def allreduce_root(gram):
    flat = gram.reshape(512, 128)
    n_sends = 7 * 5
    out = pl.pallas_call(
        _allreduce_kernel,
        out_shape=jax.ShapeDtypeStruct((512, 128), jnp.float32),
        in_specs=[pl.BlockSpec(memory_space=pltpu.VMEM)],
        out_specs=pl.BlockSpec(memory_space=pltpu.VMEM),
        scratch_shapes=[
            pltpu.VMEM((512, 128), jnp.float32),
            pltpu.VMEM((64, 128), jnp.float32),
            pltpu.VMEM((8, 128), jnp.float32),
            pltpu.VMEM((8, 64, 128), jnp.float32),
            pltpu.VMEM((8, 8, 128), jnp.float32),
            pltpu.VMEM((8, 8, 128), jnp.float32),
            pltpu.SemaphoreType.DMA((n_sends,)),
            pltpu.SemaphoreType.DMA((8,)),
            pltpu.SemaphoreType.DMA((8,)),
            pltpu.SemaphoreType.DMA((8,)),
            pltpu.SemaphoreType.DMA((8,)),
            pltpu.SemaphoreType.DMA((8,)),
        ],
        compiler_params=pltpu.CompilerParams(collective_id=0, has_side_effects=True),
        cost_estimate=pl.CostEstimate(flops=4 * 65536, bytes_accessed=3 * 262144, transcendentals=0),
    )(flat)
    return out.reshape(256, 256)


def _gather_kernel(a_ref, o_ref, gathered, ssem, rsz, rsx, lsem):
    leaf = lax.axis_index("leaf")
    sub = lax.axis_index("sub")
    x = sub // 8
    z = sub % 8
    right = ((x + 1) % 4) * 8 + z
    left = ((x + 3) % 4) * 8 + z
    peers = [(leaf, x * 8 + (z + d) % 8) for d in range(1, 8)]
    peers += [(leaf, right), (leaf, left)]
    barrier = pltpu.get_barrier_semaphore()
    for p in peers:
        pl.semaphore_signal(barrier, inc=1, device_id=p, device_id_type=MESH)
    pl.semaphore_wait(barrier, len(peers))

    sends = []

    def send(src, dst, rsem, dev):
        cp = pltpu.make_async_remote_copy(
            src_ref=src, dst_ref=dst, send_sem=ssem.at[len(sends)], recv_sem=rsem, device_id=dev, device_id_type=MESH
        )
        cp.start()
        sends.append(cp)

    def recv_wait(dst, rsem, dev):
        pltpu.make_async_remote_copy(
            src_ref=dst, dst_ref=dst, send_sem=ssem.at[0], recv_sem=rsem, device_id=dev, device_id_type=MESH
        ).wait_recv()

    for d in range(1, 8):
        zz = (z + d) % 8
        send(a_ref, gathered.at[x * 8 + z], rsz.at[z], (leaf, x * 8 + zz))
    own = pltpu.make_async_copy(a_ref, gathered.at[x * 8 + z], lsem.at[0])
    own.start()
    for d in range(1, 8):
        zz = (z + d) % 8
        recv_wait(gathered.at[x * 8 + zz], rsz.at[zz], (leaf, x * 8 + zz))
    own.wait()

    def column(xx, first, count):
        return gathered.at[pl.ds(pl.multiple_of(xx * 8 + first, 4), count)]

    x_left = (x + 3) % 4
    x_right = (x + 1) % 4
    x_far = (x + 2) % 4
    send(column(x, 0, 8), column(x, 0, 8), rsx.at[0], (leaf, right))
    send(column(x, 0, 8), column(x, 0, 8), rsx.at[1], (leaf, left))
    recv_wait(column(x_left, 0, 8), rsx.at[0], (leaf, left))
    send(column(x_left, 0, 4), column(x_left, 0, 4), rsx.at[2], (leaf, right))
    recv_wait(column(x_right, 0, 8), rsx.at[1], (leaf, right))
    send(column(x_right, 4, 4), column(x_right, 4, 4), rsx.at[3], (leaf, left))
    recv_wait(column(x_far, 0, 4), rsx.at[2], (leaf, left))
    recv_wait(column(x_far, 4, 4), rsx.at[3], (leaf, right))
    for cp in sends:
        cp.wait_send()
    o_ref[...] = gathered[...]


def gather_sub(block):
    rows = block.shape[0]
    return pl.pallas_call(
        _gather_kernel,
        out_shape=jax.ShapeDtypeStruct((32, rows, 128), block.dtype),
        in_specs=[pl.BlockSpec(memory_space=pltpu.VMEM)],
        out_specs=pl.BlockSpec(memory_space=pltpu.VMEM),
        scratch_shapes=[
            pltpu.VMEM((32, rows, 128), block.dtype),
            pltpu.SemaphoreType.DMA((11,)),
            pltpu.SemaphoreType.DMA((8,)),
            pltpu.SemaphoreType.DMA((4,)),
            pltpu.SemaphoreType.DMA((1,)),
        ],
        compiler_params=pltpu.CompilerParams(collective_id=1, has_side_effects=True),
        cost_estimate=pl.CostEstimate(flops=0, bytes_accessed=2 * 32 * rows * 128 * 2, transcendentals=0),
    )(block)


def pack_symmetric(a):
    h = a.shape[0] // 2
    row = lax.broadcasted_iota(jnp.int32, (h, h), 0)
    col = lax.broadcasted_iota(jnp.int32, (h, h), 1)
    folded = jnp.where(col <= row, a[:h, :h], a[h:, h:])
    diag = jnp.where(row == col, a[h:, h:], jnp.zeros_like(a[h:, h:]))
    diag_row = jnp.sum(diag.astype(jnp.float32), axis=0, keepdims=True).astype(a.dtype)
    pad = jnp.zeros((15, h), a.dtype)
    return jnp.concatenate([folded, a[h:, :h], diag_row, pad], axis=0)


def unpack_symmetric(packed):
    h = 128
    folded = packed[:, :h, :]
    lower = packed[:, h:2 * h, :]
    diag_row = packed[:, 2 * h:2 * h + 1, :]
    row = lax.broadcasted_iota(jnp.int32, (1, h, h), 1)
    col = lax.broadcasted_iota(jnp.int32, (1, h, h), 2)
    folded_t = jnp.swapaxes(folded, 1, 2)
    top_left = jnp.where(col <= row, folded, folded_t)
    bottom_right = jnp.where(col > row, folded, jnp.where(col < row, folded_t, diag_row))
    top = jnp.concatenate([top_left, jnp.swapaxes(lower, 1, 2)], axis=2)
    bottom = jnp.concatenate([lower, bottom_right], axis=2)
    return jnp.concatenate([top, bottom], axis=1)


def _dot(a, b):
    return jnp.dot(a, b, precision=lax.Precision.HIGHEST)


def factor_and_inverse(schur):
    h = schur.shape[0] // 2
    identity = jnp.eye(h, dtype=schur.dtype)
    f11 = jnp.linalg.cholesky(schur[:h, :h])
    i11 = jax.scipy.linalg.solve_triangular(f11, identity, lower=True)
    f21 = _dot(schur[h:, :h], i11.T)
    f22 = jnp.linalg.cholesky(schur[h:, h:] - _dot(f21, f21.T))
    i22 = jax.scipy.linalg.solve_triangular(f22, identity, lower=True)
    i21 = -_dot(_dot(i22, f21), i11)
    zero = jnp.zeros((h, h), schur.dtype)
    factor = jnp.concatenate([jnp.concatenate([f11, zero], 1), jnp.concatenate([f21, f22], 1)], 0)
    inverse = jnp.concatenate([jnp.concatenate([i11, zero], 1), jnp.concatenate([i21, i22], 1)], 0)
    return factor, inverse


def packed_times(packed, panels):
    h = 128
    folded = packed[:, :h, :]
    lower = packed[:, h:2 * h, :]
    diag_col = jnp.swapaxes(packed[:, 2 * h:2 * h + 1, :], 1, 2).astype(jnp.float32)
    row = lax.broadcasted_iota(jnp.int32, (1, h, h), 1)
    col = lax.broadcasted_iota(jnp.int32, (1, h, h), 2)
    zero = jnp.zeros_like(folded)
    low_incl = jnp.where(col <= row, folded, zero)
    low_strict = jnp.where(col < row, folded, zero)
    up_strict = jnp.where(col > row, folded, zero)
    top_in, bottom_in = panels[:, :h, :], panels[:, h:, :]

    def mul(a, b):
        return jnp.einsum("nbk,nkw->nbw", a, b, preferred_element_type=jnp.float32)

    def mul_t(a, b):
        return jnp.einsum("nkb,nkw->nbw", a, b, preferred_element_type=jnp.float32)

    top = mul(low_incl, top_in) + mul_t(low_strict, top_in) + mul_t(lower, bottom_in)
    bottom = (
        mul(lower, top_in)
        + mul(up_strict, bottom_in)
        + mul_t(up_strict, bottom_in)
        + diag_col * bottom_in.astype(jnp.float32)
    )
    return jnp.concatenate([top, bottom], axis=1)


def adjoint_block(schur, cotangent):
    factor, inverse = factor_and_inverse(schur)
    product = jnp.dot(factor.T, cotangent, precision=lax.Precision.HIGHEST)
    lowered = jnp.tril(product) - 0.5 * jnp.diag(jnp.diag(product))
    adjoint_full = jnp.dot(
        jnp.dot(inverse.T, lowered, precision=lax.Precision.HIGHEST),
        inverse,
        precision=lax.Precision.HIGHEST,
    )
    return (0.5 * (adjoint_full + adjoint_full.T)).astype(jnp.bfloat16)


def body(
    panels,
    root_panels,
    low_inverse,
    structure,
    owner_map,
    upper_block,
    upper_cot,
    root_block,
    root_cot,
):
    devices_sub = lax.axis_size("sub")
    local_gram = jnp.einsum(
        "sbw,scw->bc", root_panels, root_panels, preferred_element_type=jnp.float32
    )
    root_total = allreduce_root(local_gram)
    root_total, panels = lax.optimization_barrier((root_total, panels))
    root_adjoint = adjoint_block(root_block - root_total, root_cot)
    rows_dev, blocks_row, height, breadth = panels.shape
    item_count = rows_dev * blocks_row
    capacity = max(2, 2 * item_count // devices_sub)
    group_id = lax.axis_index("leaf")
    owners = lax.dynamic_index_in_dim(owner_map, group_id, 0, keepdims=False)
    target = jnp.take(owners, structure.reshape(item_count))
    onehot = (target[:, None] == jnp.arange(devices_sub, dtype=jnp.int32)[None, :]).astype(
        jnp.int32
    )
    earlier = jnp.cumsum(onehot, axis=0) - onehot
    slot_id = jnp.sum(earlier * onehot, axis=1)
    position = target * capacity + slot_id
    flat_panels = panels.reshape(item_count, height, breadth)
    slots = jnp.arange(devices_sub * capacity, dtype=jnp.int32)
    match = position[None, :] == slots[:, None]
    source = jnp.where(jnp.any(match, axis=1), jnp.argmax(match, axis=1), item_count)
    with_zero = jnp.concatenate([flat_panels, jnp.zeros((1, height, breadth), flat_panels.dtype)], axis=0)
    outgoing = jnp.take(with_zero, source, axis=0, mode="clip")
    incoming = lax.all_to_all(outgoing, "sub", split_axis=0, concat_axis=0, tiled=True)
    root_panel_adjoint = (
        -2.0
        * jnp.einsum("bc,scw->sbw", root_adjoint, root_panels, preferred_element_type=jnp.float32)
    ).astype(jnp.bfloat16)
    root_grad = jnp.einsum(
        "sbw,swv->sbv", root_panel_adjoint, low_inverse, preferred_element_type=jnp.float32
    ).astype(jnp.bfloat16)
    root_grad, incoming = lax.optimization_barrier((root_grad, incoming))
    gram_sum = jnp.einsum("nbw,ncw->bc", incoming, incoming, preferred_element_type=jnp.float32)
    upper_adjoint = adjoint_block(upper_block[0] - gram_sum, upper_cot[0])
    chosen = jnp.take(gather_sub(pack_symmetric(upper_adjoint)), target, axis=0)
    panel_adjoint = (-2.0 * packed_times(chosen, flat_panels)).astype(jnp.bfloat16)
    panel_adjoint = panel_adjoint.reshape(rows_dev, blocks_row, height, breadth)
    panel_grad = jnp.einsum(
        "srbw,swv->srbv", panel_adjoint, low_inverse, preferred_element_type=jnp.float32
    ).astype(jnp.bfloat16)
    return (panel_grad, root_grad)


def solution(mesh):
    in_specs = (
        P(("leaf", "sub"), None, None, None),
        P(("leaf", "sub"), None, None),
        P(("leaf", "sub"), None, None),
        P(("leaf", "sub"), None),
        P(),
        P(("leaf", "sub"), None, None),
        P(("leaf", "sub"), None, None),
        P(),
        P(),
    )
    out_specs = (P(("leaf", "sub"), None, None, None), P(("leaf", "sub"), None, None))
    return jax.shard_map(body, mesh=mesh, in_specs=in_specs, out_specs=out_specs, check_vma=False)
```

```python
import jax
import jax.numpy as jnp
from jax import lax
from jax.experimental import pallas as pl
from jax.experimental.pallas import tpu as pltpu
from jax.sharding import PartitionSpec as P

MESH = pl.DeviceIdType.MESH

def _allreduce_kernel(
    x_ref, o_ref, full, a1, a2, a3, rs1, rs2, rs3, rs4, ssem, rsem1, rsem2, rsem3, rsem4, gsem3, gsem2, gsem1
):
    leaf = lax.axis_index("leaf")
    sub = lax.axis_index("sub")
    c = leaf % 2
    y = leaf // 2
    x = sub // 8
    z = sub % 8

    def core_peer():
        return (leaf + 1 - 2 * c, sub)

    def x_peer(xx):
        return (leaf, xx * 8 + z)

    def y_peer(yy):
        return (yy * 2 + c, sub)

    def z_peer(zz):
        return (leaf, x * 8 + zz)

    peers = [core_peer()]
    peers += [x_peer((x + d) % 4) for d in range(1, 4)]
    peers += [y_peer((y + d) % 8) for d in range(1, 8)]
    peers += [z_peer((z + d) % 8) for d in range(1, 8)]
    barrier = pltpu.get_barrier_semaphore()
    for p in peers:
        pl.semaphore_signal(barrier, inc=1, device_id=p, device_id_type=MESH)
    pl.semaphore_wait(barrier, len(peers))

    sends = []

    def send(src, dst, rsem, dev):
        cp = pltpu.make_async_remote_copy(
            src_ref=src, dst_ref=dst, send_sem=ssem.at[len(sends)], recv_sem=rsem, device_id=dev, device_id_type=MESH
        )
        cp.start()
        sends.append(cp)

    def recv_wait(dst, rsem, dev):
        pltpu.make_async_remote_copy(
            src_ref=dst, dst_ref=dst, send_sem=ssem.at[0], recv_sem=rsem, device_id=dev, device_id_type=MESH
        ).wait_recv()

    mine1 = pl.multiple_of(c * 256, 256)
    send(x_ref.at[pl.ds(pl.multiple_of((1 - c) * 256, 256), 256)], rs1, rsem1.at[0], core_peer())
    recv_wait(rs1, rsem1.at[0], core_peer())
    a1[...] = x_ref[pl.ds(mine1, 256), :] + rs1[...]

    for d in range(1, 4):
        xx = (x + d) % 4
        send(a1.at[pl.ds(pl.multiple_of(xx * 64, 64), 64)], rs2.at[x], rsem2.at[x], x_peer(xx))
    for d in range(1, 4):
        xx = (x + d) % 4
        recv_wait(rs2.at[xx], rsem2.at[xx], x_peer(xx))
    rs2[x] = a1[pl.ds(pl.multiple_of(x * 64, 64), 64), :]
    a2[...] = rs2[0] + rs2[1] + rs2[2] + rs2[3]

    for d in range(1, 8):
        yy = (y + d) % 8
        send(a2.at[pl.ds(pl.multiple_of(yy * 8, 8), 8)], rs3.at[y], rsem3.at[y], y_peer(yy))
    for d in range(1, 8):
        yy = (y + d) % 8
        recv_wait(rs3.at[yy], rsem3.at[yy], y_peer(yy))
    rs3[y] = a2[pl.ds(pl.multiple_of(y * 8, 8), 8), :]
    total3 = rs3[0]
    for i in range(1, 8):
        total3 = total3 + rs3[i]
    a3[...] = total3

    for d in range(1, 8):
        zz = (z + d) % 8
        send(a3, rs4.at[z], rsem4.at[z], z_peer(zz))
    for d in range(1, 8):
        zz = (z + d) % 8
        recv_wait(rs4.at[zz], rsem4.at[zz], z_peer(zz))
    rs4[z] = a3[...]
    total4 = rs4[0]
    for i in range(1, 8):
        total4 = total4 + rs4[i]
    base2 = c * 256 + x * 64
    full[pl.ds(pl.multiple_of(base2 + y * 8, 8), 8), :] = total4

    for d in range(1, 8):
        yy = (y + d) % 8
        blk = full.at[pl.ds(pl.multiple_of(base2 + y * 8, 8), 8)]
        send(blk, blk, gsem3.at[y], y_peer(yy))
    for d in range(1, 8):
        yy = (y + d) % 8
        recv_wait(full.at[pl.ds(pl.multiple_of(base2 + yy * 8, 8), 8)], gsem3.at[yy], y_peer(yy))
    for d in range(1, 4):
        xx = (x + d) % 4
        blk = full.at[pl.ds(pl.multiple_of(base2, 64), 64)]
        send(blk, blk, gsem2.at[x], x_peer(xx))
    for d in range(1, 4):
        xx = (x + d) % 4
        recv_wait(full.at[pl.ds(pl.multiple_of(c * 256 + xx * 64, 64), 64)], gsem2.at[xx], x_peer(xx))
    blk = full.at[pl.ds(mine1, 256)]
    send(blk, blk, gsem1.at[0], core_peer())
    recv_wait(full.at[pl.ds(pl.multiple_of((1 - c) * 256, 256), 256)], gsem1.at[0], core_peer())
    for cp in sends:
        cp.wait_send()
    o_ref[...] = full[...]


def allreduce_root(gram):
    flat = gram.reshape(512, 128)
    n_sends = 1 + 3 + 7 + 7 + 7 + 3 + 1
    out = pl.pallas_call(
        _allreduce_kernel,
        out_shape=jax.ShapeDtypeStruct((512, 128), jnp.float32),
        in_specs=[pl.BlockSpec(memory_space=pltpu.VMEM)],
        out_specs=pl.BlockSpec(memory_space=pltpu.VMEM),
        scratch_shapes=[
            pltpu.VMEM((512, 128), jnp.float32),
            pltpu.VMEM((256, 128), jnp.float32),
            pltpu.VMEM((64, 128), jnp.float32),
            pltpu.VMEM((8, 128), jnp.float32),
            pltpu.VMEM((256, 128), jnp.float32),
            pltpu.VMEM((4, 64, 128), jnp.float32),
            pltpu.VMEM((8, 8, 128), jnp.float32),
            pltpu.VMEM((8, 8, 128), jnp.float32),
            pltpu.SemaphoreType.DMA((n_sends,)),
            pltpu.SemaphoreType.DMA((1,)),
            pltpu.SemaphoreType.DMA((4,)),
            pltpu.SemaphoreType.DMA((8,)),
            pltpu.SemaphoreType.DMA((8,)),
            pltpu.SemaphoreType.DMA((8,)),
            pltpu.SemaphoreType.DMA((4,)),
            pltpu.SemaphoreType.DMA((1,)),
        ],
        compiler_params=pltpu.CompilerParams(collective_id=0, has_side_effects=True),
        cost_estimate=pl.CostEstimate(flops=4 * 65536, bytes_accessed=3 * 262144, transcendentals=0),
    )(flat)
    return out.reshape(256, 256)


def _gather_kernel(a_ref, pick_ref, o_ref, gathered, ssem, rsz, rsx, lsem):
    leaf = lax.axis_index("leaf")
    sub = lax.axis_index("sub")
    x = sub // 8
    z = sub % 8
    right = ((x + 1) % 4) * 8 + z
    left = ((x + 3) % 4) * 8 + z
    peers = [(leaf, x * 8 + (z + d) % 8) for d in range(1, 8)]
    peers += [(leaf, right), (leaf, left)]
    barrier = pltpu.get_barrier_semaphore()
    for p in peers:
        pl.semaphore_signal(barrier, inc=1, device_id=p, device_id_type=MESH)
    pl.semaphore_wait(barrier, len(peers))

    sends = []

    def send(src, dst, rsem, dev):
        cp = pltpu.make_async_remote_copy(
            src_ref=src, dst_ref=dst, send_sem=ssem.at[len(sends)], recv_sem=rsem, device_id=dev, device_id_type=MESH
        )
        cp.start()
        sends.append(cp)

    def recv_wait(dst, rsem, dev):
        pltpu.make_async_remote_copy(
            src_ref=dst, dst_ref=dst, send_sem=ssem.at[0], recv_sem=rsem, device_id=dev, device_id_type=MESH
        ).wait_recv()

    for d in range(1, 8):
        zz = (z + d) % 8
        send(a_ref, gathered.at[x * 8 + z], rsz.at[z], (leaf, x * 8 + zz))
    own = pltpu.make_async_copy(a_ref, gathered.at[x * 8 + z], lsem.at[0])
    own.start()
    for d in range(1, 8):
        zz = (z + d) % 8
        recv_wait(gathered.at[x * 8 + zz], rsz.at[zz], (leaf, x * 8 + zz))
    own.wait()

    def column(xx, first, count):
        return gathered.at[pl.ds(pl.multiple_of(xx * 8 + first, 4), count)]

    x_left = (x + 3) % 4
    x_right = (x + 1) % 4
    x_far = (x + 2) % 4
    send(column(x, 0, 8), column(x, 0, 8), rsx.at[0], (leaf, right))
    send(column(x, 0, 8), column(x, 0, 8), rsx.at[1], (leaf, left))
    recv_wait(column(x_left, 0, 8), rsx.at[0], (leaf, left))
    send(column(x_left, 0, 4), column(x_left, 0, 4), rsx.at[2], (leaf, right))
    recv_wait(column(x_right, 0, 8), rsx.at[1], (leaf, right))
    send(column(x_right, 4, 4), column(x_right, 4, 4), rsx.at[3], (leaf, left))
    recv_wait(column(x_far, 0, 4), rsx.at[2], (leaf, left))
    recv_wait(column(x_far, 4, 4), rsx.at[3], (leaf, right))
    for cp in sends:
        cp.wait_send()
    for i in range(o_ref.shape[0]):
        o_ref[i] = gathered[pick_ref[i]]


def gather_sub(block, pick):
    rows = block.shape[0]
    return pl.pallas_call(
        _gather_kernel,
        out_shape=jax.ShapeDtypeStruct((pick.shape[0], rows, 128), block.dtype),
        in_specs=[pl.BlockSpec(memory_space=pltpu.VMEM), pl.BlockSpec(memory_space=pltpu.SMEM)],
        out_specs=pl.BlockSpec(memory_space=pltpu.VMEM),
        scratch_shapes=[
            pltpu.VMEM((32, rows, 128), block.dtype),
            pltpu.SemaphoreType.DMA((11,)),
            pltpu.SemaphoreType.DMA((8,)),
            pltpu.SemaphoreType.DMA((4,)),
            pltpu.SemaphoreType.DMA((1,)),
        ],
        compiler_params=pltpu.CompilerParams(collective_id=1, has_side_effects=True),
        cost_estimate=pl.CostEstimate(flops=0, bytes_accessed=2 * 32 * rows * 128 * 2, transcendentals=0),
    )(block, pick)


def pack_symmetric(a):
    h = a.shape[0] // 2
    row = lax.broadcasted_iota(jnp.int32, (h, h), 0)
    col = lax.broadcasted_iota(jnp.int32, (h, h), 1)
    folded = jnp.where(col <= row, a[:h, :h], a[h:, h:])
    diag = jnp.where(row == col, a[h:, h:], jnp.zeros_like(a[h:, h:]))
    diag_row = jnp.sum(diag.astype(jnp.float32), axis=0, keepdims=True).astype(a.dtype)
    pad = jnp.zeros((15, h), a.dtype)
    return jnp.concatenate([folded, a[h:, :h], diag_row, pad], axis=0)


def unpack_symmetric(packed):
    h = 128
    folded = packed[:, :h, :]
    lower = packed[:, h:2 * h, :]
    diag_row = packed[:, 2 * h:2 * h + 1, :]
    row = lax.broadcasted_iota(jnp.int32, (1, h, h), 1)
    col = lax.broadcasted_iota(jnp.int32, (1, h, h), 2)
    folded_t = jnp.swapaxes(folded, 1, 2)
    top_left = jnp.where(col <= row, folded, folded_t)
    bottom_right = jnp.where(col > row, folded, jnp.where(col < row, folded_t, diag_row))
    top = jnp.concatenate([top_left, jnp.swapaxes(lower, 1, 2)], axis=2)
    bottom = jnp.concatenate([lower, bottom_right], axis=2)
    return jnp.concatenate([top, bottom], axis=1)


def _dot(a, b):
    return jnp.dot(a, b, precision=lax.Precision.HIGHEST)


def factor_and_inverse(schur):
    h = schur.shape[0] // 2
    identity = jnp.eye(h, dtype=schur.dtype)
    f11 = jnp.linalg.cholesky(schur[:h, :h])
    i11 = jax.scipy.linalg.solve_triangular(f11, identity, lower=True)
    f21 = _dot(schur[h:, :h], i11.T)
    f22 = jnp.linalg.cholesky(schur[h:, h:] - _dot(f21, f21.T))
    i22 = jax.scipy.linalg.solve_triangular(f22, identity, lower=True)
    i21 = -_dot(_dot(i22, f21), i11)
    zero = jnp.zeros((h, h), schur.dtype)
    factor = jnp.concatenate([jnp.concatenate([f11, zero], 1), jnp.concatenate([f21, f22], 1)], 0)
    inverse = jnp.concatenate([jnp.concatenate([i11, zero], 1), jnp.concatenate([i21, i22], 1)], 0)
    return factor, inverse


def packed_times(packed, panels):
    h = 128
    folded = packed[:, :h, :]
    lower = packed[:, h:2 * h, :]
    diag_col = jnp.swapaxes(packed[:, 2 * h:2 * h + 1, :], 1, 2).astype(jnp.float32)
    row = lax.broadcasted_iota(jnp.int32, (1, h, h), 1)
    col = lax.broadcasted_iota(jnp.int32, (1, h, h), 2)
    zero = jnp.zeros_like(folded)
    low_incl = jnp.where(col <= row, folded, zero)
    low_strict = jnp.where(col < row, folded, zero)
    up_strict = jnp.where(col > row, folded, zero)
    top_in, bottom_in = panels[:, :h, :], panels[:, h:, :]

    def mul(a, b):
        return jnp.einsum("nbk,nkw->nbw", a, b, preferred_element_type=jnp.float32)

    def mul_t(a, b):
        return jnp.einsum("nkb,nkw->nbw", a, b, preferred_element_type=jnp.float32)

    top = mul(low_incl, top_in) + mul_t(low_strict, top_in) + mul_t(lower, bottom_in)
    bottom = (
        mul(lower, top_in)
        + mul(up_strict, bottom_in)
        + mul_t(up_strict, bottom_in)
        + diag_col * bottom_in.astype(jnp.float32)
    )
    return jnp.concatenate([top, bottom], axis=1)


def adjoint_block(schur, cotangent):
    factor, inverse = factor_and_inverse(schur)
    product = jnp.dot(factor.T, cotangent, precision=lax.Precision.HIGHEST)
    lowered = jnp.tril(product) - 0.5 * jnp.diag(jnp.diag(product))
    adjoint_full = jnp.dot(
        jnp.dot(inverse.T, lowered, precision=lax.Precision.HIGHEST),
        inverse,
        precision=lax.Precision.HIGHEST,
    )
    return (0.5 * (adjoint_full + adjoint_full.T)).astype(jnp.bfloat16)


def body(
    panels,
    root_panels,
    low_inverse,
    structure,
    owner_map,
    upper_block,
    upper_cot,
    root_block,
    root_cot,
):
    devices_sub = lax.axis_size("sub")
    local_gram = jnp.einsum(
        "sbw,scw->bc", root_panels, root_panels, preferred_element_type=jnp.float32
    )
    root_total = allreduce_root(local_gram)
    root_total, panels = lax.optimization_barrier((root_total, panels))
    root_adjoint = adjoint_block(root_block - root_total, root_cot)
    rows_dev, blocks_row, height, breadth = panels.shape
    item_count = rows_dev * blocks_row
    capacity = max(2, 2 * item_count // devices_sub)
    group_id = lax.axis_index("leaf")
    owners = lax.dynamic_index_in_dim(owner_map, group_id, 0, keepdims=False)
    target = jnp.take(owners, structure.reshape(item_count))
    onehot = (target[:, None] == jnp.arange(devices_sub, dtype=jnp.int32)[None, :]).astype(
        jnp.int32
    )
    earlier = jnp.cumsum(onehot, axis=0) - onehot
    slot_id = jnp.sum(earlier * onehot, axis=1)
    position = target * capacity + slot_id
    flat_panels = panels.reshape(item_count, height, breadth)
    slots = jnp.arange(devices_sub * capacity, dtype=jnp.int32)
    match = position[None, :] == slots[:, None]
    source = jnp.where(jnp.any(match, axis=1), jnp.argmax(match, axis=1), item_count)
    with_zero = jnp.concatenate([flat_panels, jnp.zeros((1, height, breadth), flat_panels.dtype)], axis=0)
    outgoing = jnp.take(with_zero, source, axis=0, mode="clip")
    incoming = lax.all_to_all(outgoing, "sub", split_axis=0, concat_axis=0, tiled=True)
    root_panel_adjoint = (
        -2.0
        * jnp.einsum("bc,scw->sbw", root_adjoint, root_panels, preferred_element_type=jnp.float32)
    ).astype(jnp.bfloat16)
    root_grad = jnp.einsum(
        "sbw,swv->sbv", root_panel_adjoint, low_inverse, preferred_element_type=jnp.float32
    ).astype(jnp.bfloat16)
    root_grad, incoming = lax.optimization_barrier((root_grad, incoming))
    gram_sum = jnp.einsum("nbw,ncw->bc", incoming, incoming, preferred_element_type=jnp.float32)
    upper_adjoint = adjoint_block(upper_block[0] - gram_sum, upper_cot[0])
    chosen = gather_sub(pack_symmetric(upper_adjoint), target)
    panel_adjoint = (-2.0 * packed_times(chosen, flat_panels)).astype(jnp.bfloat16)
    panel_adjoint = panel_adjoint.reshape(rows_dev, blocks_row, height, breadth)
    panel_grad = jnp.einsum(
        "srbw,swv->srbv", panel_adjoint, low_inverse, preferred_element_type=jnp.float32
    ).astype(jnp.bfloat16)
    return (panel_grad, root_grad)


def solution(mesh):
    in_specs = (
        P(("leaf", "sub"), None, None, None),
        P(("leaf", "sub"), None, None),
        P(("leaf", "sub"), None, None),
        P(("leaf", "sub"), None),
        P(),
        P(("leaf", "sub"), None, None),
        P(("leaf", "sub"), None, None),
        P(),
        P(),
    )
    out_specs = (P(("leaf", "sub"), None, None, None), P(("leaf", "sub"), None, None))
    return jax.shard_map(body, mesh=mesh, in_specs=in_specs, out_specs=out_specs, check_vma=False)
```

```python
import jax
import jax.numpy as jnp
from jax import lax
from jax.experimental import pallas as pl
from jax.experimental.pallas import tpu as pltpu
from jax.sharding import PartitionSpec as P

MESH = pl.DeviceIdType.MESH

def _allreduce_kernel(
    x_ref, o_ref, full, a1, a2, a3, rs1, rs2, rs3, rs4, ssem, rsem1, rsem2, rsem3, rsem4, gsem3, gsem2, gsem1
):
    leaf = lax.axis_index("leaf")
    sub = lax.axis_index("sub")
    c = leaf % 2
    y = leaf // 2
    x = sub // 8
    z = sub % 8

    def core_peer():
        return (leaf + 1 - 2 * c, sub)

    def x_peer(xx):
        return (leaf, xx * 8 + z)

    def y_peer(yy):
        return (yy * 2 + c, sub)

    def z_peer(zz):
        return (leaf, x * 8 + zz)

    peers = [core_peer()]
    peers += [x_peer((x + d) % 4) for d in range(1, 4)]
    peers += [y_peer((y + d) % 8) for d in range(1, 8)]
    peers += [z_peer((z + d) % 8) for d in range(1, 8)]
    barrier = pltpu.get_barrier_semaphore()
    for p in peers:
        pl.semaphore_signal(barrier, inc=1, device_id=p, device_id_type=MESH)
    pl.semaphore_wait(barrier, len(peers))

    sends = []

    def send(src, dst, rsem, dev):
        cp = pltpu.make_async_remote_copy(
            src_ref=src, dst_ref=dst, send_sem=ssem.at[len(sends)], recv_sem=rsem, device_id=dev, device_id_type=MESH
        )
        cp.start()
        sends.append(cp)

    def recv_wait(dst, rsem, dev):
        pltpu.make_async_remote_copy(
            src_ref=dst, dst_ref=dst, send_sem=ssem.at[0], recv_sem=rsem, device_id=dev, device_id_type=MESH
        ).wait_recv()

    mine1 = pl.multiple_of(c * 256, 256)
    send(x_ref.at[pl.ds(pl.multiple_of((1 - c) * 256, 256), 256)], rs1, rsem1.at[0], core_peer())
    recv_wait(rs1, rsem1.at[0], core_peer())
    a1[...] = x_ref[pl.ds(mine1, 256), :] + rs1[...]

    for d in range(1, 4):
        xx = (x + d) % 4
        send(a1.at[pl.ds(pl.multiple_of(xx * 64, 64), 64)], rs2.at[x], rsem2.at[x], x_peer(xx))
    for d in range(1, 4):
        xx = (x + d) % 4
        recv_wait(rs2.at[xx], rsem2.at[xx], x_peer(xx))
    rs2[x] = a1[pl.ds(pl.multiple_of(x * 64, 64), 64), :]
    a2[...] = rs2[0] + rs2[1] + rs2[2] + rs2[3]

    for d in range(1, 8):
        yy = (y + d) % 8
        send(a2.at[pl.ds(pl.multiple_of(yy * 8, 8), 8)], rs3.at[y], rsem3.at[y], y_peer(yy))
    for d in range(1, 8):
        yy = (y + d) % 8
        recv_wait(rs3.at[yy], rsem3.at[yy], y_peer(yy))
    rs3[y] = a2[pl.ds(pl.multiple_of(y * 8, 8), 8), :]
    total3 = rs3[0]
    for i in range(1, 8):
        total3 = total3 + rs3[i]
    a3[...] = total3

    for d in range(1, 8):
        zz = (z + d) % 8
        send(a3, rs4.at[z], rsem4.at[z], z_peer(zz))
    for d in range(1, 8):
        zz = (z + d) % 8
        recv_wait(rs4.at[zz], rsem4.at[zz], z_peer(zz))
    rs4[z] = a3[...]
    total4 = rs4[0]
    for i in range(1, 8):
        total4 = total4 + rs4[i]
    base2 = c * 256 + x * 64
    full[pl.ds(pl.multiple_of(base2 + y * 8, 8), 8), :] = total4

    for d in range(1, 8):
        yy = (y + d) % 8
        blk = full.at[pl.ds(pl.multiple_of(base2 + y * 8, 8), 8)]
        send(blk, blk, gsem3.at[y], y_peer(yy))
    for d in range(1, 8):
        yy = (y + d) % 8
        recv_wait(full.at[pl.ds(pl.multiple_of(base2 + yy * 8, 8), 8)], gsem3.at[yy], y_peer(yy))
    for d in range(1, 4):
        xx = (x + d) % 4
        blk = full.at[pl.ds(pl.multiple_of(base2, 64), 64)]
        send(blk, blk, gsem2.at[x], x_peer(xx))
    for d in range(1, 4):
        xx = (x + d) % 4
        recv_wait(full.at[pl.ds(pl.multiple_of(c * 256 + xx * 64, 64), 64)], gsem2.at[xx], x_peer(xx))
    blk = full.at[pl.ds(mine1, 256)]
    send(blk, blk, gsem1.at[0], core_peer())
    recv_wait(full.at[pl.ds(pl.multiple_of((1 - c) * 256, 256), 256)], gsem1.at[0], core_peer())
    for cp in sends:
        cp.wait_send()
    o_ref[...] = full[...]


def allreduce_root(gram):
    flat = gram.reshape(512, 128)
    n_sends = 1 + 3 + 7 + 7 + 7 + 3 + 1
    out = pl.pallas_call(
        _allreduce_kernel,
        out_shape=jax.ShapeDtypeStruct((512, 128), jnp.float32),
        in_specs=[pl.BlockSpec(memory_space=pltpu.VMEM)],
        out_specs=pl.BlockSpec(memory_space=pltpu.VMEM),
        scratch_shapes=[
            pltpu.VMEM((512, 128), jnp.float32),
            pltpu.VMEM((256, 128), jnp.float32),
            pltpu.VMEM((64, 128), jnp.float32),
            pltpu.VMEM((8, 128), jnp.float32),
            pltpu.VMEM((256, 128), jnp.float32),
            pltpu.VMEM((4, 64, 128), jnp.float32),
            pltpu.VMEM((8, 8, 128), jnp.float32),
            pltpu.VMEM((8, 8, 128), jnp.float32),
            pltpu.SemaphoreType.DMA((n_sends,)),
            pltpu.SemaphoreType.DMA((1,)),
            pltpu.SemaphoreType.DMA((4,)),
            pltpu.SemaphoreType.DMA((8,)),
            pltpu.SemaphoreType.DMA((8,)),
            pltpu.SemaphoreType.DMA((8,)),
            pltpu.SemaphoreType.DMA((4,)),
            pltpu.SemaphoreType.DMA((1,)),
        ],
        compiler_params=pltpu.CompilerParams(collective_id=0, has_side_effects=True),
        cost_estimate=pl.CostEstimate(flops=4 * 65536, bytes_accessed=3 * 262144, transcendentals=0),
    )(flat)
    return out.reshape(256, 256)


def _gather_kernel(a_ref, pick_ref, o_ref, gathered, ssem, rsz, rsx, lsem):
    leaf = lax.axis_index("leaf")
    sub = lax.axis_index("sub")
    x = sub // 8
    z = sub % 8
    right = ((x + 1) % 4) * 8 + z
    left = ((x + 3) % 4) * 8 + z
    peers = [(leaf, x * 8 + (z + d) % 8) for d in range(1, 8)]
    peers += [(leaf, right), (leaf, left)]
    barrier = pltpu.get_barrier_semaphore()
    for p in peers:
        pl.semaphore_signal(barrier, inc=1, device_id=p, device_id_type=MESH)
    pl.semaphore_wait(barrier, len(peers))

    sends = []

    def send(src, dst, rsem, dev):
        cp = pltpu.make_async_remote_copy(
            src_ref=src, dst_ref=dst, send_sem=ssem.at[len(sends)], recv_sem=rsem, device_id=dev, device_id_type=MESH
        )
        cp.start()
        sends.append(cp)

    def recv_wait(dst, rsem, dev):
        pltpu.make_async_remote_copy(
            src_ref=dst, dst_ref=dst, send_sem=ssem.at[0], recv_sem=rsem, device_id=dev, device_id_type=MESH
        ).wait_recv()

    for d in range(1, 8):
        zz = (z + d) % 8
        send(a_ref, gathered.at[x * 8 + z], rsz.at[z], (leaf, x * 8 + zz))
    own = pltpu.make_async_copy(a_ref, gathered.at[x * 8 + z], lsem.at[0])
    own.start()
    for d in range(1, 8):
        zz = (z + d) % 8
        recv_wait(gathered.at[x * 8 + zz], rsz.at[zz], (leaf, x * 8 + zz))
    own.wait()

    def column(xx, first, count):
        return gathered.at[pl.ds(pl.multiple_of(xx * 8 + first, 4), count)]

    x_left = (x + 3) % 4
    x_right = (x + 1) % 4
    x_far = (x + 2) % 4
    send(column(x, 0, 8), column(x, 0, 8), rsx.at[0], (leaf, right))
    send(column(x, 0, 8), column(x, 0, 8), rsx.at[1], (leaf, left))
    recv_wait(column(x_left, 0, 8), rsx.at[0], (leaf, left))
    send(column(x_left, 0, 4), column(x_left, 0, 4), rsx.at[2], (leaf, right))
    recv_wait(column(x_right, 0, 8), rsx.at[1], (leaf, right))
    send(column(x_right, 4, 4), column(x_right, 4, 4), rsx.at[3], (leaf, left))
    recv_wait(column(x_far, 0, 4), rsx.at[2], (leaf, left))
    recv_wait(column(x_far, 4, 4), rsx.at[3], (leaf, right))
    for cp in sends:
        cp.wait_send()
    for i in range(o_ref.shape[0]):
        o_ref[i] = gathered[pick_ref[i]]


def gather_sub(block, pick):
    rows = block.shape[0]
    return pl.pallas_call(
        _gather_kernel,
        out_shape=jax.ShapeDtypeStruct((pick.shape[0], rows, 128), block.dtype),
        in_specs=[pl.BlockSpec(memory_space=pltpu.VMEM), pl.BlockSpec(memory_space=pltpu.SMEM)],
        out_specs=pl.BlockSpec(memory_space=pltpu.VMEM),
        scratch_shapes=[
            pltpu.VMEM((32, rows, 128), block.dtype),
            pltpu.SemaphoreType.DMA((11,)),
            pltpu.SemaphoreType.DMA((8,)),
            pltpu.SemaphoreType.DMA((4,)),
            pltpu.SemaphoreType.DMA((1,)),
        ],
        compiler_params=pltpu.CompilerParams(collective_id=1, has_side_effects=True),
        cost_estimate=pl.CostEstimate(flops=0, bytes_accessed=2 * 32 * rows * 128 * 2, transcendentals=0),
    )(block, pick)


def pack_symmetric(a):
    h = a.shape[0] // 2
    row = lax.broadcasted_iota(jnp.int32, (h, h), 0)
    col = lax.broadcasted_iota(jnp.int32, (h, h), 1)
    folded = jnp.where(col <= row, a[:h, :h], a[h:, h:])
    diag = jnp.where(row == col, a[h:, h:], jnp.zeros_like(a[h:, h:]))
    diag_row = jnp.sum(diag.astype(jnp.float32), axis=0, keepdims=True).astype(a.dtype)
    pad = jnp.zeros((15, h), a.dtype)
    return jnp.concatenate([folded, a[h:, :h], diag_row, pad], axis=0)


def unpack_symmetric(packed):
    h = 128
    folded = packed[:, :h, :]
    lower = packed[:, h:2 * h, :]
    diag_row = packed[:, 2 * h:2 * h + 1, :]
    row = lax.broadcasted_iota(jnp.int32, (1, h, h), 1)
    col = lax.broadcasted_iota(jnp.int32, (1, h, h), 2)
    folded_t = jnp.swapaxes(folded, 1, 2)
    top_left = jnp.where(col <= row, folded, folded_t)
    bottom_right = jnp.where(col > row, folded, jnp.where(col < row, folded_t, diag_row))
    top = jnp.concatenate([top_left, jnp.swapaxes(lower, 1, 2)], axis=2)
    bottom = jnp.concatenate([lower, bottom_right], axis=2)
    return jnp.concatenate([top, bottom], axis=1)


def _dot(a, b):
    return jnp.dot(a, b, precision=lax.Precision.HIGHEST)


def factor_and_inverse(schur):
    h = schur.shape[0] // 2
    return factor_and_inverse_blocks(schur[:h, :h], schur[h:, :h], schur[h:, h:])


def factor_and_inverse_blocks(s11, s21, s22):
    schur = s11
    h = s11.shape[0]
    identity = jnp.eye(h, dtype=schur.dtype)
    f11 = jnp.linalg.cholesky(s11)
    i11 = jax.scipy.linalg.solve_triangular(f11, identity, lower=True)
    f21 = _dot(s21, i11.T)
    f22 = jnp.linalg.cholesky(s22 - _dot(f21, f21.T))
    i22 = jax.scipy.linalg.solve_triangular(f22, identity, lower=True)
    i21 = -_dot(_dot(i22, f21), i11)
    zero = jnp.zeros((h, h), schur.dtype)
    factor = jnp.concatenate([jnp.concatenate([f11, zero], 1), jnp.concatenate([f21, f22], 1)], 0)
    inverse = jnp.concatenate([jnp.concatenate([i11, zero], 1), jnp.concatenate([i21, i22], 1)], 0)
    return factor, inverse


def packed_times(packed, panels):
    h = 128
    folded = packed[:, :h, :]
    lower = packed[:, h:2 * h, :]
    diag_col = jnp.swapaxes(packed[:, 2 * h:2 * h + 1, :], 1, 2).astype(jnp.float32)
    row = lax.broadcasted_iota(jnp.int32, (1, h, h), 1)
    col = lax.broadcasted_iota(jnp.int32, (1, h, h), 2)
    zero = jnp.zeros_like(folded)
    low_incl = jnp.where(col <= row, folded, zero)
    low_strict = jnp.where(col < row, folded, zero)
    up_strict = jnp.where(col > row, folded, zero)
    top_in, bottom_in = panels[:, :h, :], panels[:, h:, :]

    def mul(a, b):
        return jnp.einsum("nbk,nkw->nbw", a, b, preferred_element_type=jnp.float32)

    def mul_t(a, b):
        return jnp.einsum("nkb,nkw->nbw", a, b, preferred_element_type=jnp.float32)

    top = mul(low_incl, top_in) + mul_t(low_strict, top_in) + mul_t(lower, bottom_in)
    bottom = (
        mul(lower, top_in)
        + mul(up_strict, bottom_in)
        + mul_t(up_strict, bottom_in)
        + diag_col * bottom_in.astype(jnp.float32)
    )
    return jnp.concatenate([top, bottom], axis=1)


def adjoint_block(schur, cotangent):
    return adjoint_of_factor(factor_and_inverse(schur), cotangent)


def adjoint_of_factor(factored, cotangent):
    factor, inverse = factored
    product = jnp.dot(factor.T, cotangent, precision=lax.Precision.HIGHEST)
    lowered = jnp.tril(product) - 0.5 * jnp.diag(jnp.diag(product))
    adjoint_full = jnp.dot(
        jnp.dot(inverse.T, lowered, precision=lax.Precision.HIGHEST),
        inverse,
        precision=lax.Precision.HIGHEST,
    )
    return (0.5 * (adjoint_full + adjoint_full.T)).astype(jnp.bfloat16)


def body(
    panels,
    root_panels,
    low_inverse,
    structure,
    owner_map,
    upper_block,
    upper_cot,
    root_block,
    root_cot,
):
    devices_sub = lax.axis_size("sub")
    local_gram = jnp.einsum(
        "sbw,scw->bc", root_panels, root_panels, preferred_element_type=jnp.float32
    )
    root_total = allreduce_root(local_gram)
    root_total, panels = lax.optimization_barrier((root_total, panels))
    root_adjoint = adjoint_block(root_block - root_total, root_cot)
    rows_dev, blocks_row, height, breadth = panels.shape
    item_count = rows_dev * blocks_row
    capacity = max(2, 2 * item_count // devices_sub)
    group_id = lax.axis_index("leaf")
    owners = lax.dynamic_index_in_dim(owner_map, group_id, 0, keepdims=False)
    target = jnp.take(owners, structure.reshape(item_count))
    onehot = (target[:, None] == jnp.arange(devices_sub, dtype=jnp.int32)[None, :]).astype(
        jnp.int32
    )
    earlier = jnp.cumsum(onehot, axis=0) - onehot
    slot_id = jnp.sum(earlier * onehot, axis=1)
    position = target * capacity + slot_id
    flat_panels = panels.reshape(item_count, height, breadth)
    slots = jnp.arange(devices_sub * capacity, dtype=jnp.int32)
    match = position[None, :] == slots[:, None]
    source = jnp.where(jnp.any(match, axis=1), jnp.argmax(match, axis=1), item_count)
    with_zero = jnp.concatenate([flat_panels, jnp.zeros((1, height, breadth), flat_panels.dtype)], axis=0)
    outgoing = jnp.take(with_zero, source, axis=0, mode="clip")
    incoming = lax.all_to_all(outgoing, "sub", split_axis=0, concat_axis=0, tiled=True)
    root_panel_adjoint = (
        -2.0
        * jnp.einsum("bc,scw->sbw", root_adjoint, root_panels, preferred_element_type=jnp.float32)
    ).astype(jnp.bfloat16)
    root_grad = jnp.einsum(
        "sbw,swv->sbv", root_panel_adjoint, low_inverse, preferred_element_type=jnp.float32
    ).astype(jnp.bfloat16)
    root_grad, incoming = lax.optimization_barrier((root_grad, incoming))
    half = height // 2
    top, bottom = incoming[:, :half, :], incoming[:, half:, :]

    def gram(a, b):
        return jnp.einsum("nbw,ncw->bc", a, b, preferred_element_type=jnp.float32)

    block = upper_block[0]
    factored = factor_and_inverse_blocks(
        block[:half, :half] - gram(top, top),
        block[half:, :half] - gram(bottom, top),
        block[half:, half:] - gram(bottom, bottom),
    )
    upper_adjoint = adjoint_of_factor(factored, upper_cot[0])
    chosen = gather_sub(pack_symmetric(upper_adjoint), target)
    panel_adjoint = (-2.0 * packed_times(chosen, flat_panels)).astype(jnp.bfloat16)
    panel_adjoint = panel_adjoint.reshape(rows_dev, blocks_row, height, breadth)
    panel_grad = jnp.einsum(
        "srbw,swv->srbv", panel_adjoint, low_inverse, preferred_element_type=jnp.float32
    ).astype(jnp.bfloat16)
    return (panel_grad, root_grad)


def solution(mesh):
    in_specs = (
        P(("leaf", "sub"), None, None, None),
        P(("leaf", "sub"), None, None),
        P(("leaf", "sub"), None, None),
        P(("leaf", "sub"), None),
        P(),
        P(("leaf", "sub"), None, None),
        P(("leaf", "sub"), None, None),
        P(),
        P(),
    )
    out_specs = (P(("leaf", "sub"), None, None, None), P(("leaf", "sub"), None, None))
    return jax.shard_map(body, mesh=mesh, in_specs=in_specs, out_specs=out_specs, check_vma=False)
```

```python
import jax
import jax.numpy as jnp
from jax import lax
from jax.experimental import pallas as pl
from jax.experimental.pallas import tpu as pltpu
from jax.sharding import PartitionSpec as P

MESH = pl.DeviceIdType.MESH

def _allreduce_kernel(
    x_ref, o_ref, full, a1, a2, a3, rs1, rs2, rs3, rs4, ssem, rsem1, rsem2, rsem3, rsem4, gsem3, gsem2, gsem1
):
    leaf = lax.axis_index("leaf")
    sub = lax.axis_index("sub")
    c = leaf % 2
    y = leaf // 2
    x = sub // 8
    z = sub % 8

    def core_peer():
        return (leaf + 1 - 2 * c, sub)

    def x_peer(xx):
        return (leaf, xx * 8 + z)

    def y_peer(yy):
        return (yy * 2 + c, sub)

    def z_peer(zz):
        return (leaf, x * 8 + zz)

    peers = [core_peer()]
    peers += [x_peer((x + d) % 4) for d in range(1, 4)]
    peers += [y_peer((y + d) % 8) for d in range(1, 8)]
    peers += [z_peer((z + d) % 8) for d in range(1, 8)]
    barrier = pltpu.get_barrier_semaphore()
    for p in peers:
        pl.semaphore_signal(barrier, inc=1, device_id=p, device_id_type=MESH)
    pl.semaphore_wait(barrier, len(peers))

    sends = []

    def send(src, dst, rsem, dev):
        cp = pltpu.make_async_remote_copy(
            src_ref=src, dst_ref=dst, send_sem=ssem.at[len(sends)], recv_sem=rsem, device_id=dev, device_id_type=MESH
        )
        cp.start()
        sends.append(cp)

    def recv_wait(dst, rsem, dev):
        pltpu.make_async_remote_copy(
            src_ref=dst, dst_ref=dst, send_sem=ssem.at[0], recv_sem=rsem, device_id=dev, device_id_type=MESH
        ).wait_recv()

    mine1 = pl.multiple_of(c * 256, 256)
    send(x_ref.at[pl.ds(pl.multiple_of((1 - c) * 256, 256), 256)], rs1, rsem1.at[0], core_peer())
    recv_wait(rs1, rsem1.at[0], core_peer())
    a1[...] = x_ref[pl.ds(mine1, 256), :] + rs1[...]

    for d in range(1, 4):
        xx = (x + d) % 4
        send(a1.at[pl.ds(pl.multiple_of(xx * 64, 64), 64)], rs2.at[x], rsem2.at[x], x_peer(xx))
    for d in range(1, 4):
        xx = (x + d) % 4
        recv_wait(rs2.at[xx], rsem2.at[xx], x_peer(xx))
    rs2[x] = a1[pl.ds(pl.multiple_of(x * 64, 64), 64), :]
    a2[...] = rs2[0] + rs2[1] + rs2[2] + rs2[3]

    for d in range(1, 8):
        yy = (y + d) % 8
        send(a2.at[pl.ds(pl.multiple_of(yy * 8, 8), 8)], rs3.at[y], rsem3.at[y], y_peer(yy))
    for d in range(1, 8):
        yy = (y + d) % 8
        recv_wait(rs3.at[yy], rsem3.at[yy], y_peer(yy))
    rs3[y] = a2[pl.ds(pl.multiple_of(y * 8, 8), 8), :]
    total3 = rs3[0]
    for i in range(1, 8):
        total3 = total3 + rs3[i]
    a3[...] = total3

    for d in range(1, 8):
        zz = (z + d) % 8
        send(a3, rs4.at[z], rsem4.at[z], z_peer(zz))
    for d in range(1, 8):
        zz = (z + d) % 8
        recv_wait(rs4.at[zz], rsem4.at[zz], z_peer(zz))
    rs4[z] = a3[...]
    total4 = rs4[0]
    for i in range(1, 8):
        total4 = total4 + rs4[i]
    base2 = c * 256 + x * 64
    full[pl.ds(pl.multiple_of(base2 + y * 8, 8), 8), :] = total4

    for d in range(1, 8):
        yy = (y + d) % 8
        blk = full.at[pl.ds(pl.multiple_of(base2 + y * 8, 8), 8)]
        send(blk, blk, gsem3.at[y], y_peer(yy))
    for d in range(1, 8):
        yy = (y + d) % 8
        recv_wait(full.at[pl.ds(pl.multiple_of(base2 + yy * 8, 8), 8)], gsem3.at[yy], y_peer(yy))
    for d in range(1, 4):
        xx = (x + d) % 4
        blk = full.at[pl.ds(pl.multiple_of(base2, 64), 64)]
        send(blk, blk, gsem2.at[x], x_peer(xx))
    for d in range(1, 4):
        xx = (x + d) % 4
        recv_wait(full.at[pl.ds(pl.multiple_of(c * 256 + xx * 64, 64), 64)], gsem2.at[xx], x_peer(xx))
    blk = full.at[pl.ds(mine1, 256)]
    send(blk, blk, gsem1.at[0], core_peer())
    recv_wait(full.at[pl.ds(pl.multiple_of((1 - c) * 256, 256), 256)], gsem1.at[0], core_peer())
    for cp in sends:
        cp.wait_send()
    o_ref[...] = full[...]


def allreduce_root(gram):
    flat = gram.reshape(512, 128)
    n_sends = 1 + 3 + 7 + 7 + 7 + 3 + 1
    out = pl.pallas_call(
        _allreduce_kernel,
        out_shape=jax.ShapeDtypeStruct((512, 128), jnp.float32),
        in_specs=[pl.BlockSpec(memory_space=pltpu.VMEM)],
        out_specs=pl.BlockSpec(memory_space=pltpu.VMEM),
        scratch_shapes=[
            pltpu.VMEM((512, 128), jnp.float32),
            pltpu.VMEM((256, 128), jnp.float32),
            pltpu.VMEM((64, 128), jnp.float32),
            pltpu.VMEM((8, 128), jnp.float32),
            pltpu.VMEM((256, 128), jnp.float32),
            pltpu.VMEM((4, 64, 128), jnp.float32),
            pltpu.VMEM((8, 8, 128), jnp.float32),
            pltpu.VMEM((8, 8, 128), jnp.float32),
            pltpu.SemaphoreType.DMA((n_sends,)),
            pltpu.SemaphoreType.DMA((1,)),
            pltpu.SemaphoreType.DMA((4,)),
            pltpu.SemaphoreType.DMA((8,)),
            pltpu.SemaphoreType.DMA((8,)),
            pltpu.SemaphoreType.DMA((8,)),
            pltpu.SemaphoreType.DMA((4,)),
            pltpu.SemaphoreType.DMA((1,)),
        ],
        compiler_params=pltpu.CompilerParams(collective_id=0, has_side_effects=True),
        cost_estimate=pl.CostEstimate(flops=4 * 65536, bytes_accessed=3 * 262144, transcendentals=0),
    )(flat)
    return out


def _gather_kernel(a_ref, pick_ref, o_ref, gathered, ssem, rsz, rsx, lsem):
    leaf = lax.axis_index("leaf")
    sub = lax.axis_index("sub")
    x = sub // 8
    z = sub % 8
    right = ((x + 1) % 4) * 8 + z
    left = ((x + 3) % 4) * 8 + z
    peers = [(leaf, x * 8 + (z + d) % 8) for d in range(1, 8)]
    peers += [(leaf, right), (leaf, left)]
    barrier = pltpu.get_barrier_semaphore()
    for p in peers:
        pl.semaphore_signal(barrier, inc=1, device_id=p, device_id_type=MESH)
    pl.semaphore_wait(barrier, len(peers))

    sends = []

    def send(src, dst, rsem, dev):
        cp = pltpu.make_async_remote_copy(
            src_ref=src, dst_ref=dst, send_sem=ssem.at[len(sends)], recv_sem=rsem, device_id=dev, device_id_type=MESH
        )
        cp.start()
        sends.append(cp)

    def recv_wait(dst, rsem, dev):
        pltpu.make_async_remote_copy(
            src_ref=dst, dst_ref=dst, send_sem=ssem.at[0], recv_sem=rsem, device_id=dev, device_id_type=MESH
        ).wait_recv()

    for d in range(1, 8):
        zz = (z + d) % 8
        send(a_ref, gathered.at[x * 8 + z], rsz.at[z], (leaf, x * 8 + zz))
    own = pltpu.make_async_copy(a_ref, gathered.at[x * 8 + z], lsem.at[0])
    own.start()
    for d in range(1, 8):
        zz = (z + d) % 8
        recv_wait(gathered.at[x * 8 + zz], rsz.at[zz], (leaf, x * 8 + zz))
    own.wait()

    def column(xx, first, count):
        return gathered.at[pl.ds(pl.multiple_of(xx * 8 + first, 4), count)]

    x_left = (x + 3) % 4
    x_right = (x + 1) % 4
    x_far = (x + 2) % 4
    send(column(x, 0, 8), column(x, 0, 8), rsx.at[0], (leaf, right))
    send(column(x, 0, 8), column(x, 0, 8), rsx.at[1], (leaf, left))
    recv_wait(column(x_left, 0, 8), rsx.at[0], (leaf, left))
    send(column(x_left, 0, 4), column(x_left, 0, 4), rsx.at[2], (leaf, right))
    recv_wait(column(x_right, 0, 8), rsx.at[1], (leaf, right))
    send(column(x_right, 4, 4), column(x_right, 4, 4), rsx.at[3], (leaf, left))
    recv_wait(column(x_far, 0, 4), rsx.at[2], (leaf, left))
    recv_wait(column(x_far, 4, 4), rsx.at[3], (leaf, right))
    for cp in sends:
        cp.wait_send()
    for i in range(o_ref.shape[0]):
        o_ref[i] = gathered[pick_ref[i]]


def gather_sub(block, pick):
    rows = block.shape[0]
    return pl.pallas_call(
        _gather_kernel,
        out_shape=jax.ShapeDtypeStruct((pick.shape[0], rows, 128), block.dtype),
        in_specs=[pl.BlockSpec(memory_space=pltpu.VMEM), pl.BlockSpec(memory_space=pltpu.SMEM)],
        out_specs=pl.BlockSpec(memory_space=pltpu.VMEM),
        scratch_shapes=[
            pltpu.VMEM((32, rows, 128), block.dtype),
            pltpu.SemaphoreType.DMA((11,)),
            pltpu.SemaphoreType.DMA((8,)),
            pltpu.SemaphoreType.DMA((4,)),
            pltpu.SemaphoreType.DMA((1,)),
        ],
        compiler_params=pltpu.CompilerParams(collective_id=1, has_side_effects=True),
        cost_estimate=pl.CostEstimate(flops=0, bytes_accessed=2 * 32 * rows * 128 * 2, transcendentals=0),
    )(block, pick)


def pack_symmetric(a):
    h = a.shape[0] // 2
    row = lax.broadcasted_iota(jnp.int32, (h, h), 0)
    col = lax.broadcasted_iota(jnp.int32, (h, h), 1)
    folded = jnp.where(col <= row, a[:h, :h], a[h:, h:])
    diag = jnp.where(row == col, a[h:, h:], jnp.zeros_like(a[h:, h:]))
    diag_row = jnp.sum(diag.astype(jnp.float32), axis=0, keepdims=True).astype(a.dtype)
    pad = jnp.zeros((15, h), a.dtype)
    return jnp.concatenate([folded, a[h:, :h], diag_row, pad], axis=0)


def unpack_symmetric(packed):
    h = 128
    folded = packed[:, :h, :]
    lower = packed[:, h:2 * h, :]
    diag_row = packed[:, 2 * h:2 * h + 1, :]
    row = lax.broadcasted_iota(jnp.int32, (1, h, h), 1)
    col = lax.broadcasted_iota(jnp.int32, (1, h, h), 2)
    folded_t = jnp.swapaxes(folded, 1, 2)
    top_left = jnp.where(col <= row, folded, folded_t)
    bottom_right = jnp.where(col > row, folded, jnp.where(col < row, folded_t, diag_row))
    top = jnp.concatenate([top_left, jnp.swapaxes(lower, 1, 2)], axis=2)
    bottom = jnp.concatenate([lower, bottom_right], axis=2)
    return jnp.concatenate([top, bottom], axis=1)


def _dot(a, b):
    return jnp.dot(a, b, precision=lax.Precision.HIGHEST)


def factor_and_inverse(schur):
    h = schur.shape[0] // 2
    identity = jnp.eye(h, dtype=schur.dtype)
    f11 = jnp.linalg.cholesky(schur[:h, :h])
    i11 = jax.scipy.linalg.solve_triangular(f11, identity, lower=True)
    f21 = _dot(schur[h:, :h], i11.T)
    f22 = jnp.linalg.cholesky(schur[h:, h:] - _dot(f21, f21.T))
    i22 = jax.scipy.linalg.solve_triangular(f22, identity, lower=True)
    i21 = -_dot(_dot(i22, f21), i11)
    zero = jnp.zeros((h, h), schur.dtype)
    factor = jnp.concatenate([jnp.concatenate([f11, zero], 1), jnp.concatenate([f21, f22], 1)], 0)
    inverse = jnp.concatenate([jnp.concatenate([i11, zero], 1), jnp.concatenate([i21, i22], 1)], 0)
    return factor, inverse


def packed_times(packed, panels):
    h = 128
    folded = packed[:, :h, :]
    lower = packed[:, h:2 * h, :]
    diag_col = jnp.swapaxes(packed[:, 2 * h:2 * h + 1, :], 1, 2).astype(jnp.float32)
    row = lax.broadcasted_iota(jnp.int32, (1, h, h), 1)
    col = lax.broadcasted_iota(jnp.int32, (1, h, h), 2)
    zero = jnp.zeros_like(folded)
    low_incl = jnp.where(col <= row, folded, zero)
    low_strict = jnp.where(col < row, folded, zero)
    up_strict = jnp.where(col > row, folded, zero)
    top_in, bottom_in = panels[:, :h, :], panels[:, h:, :]

    def mul(a, b):
        return jnp.einsum("nbk,nkw->nbw", a, b, preferred_element_type=jnp.float32)

    def mul_t(a, b):
        return jnp.einsum("nkb,nkw->nbw", a, b, preferred_element_type=jnp.float32)

    top = mul(low_incl, top_in) + mul_t(low_strict, top_in) + mul_t(lower, bottom_in)
    bottom = (
        mul(lower, top_in)
        + mul(up_strict, bottom_in)
        + mul_t(up_strict, bottom_in)
        + diag_col * bottom_in.astype(jnp.float32)
    )
    return jnp.concatenate([top, bottom], axis=1)


def adjoint_block(schur, cotangent):
    factor, inverse = factor_and_inverse(schur)
    product = jnp.dot(factor.T, cotangent, precision=lax.Precision.HIGHEST)
    lowered = jnp.tril(product) - 0.5 * jnp.diag(jnp.diag(product))
    adjoint_full = jnp.dot(
        jnp.dot(inverse.T, lowered, precision=lax.Precision.HIGHEST),
        inverse,
        precision=lax.Precision.HIGHEST,
    )
    return (0.5 * (adjoint_full + adjoint_full.T)).astype(jnp.bfloat16)


def body(
    panels,
    root_panels,
    low_inverse,
    structure,
    owner_map,
    upper_block,
    upper_cot,
    root_block,
    root_cot,
):
    devices_sub = lax.axis_size("sub")
    local_gram = jnp.einsum(
        "sbw,scw->bc", root_panels, root_panels, preferred_element_type=jnp.float32
    )
    root_flat = allreduce_root(local_gram)
    root_flat, panels = lax.optimization_barrier((root_flat, panels))
    root_total = root_flat.reshape(local_gram.shape)
    root_adjoint = adjoint_block(root_block - root_total, root_cot)
    rows_dev, blocks_row, height, breadth = panels.shape
    item_count = rows_dev * blocks_row
    capacity = max(2, 2 * item_count // devices_sub)
    group_id = lax.axis_index("leaf")
    owners = lax.dynamic_index_in_dim(owner_map, group_id, 0, keepdims=False)
    target = jnp.take(owners, structure.reshape(item_count))
    onehot = (target[:, None] == jnp.arange(devices_sub, dtype=jnp.int32)[None, :]).astype(
        jnp.int32
    )
    earlier = jnp.cumsum(onehot, axis=0) - onehot
    slot_id = jnp.sum(earlier * onehot, axis=1)
    position = target * capacity + slot_id
    flat_panels = panels.reshape(item_count, height, breadth)
    slots = jnp.arange(devices_sub * capacity, dtype=jnp.int32)
    match = position[None, :] == slots[:, None]
    source = jnp.where(jnp.any(match, axis=1), jnp.argmax(match, axis=1), item_count)
    with_zero = jnp.concatenate([flat_panels, jnp.zeros((1, height, breadth), flat_panels.dtype)], axis=0)
    outgoing = jnp.take(with_zero, source, axis=0, mode="clip")
    incoming = lax.all_to_all(outgoing, "sub", split_axis=0, concat_axis=0, tiled=True)
    root_panel_adjoint = (
        -2.0
        * jnp.einsum("bc,scw->sbw", root_adjoint, root_panels, preferred_element_type=jnp.float32)
    ).astype(jnp.bfloat16)
    root_grad = jnp.einsum(
        "sbw,swv->sbv", root_panel_adjoint, low_inverse, preferred_element_type=jnp.float32
    ).astype(jnp.bfloat16)
    root_grad, incoming = lax.optimization_barrier((root_grad, incoming))
    gram_sum = jnp.einsum("nbw,ncw->bc", incoming, incoming, preferred_element_type=jnp.float32)
    upper_adjoint = adjoint_block(upper_block[0] - gram_sum, upper_cot[0])
    chosen = gather_sub(pack_symmetric(upper_adjoint), target)
    panel_adjoint = (-2.0 * packed_times(chosen, flat_panels)).astype(jnp.bfloat16)
    panel_adjoint = panel_adjoint.reshape(rows_dev, blocks_row, height, breadth)
    panel_grad = jnp.einsum(
        "srbw,swv->srbv", panel_adjoint, low_inverse, preferred_element_type=jnp.float32
    ).astype(jnp.bfloat16)
    return (panel_grad, root_grad)


def solution(mesh):
    in_specs = (
        P(("leaf", "sub"), None, None, None),
        P(("leaf", "sub"), None, None),
        P(("leaf", "sub"), None, None),
        P(("leaf", "sub"), None),
        P(),
        P(("leaf", "sub"), None, None),
        P(("leaf", "sub"), None, None),
        P(),
        P(),
    )
    out_specs = (P(("leaf", "sub"), None, None, None), P(("leaf", "sub"), None, None))
    return jax.shard_map(body, mesh=mesh, in_specs=in_specs, out_specs=out_specs, check_vma=False)
```
